32 devices in a mesh: axial: 16 (over z, x, core), azim: 2 (over y).
Axes of the slice: x: 2, y: 2, z: 4, core: 2. Of those that a mesh axis runs over, the one named last changes fastest.
Arguments:
- velocity: float32 [3, 8, 8, 8, 16, 2, 128], P(None, None, None, None, 'axial', 'azim'), may hold values from -6 to 6
- diffusivity: float32 [8, 8, 8, 16, 2, 128], P(None, None, None, 'axial', 'azim'), may hold values from 1 to 10
- coarse_factor: float32 [32, 32], P(('axial', 'azim')), may hold values from -0.0625 to 0.0625
Outputs:
- pressure: float32 [8, 8, 8, 16, 2, 128], P(None, None, None, 'axial', 'azim')
- residual: float32 [8, 8, 8, 16, 2, 128], P(None, None, None, 'axial', 'azim')
- direction: float32 [8, 8, 8, 16, 2, 128], P(None, None, None, 'axial', 'azim')
The draws below stay inside these ranges and needn't reach their ends.
All inputs are finite; a program needn't handle non-finite values.
Results may differ from the reference program's by a relative error of at most 0.02.
Values sent between devices are 32-bit elements; how exact they have to be, the bound alone decides.
No kernel may reach another device: no remote copies, remote signals or barrier semaphores. Data moves between devices by JAX's collectives and lax.ppermute only.
A program may use at most 128 MiB of HBM per device.

```python
import math
import jax
import jax.numpy as jnp
from jax import lax

NODES_PER_SIDE = 8
EA = 1
EZ = 1
RADIAL_ELEMENTS = 128
ITERS = 2
AXIAL_ELEMENTS = 16
AZIMUTH_ELEMENTS = 2
NC = 32
N_AXIAL = 16
N_AZIM = 2


def shard_levels(rng, shape, cuts, least, top_value):
    def one(dim, parts):
        heights = jax.random.uniform(jax.random.fold_in(jax.random.fold_in(rng, 6), dim), (parts,), jnp.float32, least / len(cuts), top_value / len(cuts))
        return jnp.repeat(jnp.exp(heights), shape[dim] // parts).reshape((-1,) + (1,) * (len(shape) - dim - 1))

    loudness = one(*cuts[0])
    for cut in cuts[1:]:
        loudness = loudness * one(*cut)
    return loudness


def centred(key, dims, scale, most, pieces=(), kind=jnp.bfloat16):
    result = jax.random.normal(key, dims, jnp.float32) * scale
    if len(pieces) > 0:
        result = shard_levels(key, dims, pieces, -0.22, 0.18) * result
    return jnp.clip(result, min=-most, max=most).astype(kind)


def setup_inputs(seed: int = 0) -> dict:
    splits = jax.random.split(jax.random.key(seed), 4)
    velocity = centred(splits[0], (3, NODES_PER_SIDE, NODES_PER_SIDE, NODES_PER_SIDE, AXIAL_ELEMENTS, AZIMUTH_ELEMENTS, RADIAL_ELEMENTS), 1.0, 6.0, ((4, 16), (5, 2)), jnp.float32)
    diffusivity = jnp.clip(jnp.exp(math.log(10.0) - 2.3025851 * jax.random.uniform(splits[1], (NODES_PER_SIDE, NODES_PER_SIDE, NODES_PER_SIDE, AXIAL_ELEMENTS, AZIMUTH_ELEMENTS, RADIAL_ELEMENTS), jnp.float32) ** shard_levels(splits[1], (NODES_PER_SIDE, NODES_PER_SIDE, NODES_PER_SIDE, AXIAL_ELEMENTS, AZIMUTH_ELEMENTS, RADIAL_ELEMENTS), ((3, 16), (4, 2)), -0.2, 0.2)), 1.0, 10.0)
    coarse_factor = centred(splits[2], (NC, NC), (NC * 256) ** -0.5, 0.0625, ((0, 32),), jnp.float32)
    return {"velocity": velocity, "diffusivity": diffusivity, "coarse_factor": coarse_factor}


HIGHEST = lax.Precision.HIGHEST
time_increment = 0.02
mass_shift = 0.05
gll_points = [-1.0, -0.8717401485096066, -0.5917001814331423, -0.20929921790247888, 0.20929921790247888, 0.5917001814331423, 0.8717401485096066, 1.0]

def legendre_value(order, point):
    before = 1.0
    current = point
    for step_idx in range(1, order):
        after = ((2 * step_idx + 1) * point * current - step_idx * before) / (step_idx + 1)
        before = current
        current = after
    return current

def jacobi_eigen(matrix):
    size_n = len(matrix)
    work = [list(row) for row in matrix]
    vectors = [[1.0 if row_idx == col_idx else 0.0 for col_idx in range(size_n)] for row_idx in range(size_n)]
    for sweep_idx in range(15):
        for row_idx in range(size_n):
            for col_idx in range(row_idx + 1, size_n):
                off_value = work[row_idx][col_idx]
                if off_value != 0.0:
                    theta = (work[col_idx][col_idx] - work[row_idx][row_idx]) / (2.0 * off_value)
                    root_val = math.sqrt(theta * theta + 1.0)
                    tangent = 1.0 / (theta + root_val) if theta >= 0.0 else 1.0 / (theta - root_val)
                    cosine = 1.0 / math.sqrt(tangent * tangent + 1.0)
                    sine = tangent * cosine
                    for other in range(size_n):
                        left_val = work[other][row_idx]
                        right_val = work[other][col_idx]
                        work[other][row_idx] = cosine * left_val - sine * right_val
                        work[other][col_idx] = sine * left_val + cosine * right_val
                    for other in range(size_n):
                        left_val = work[row_idx][other]
                        right_val = work[col_idx][other]
                        work[row_idx][other] = cosine * left_val - sine * right_val
                        work[col_idx][other] = sine * left_val + cosine * right_val
                    for other in range(size_n):
                        left_val = vectors[other][row_idx]
                        right_val = vectors[other][col_idx]
                        vectors[other][row_idx] = cosine * left_val - sine * right_val
                        vectors[other][col_idx] = sine * left_val + cosine * right_val
    return ([work[row_idx][row_idx] for row_idx in range(size_n)], vectors)

def gll_tables():
    degree = 7
    points = degree + 1
    legendre_at = [legendre_value(degree, node_val) for node_val in gll_points]
    weights = [2.0 / (degree * (degree + 1) * value * value) for value in legendre_at]
    derivative = [[0.0] * points for row_idx in range(points)]
    for row_idx in range(points):
        for col_idx in range(points):
            if row_idx != col_idx:
                derivative[row_idx][col_idx] = legendre_at[row_idx] / (legendre_at[col_idx] * (gll_points[row_idx] - gll_points[col_idx]))
    derivative[0][0] = -degree * (degree + 1) / 4.0
    derivative[degree][degree] = degree * (degree + 1) / 4.0
    stiffness = [[sum((derivative[mid_idx][row_idx] * weights[mid_idx] * derivative[mid_idx][col_idx] for mid_idx in range(points))) for col_idx in range(points)] for row_idx in range(points)]
    line_len = 3 * degree + 1
    big_stiff = [[0.0] * line_len for row_idx in range(line_len)]
    big_mass = [0.0] * line_len
    for element in range(3):
        offset = element * degree
        for row_idx in range(points):
            big_mass[offset + row_idx] += weights[row_idx]
            for col_idx in range(points):
                big_stiff[offset + row_idx][offset + col_idx] += stiffness[row_idx][col_idx]
    start_node = degree - 1
    box_len = degree + 3
    scaling = [1.0 / math.sqrt(big_mass[start_node + row_idx]) for row_idx in range(box_len)]
    symmetric = [[scaling[row_idx] * big_stiff[start_node + row_idx][start_node + col_idx] * scaling[col_idx] for col_idx in range(box_len)] for row_idx in range(box_len)]
    eigval, eigvec = jacobi_eigen(symmetric)
    fdm_basis = [[scaling[row_idx] * eigvec[row_idx][col_idx] for col_idx in range(box_len)] for row_idx in range(box_len)]
    return (weights, derivative, fdm_basis, eigval)

def device_tables():
    weights, derivative, fdm_basis, eigval = gll_tables()
    return (jnp.asarray(weights, dtype=jnp.float32), jnp.asarray(derivative, dtype=jnp.float32), jnp.asarray(fdm_basis, dtype=jnp.float32), jnp.asarray(eigval, dtype=jnp.float32))

def along(matrix, values, axis):
    letters = 'abcdefgh'[:values.ndim]
    source = letters[axis]
    target = letters.replace(source, 'z')
    return jnp.einsum('z' + source + ',' + letters + '->' + target, matrix, values, precision=HIGHEST)

def element_weights(weights):
    cube = weights[:, None, None] * weights[None, :, None] * weights[None, None, :]
    return cube[:, :, :, None, None, None]

def multiplicity(radial_count):
    node_ids = jnp.arange(8)
    ends = jnp.where((node_ids == 0) | (node_ids == 7), 2.0, 1.0).astype(jnp.float32)
    layer_ids = node_ids[:, None]
    elem_ids = jnp.arange(radial_count)[None, :]
    radial_coordinate = jnp.where((layer_ids == 0) & (elem_ids > 0) | (layer_ids == 7) & (elem_ids < radial_count - 1), 2.0, 1.0).astype(jnp.float32)
    return ends[:, None, None, None, None, None] * ends[None, :, None, None, None, None] * radial_coordinate[None, None, :, None, None, :]

def place(face_vals, position, axis):
    one_hot = (jnp.arange(8) == position).astype(jnp.float32)
    hot_shape = [1] * (face_vals.ndim + 1)
    hot_shape[axis] = 8
    return jnp.expand_dims(face_vals, axis) * one_hot.reshape(hot_shape)

def build_box(center, layers):
    dim_count = center.ndim
    left_layer, right_layer = layers[0]
    box_field = jnp.concatenate([left_layer[None], center, right_layer[None]], axis=0)
    pad_first = [(1, 1), (0, 0)] + [(0, 0)] * (dim_count - 3)
    left_layer, right_layer = layers[1]
    box_field = jnp.concatenate([jnp.pad(left_layer, pad_first)[:, None], box_field, jnp.pad(right_layer, pad_first)[:, None]], axis=1)
    pad_second = [(1, 1), (1, 1)] + [(0, 0)] * (dim_count - 3)
    left_layer, right_layer = layers[2]
    box_field = jnp.concatenate([jnp.pad(left_layer, pad_second)[:, :, None], box_field, jnp.pad(right_layer, pad_second)[:, :, None]], axis=2)
    return box_field

def solve_box(box_field, mean_coef, fdm_basis, eigval):
    spectral = along(fdm_basis.T, box_field, 0)
    spectral = along(fdm_basis.T, spectral, 1)
    spectral = along(fdm_basis.T, spectral, 2)
    spectrum = eigval[:, None, None] + eigval[None, :, None] + eigval[None, None, :]
    spectrum = spectrum.reshape((10, 10, 10) + (1,) * (box_field.ndim - 3))
    spectral = spectral / (mean_coef[None, None, None] * spectrum + mass_shift)
    solved = along(fdm_basis, spectral, 0)
    solved = along(fdm_basis, solved, 1)
    return along(fdm_basis, solved, 2)

def box_faces(solved, node):
    if node == 0:
        return (solved[0, 1:9, 1:9], solved[9, 1:9, 1:9])
    if node == 1:
        return (solved[1:9, 0, 1:9], solved[1:9, 9, 1:9])
    return (solved[1:9, 1:9, 0], solved[1:9, 1:9, 9])

def apply_local(values, diffusivity, element_quadrature, derivative):
    total = along(derivative.T, element_quadrature * diffusivity * along(derivative, values, 0), 0)
    total = total + along(derivative.T, element_quadrature * diffusivity * along(derivative, values, 1), 1)
    total = total + along(derivative.T, element_quadrature * diffusivity * along(derivative, values, 2), 2)
    return total + mass_shift * element_quadrature * values

def ref_neighbours(low, high, axis, wrap):
    if wrap:
        return (jnp.roll(high, 1, axis), jnp.roll(low, -1, axis))
    count = low.shape[axis]
    empty_piece = jnp.zeros_like(lax.slice_in_dim(low, 0, 1, axis=axis))
    prev_high = jnp.concatenate([empty_piece, lax.slice_in_dim(high, 0, count - 1, axis=axis)], axis)
    next_low = jnp.concatenate([lax.slice_in_dim(low, 1, count, axis=axis), empty_piece], axis)
    return (prev_high, next_low)

def assemble(stack):
    for node in (1, 2, 3):
        low = lax.index_in_dim(stack, 0, node, keepdims=False)
        high = lax.index_in_dim(stack, 7, node, keepdims=False)
        prev_high, next_low = ref_neighbours(low, high, node + 2, node < 3)
        new_low = low + prev_high
        new_high = high + next_low
        middle = lax.slice_in_dim(stack, 1, 7, axis=node)
        stack = jnp.concatenate([jnp.expand_dims(new_low, node), middle, jnp.expand_dims(new_high, node)], node)
    return stack

def precondition(residual, diffusivity, inv_mult, coarse_factor, fdm_basis, eigval):
    stacked = residual[None]
    layers = []
    for node in range(3):
        six_layer = lax.index_in_dim(stacked, 6, node + 1, keepdims=False)
        one_layer = lax.index_in_dim(stacked, 1, node + 1, keepdims=False)
        left_layer, right_layer = ref_neighbours(one_layer, six_layer, node + 3, node < 2)
        layers.append((left_layer[0], right_layer[0]))
    box_field = build_box(residual, layers)
    mean_coef = lax.optimization_barrier(jnp.mean(diffusivity, axis=(0, 1, 2)))
    solved = solve_box(box_field, mean_coef, fdm_basis, eigval)
    local_part = solved[1:9, 1:9, 1:9]
    for node in range(3):
        low_face, high_face = box_faces(solved, node)
        prev_high, next_low = ref_neighbours(low_face[None], high_face[None], node + 3, node < 2)
        local_part = local_part + place(prev_high[0], 1, node) + place(next_low[0], 6, node)
    weighted = inv_mult * residual
    blocks = weighted.reshape(8, 8, 8, N_AXIAL, EA, N_AZIM, EZ, RADIAL_ELEMENTS)
    per_block = lax.optimization_barrier(jnp.sum(blocks, axis=(0, 1, 2, 4, 6, 7))).reshape(NC)
    coarse_vec = jnp.dot(per_block, coarse_factor, precision=HIGHEST)
    correction = jnp.dot(coarse_factor, coarse_vec, precision=HIGHEST).reshape(N_AXIAL, N_AZIM)
    spread = jnp.repeat(jnp.repeat(correction, EA, axis=0), EZ, axis=1)[None, None, None, :, :, None]
    smooth = assemble((local_part + inv_mult * spread)[None])[0]
    return (smooth, jnp.sum(inv_mult * residual * smooth))

def reference(velocity, diffusivity, coarse_factor):
    weights, derivative, fdm_basis, eigval = device_tables()
    element_quadrature = element_weights(weights)
    mult = multiplicity(velocity.shape[-1])
    inv_mult = 1.0 / mult
    components = [velocity[0], velocity[1], velocity[2]]
    conv_terms = jnp.stack([element_quadrature * (components[0] * along(derivative, component, 0) + components[1] * along(derivative, component, 1) + components[2] * along(derivative, component, 2)) for component in components])
    convection = assemble(conv_terms) / (element_quadrature * mult)
    moved = velocity - time_increment * convection
    divergence = along(derivative.T, element_quadrature * moved[0], 0) + along(derivative.T, element_quadrature * moved[1], 1) + along(derivative.T, element_quadrature * moved[2], 2)
    source_term = assemble(divergence[None])[0]
    pressure = jnp.zeros_like(source_term)
    residual = source_term
    smooth, rz_now = precondition(residual, diffusivity, inv_mult, coarse_factor, fdm_basis, eigval)
    direction = smooth
    for step in range(ITERS):
        image = assemble(apply_local(direction, diffusivity, element_quadrature, derivative)[None])[0]
        alpha = rz_now / jnp.sum(inv_mult * direction * image)
        pressure = pressure + alpha * direction
        residual = residual - alpha * image
        smooth, rz_next = precondition(residual, diffusivity, inv_mult, coarse_factor, fdm_basis, eigval)
        direction = smooth + rz_next / rz_now * direction
        rz_now = rz_next
    return (pressure, residual, direction)
```

```python
import math

import jax
import jax.numpy as jnp
import numpy as np
from jax import lax
from jax.sharding import PartitionSpec as P

HIGHEST = lax.Precision.HIGHEST
ALL = ("axial", "azim")
time_increment = 0.02
mass_shift = 0.05
gll_points = [
    -1.0,
    -0.8717401485096066,
    -0.5917001814331423,
    -0.20929921790247888,
    0.20929921790247888,
    0.5917001814331423,
    0.8717401485096066,
    1.0,
]


def legendre_value(order, point):
    before = 1.0
    current = point
    for step_idx in range(1, order):
        after = ((2 * step_idx + 1) * point * current - step_idx * before) / (step_idx + 1)
        before = current
        current = after
    return current


def jacobi_eigen(matrix):
    size_n = len(matrix)
    work = [list(row) for row in matrix]
    vectors = [
        [1.0 if row_idx == col_idx else 0.0 for col_idx in range(size_n)]
        for row_idx in range(size_n)
    ]
    for sweep_idx in range(15):
        for row_idx in range(size_n):
            for col_idx in range(row_idx + 1, size_n):
                off_value = work[row_idx][col_idx]
                if off_value != 0.0:
                    theta = (work[col_idx][col_idx] - work[row_idx][row_idx]) / (2.0 * off_value)
                    root_val = math.sqrt(theta * theta + 1.0)
                    tangent = 1.0 / (theta + root_val) if theta >= 0.0 else 1.0 / (theta - root_val)
                    cosine = 1.0 / math.sqrt(tangent * tangent + 1.0)
                    sine = tangent * cosine
                    for other in range(size_n):
                        left_val = work[other][row_idx]
                        right_val = work[other][col_idx]
                        work[other][row_idx] = cosine * left_val - sine * right_val
                        work[other][col_idx] = sine * left_val + cosine * right_val
                    for other in range(size_n):
                        left_val = work[row_idx][other]
                        right_val = work[col_idx][other]
                        work[row_idx][other] = cosine * left_val - sine * right_val
                        work[col_idx][other] = sine * left_val + cosine * right_val
                    for other in range(size_n):
                        left_val = vectors[other][row_idx]
                        right_val = vectors[other][col_idx]
                        vectors[other][row_idx] = cosine * left_val - sine * right_val
                        vectors[other][col_idx] = sine * left_val + cosine * right_val
    return ([work[row_idx][row_idx] for row_idx in range(size_n)], vectors)


def gll_tables():
    degree = 7
    points = degree + 1
    legendre_at = [legendre_value(degree, node_val) for node_val in gll_points]
    weights = [2.0 / (degree * (degree + 1) * value * value) for value in legendre_at]
    derivative = [[0.0] * points for row_idx in range(points)]
    for row_idx in range(points):
        for col_idx in range(points):
            if row_idx != col_idx:
                derivative[row_idx][col_idx] = legendre_at[row_idx] / (
                    legendre_at[col_idx] * (gll_points[row_idx] - gll_points[col_idx])
                )
    derivative[0][0] = -degree * (degree + 1) / 4.0
    derivative[degree][degree] = degree * (degree + 1) / 4.0
    stiffness = [
        [
            sum(
                (
                    derivative[mid_idx][row_idx] * weights[mid_idx] * derivative[mid_idx][col_idx]
                    for mid_idx in range(points)
                )
            )
            for col_idx in range(points)
        ]
        for row_idx in range(points)
    ]
    line_len = 3 * degree + 1
    big_stiff = [[0.0] * line_len for row_idx in range(line_len)]
    big_mass = [0.0] * line_len
    for element in range(3):
        offset = element * degree
        for row_idx in range(points):
            big_mass[offset + row_idx] += weights[row_idx]
            for col_idx in range(points):
                big_stiff[offset + row_idx][offset + col_idx] += stiffness[row_idx][col_idx]
    start_node = degree - 1
    box_len = degree + 3
    scaling = [1.0 / math.sqrt(big_mass[start_node + row_idx]) for row_idx in range(box_len)]
    symmetric = [
        [
            scaling[row_idx]
            * big_stiff[start_node + row_idx][start_node + col_idx]
            * scaling[col_idx]
            for col_idx in range(box_len)
        ]
        for row_idx in range(box_len)
    ]
    eigval, eigvec = jacobi_eigen(symmetric)
    fdm_basis = [
        [scaling[row_idx] * eigvec[row_idx][col_idx] for col_idx in range(box_len)]
        for row_idx in range(box_len)
    ]
    return (weights, derivative, fdm_basis, eigval)

WEIGHTS, DERIV, BASIS, EIGVAL = (np.asarray(t, np.float64) for t in gll_tables())
CUBE = (WEIGHTS[:, None, None] * WEIGHTS[None, :, None] * WEIGHTS[None, None, :])[..., None]
SHARE = np.zeros((8, 3))
SHARE[:, 1] = 1.0
SHARE[0] = (0.5, 0.5, 0.0)
SHARE[7] = (0.0, 0.5, 0.5)


def f32(table):
    return jnp.asarray(table, jnp.float32)


def along(matrix, values, axis):
    letters = "abcdefgh"[: values.ndim]
    source = letters[axis]
    target = letters.replace(source, "z")
    return jnp.einsum(
        "z" + source + "," + letters + "->" + target, f32(matrix), values, precision=HIGHEST
    )


def axial_exchange(low, high):
    count = lax.axis_size("axial")
    even = lax.axis_index("axial") % 2 == 0
    inner = [(i, i ^ 1) for i in range(count)]
    outer = [((2 * i + 1) % count, (2 * i + 2) % count) for i in range(count // 2)]
    outer = outer + [(b, a) for a, b in outer]
    from_inner = lax.ppermute(jnp.where(even, high, low), "axial", inner)
    from_outer = lax.ppermute(jnp.where(even, low, high), "axial", outer)
    return jnp.where(even, from_outer, from_inner), jnp.where(even, from_inner, from_outer)


def azim_exchange(low, high):
    count = lax.axis_size("azim")
    if count == 2:
        got = lax.ppermute(jnp.stack([low, high]), "azim", [(0, 1), (1, 0)])
        return got[1], got[0]
    before = lax.ppermute(high, "azim", [(i, (i + 1) % count) for i in range(count)])
    after = lax.ppermute(low, "azim", [((i + 1) % count, i) for i in range(count)])
    return before, after


def global_sum(vector):
    count = lax.axis_size("axial") * lax.axis_size("azim")
    size = vector.shape[0]
    padded = -(-size // 128) * 128
    row = jnp.pad(vector, (0, padded - size))
    rows = jnp.broadcast_to(row, (count, padded))
    return lax.all_to_all(rows, ALL, 0, 0, tiled=True).sum(0)[:size]


def lane_before(values):
    return jnp.pad(values, [(0, 0)] * (values.ndim - 1) + [(1, 0)])[..., :-1]


def lane_after(values):
    return jnp.pad(values, [(0, 0)] * (values.ndim - 1) + [(0, 1)])[..., 1:]


def radial_assemble(values):
    low = values[..., :1, :] + lane_before(values[..., 7:, :])
    high = values[..., 7:, :] + lane_after(values[..., :1, :])
    return jnp.concatenate([low, values[..., 1:7, :], high], -2)


def assemble_with_halo(raw):
    g = radial_assemble(raw)
    before, after = axial_exchange(jnp.stack([g[0], g[1]]), jnp.stack([g[7], g[6]]))
    wide = jnp.concatenate(
        [before[1][None], (g[0] + before[0])[None], g[1:7], (g[7] + after[0])[None], after[1][None]]
    )
    low = jnp.concatenate([wide[:, 0], wide[1:9, 1]])
    high = jnp.concatenate([wide[:, 7], wide[1:9, 6]])
    prev, following = azim_exchange(low, high)
    wide = jnp.concatenate(
        [
            (wide[:, 0] + prev[:10])[:, None],
            wide[:, 1:7],
            (wide[:, 7] + following[:10])[:, None],
        ],
        1,
    )
    return (
        wide[1:9],
        jnp.stack([wide[0], wide[9]]),
        jnp.stack([prev[10:], following[10:]]),
    )


def assemble_boxes(solved):
    part = solved[1:9, 1:9, 1:9]
    first = lane_before(solved[1:9, 1:9, 9:10])
    last = lane_after(solved[1:9, 1:9, 0:1])
    part = jnp.concatenate(
        [part[:, :, :1], part[:, :, 1:2] + first, part[:, :, 2:6], part[:, :, 6:7] + last, part[:, :, 7:]],
        2,
    )
    part = radial_assemble(part)
    faces_a = radial_assemble(jnp.stack([solved[0, 1:9, 1:9], solved[9, 1:9, 1:9]]))
    faces_b = radial_assemble(jnp.stack([solved[1:9, 0, 1:9], solved[1:9, 9, 1:9]]))
    before, after = axial_exchange(
        jnp.concatenate([part[0], faces_a[0], faces_b[:, 0]]),
        jnp.concatenate([part[7], faces_a[1], faces_b[:, 7]]),
    )
    part = jnp.concatenate(
        [
            (part[0] + before[:8])[None],
            (part[1] + before[8:16])[None],
            part[2:6],
            (part[6] + after[8:16])[None],
            (part[7] + after[:8])[None],
        ]
    )
    faces_b = jnp.concatenate(
        [
            (faces_b[:, 0] + before[16:])[:, None],
            faces_b[:, 1:7],
            (faces_b[:, 7] + after[16:])[:, None],
        ],
        1,
    )
    prev, following = azim_exchange(
        jnp.concatenate([part[:, 0], faces_b[0]]), jnp.concatenate([part[:, 7], faces_b[1]])
    )
    return jnp.concatenate(
        [
            (part[:, 0] + prev[:8])[:, None],
            (part[:, 1] + prev[8:])[:, None],
            part[:, 2:6],
            (part[:, 6] + following[8:])[:, None],
            (part[:, 7] + following[:8])[:, None],
        ],
        1,
    )


def make_box(field, halo_a, halo_b):
    box = jnp.concatenate([halo_a[:1], field, halo_a[1:]])
    pad_a = [(1, 1), (0, 0), (0, 0)]
    box = jnp.concatenate(
        [jnp.pad(halo_b[0], pad_a)[:, None], box, jnp.pad(halo_b[1], pad_a)[:, None]], 1
    )
    pad_ab = [(1, 1), (1, 1), (0, 0), (0, 0)]
    first = jnp.pad(lane_before(field[:, :, 6:7]), pad_ab)
    last = jnp.pad(lane_after(field[:, :, 1:2]), pad_ab)
    return jnp.concatenate([first, box, last], 2)


def solve_box(box, mean_coef):
    spectral = box
    for axis in range(3):
        spectral = along(BASIS.T, spectral, axis)
    spectrum = EIGVAL[:, None, None] + EIGVAL[None, :, None] + EIGVAL[None, None, :]
    spectral = spectral / (mean_coef * f32(spectrum)[..., None] + mass_shift)
    for axis in range(3):
        spectral = along(BASIS, spectral, axis)
    return spectral


def apply_local(values, coef):
    total = mass_shift * f32(CUBE) * values
    for axis in range(3):
        total = total + along(DERIV.T, coef * along(DERIV, values, axis), axis)
    return total


def per_device(velocity, diffusivity, coarse_factor):
    radial = velocity.shape[-1]
    coarse_size = coarse_factor.shape[1]
    u = velocity.reshape(3, 8, 8, 8, radial)
    diff = diffusivity.reshape(8, 8, 8, radial)
    cube = f32(CUBE)
    conv = jnp.stack([cube * sum(u[d] * along(DERIV, u[c], d) for d in range(3)) for c in range(3)])
    conv = radial_assemble(conv)
    blocks = -(-coarse_size // (8 * radial))
    row = jnp.pad(coarse_factor[0], (0, blocks * 8 * radial - coarse_size)).reshape(blocks, 8, radial)
    before, after = axial_exchange(
        jnp.concatenate([conv[:, 0].reshape(24, 8, radial), row]),
        jnp.concatenate([conv[:, 7].reshape(24, 8, radial), row]),
    )
    conv = jnp.concatenate(
        [
            (conv[:, 0] + before[:24].reshape(3, 8, 8, radial))[:, None],
            conv[:, 1:7],
            (conv[:, 7] + after[:24].reshape(3, 8, 8, radial))[:, None],
        ],
        1,
    )
    rows = jnp.concatenate([before[24:], row, after[24:]])
    prev, following = azim_exchange(
        jnp.concatenate([conv[:, :, 0].reshape(24, 8, radial), rows]),
        jnp.concatenate([conv[:, :, 7].reshape(24, 8, radial), rows]),
    )
    conv = jnp.concatenate(
        [
            (conv[:, :, 0] + prev[:24].reshape(3, 8, 8, radial))[:, :, None],
            conv[:, :, 1:7],
            (conv[:, :, 7] + following[:24].reshape(3, 8, 8, radial))[:, :, None],
        ],
        2,
    )
    near = jnp.stack([prev[24:], rows, following[24:]])
    near = near.reshape(3, 3, -1)[:, :, :coarse_size]
    weights = np.einsum("ai,bj->abji", SHARE, SHARE).reshape(64, 9)
    prolong = jnp.dot(f32(weights), near.reshape(9, coarse_size), precision=HIGHEST)

    def coarse_share(raw):
        sums = jnp.sum(raw, axis=(2, 3)).reshape(64)
        return jnp.dot(sums, prolong, precision=HIGHEST)

    def coarse_field(vector):
        return jnp.dot(prolong, vector, precision=HIGHEST).reshape(8, 8, 1, 1)

    ends = np.array([2.0, 1, 1, 1, 1, 1, 1, 2.0])
    mult_r = np.ones((8, radial))
    mult_r[0, 1:] = 2.0
    mult_r[7, :-1] = 2.0
    mult = ends[:, None, None, None] * ends[None, :, None, None] * mult_r[None, None]
    moved = cube * u - time_increment * conv / f32(mult)
    raw = sum(along(DERIV.T, moved[d], d) for d in range(3))
    mean_coef = jnp.mean(diff, axis=(0, 1, 2))
    coef = cube * diff

    coarse_r = global_sum(coarse_share(raw))
    field_r, halo_ra, halo_rb = assemble_with_halo(raw)
    box_r = make_box(field_r, halo_ra, halo_rb)
    solved = solve_box(box_r, mean_coef)
    local_rz = jnp.sum(box_r * solved)
    d0 = assemble_boxes(solved) + coarse_field(coarse_r)

    raw = apply_local(d0, coef)
    raw0 = raw
    got = global_sum(jnp.concatenate([coarse_share(raw), jnp.stack([local_rz, jnp.sum(d0 * raw)])]))
    coarse_q = got[:coarse_size]
    rz0 = got[coarse_size] + jnp.sum(coarse_r * coarse_r)
    curv0 = got[coarse_size + 1]
    alpha0 = rz0 / curv0
    field_q, halo_qa, halo_qb = assemble_with_halo(raw)
    field_r = field_r - alpha0 * field_q
    halo_ra = halo_ra - alpha0 * halo_qa
    halo_rb = halo_rb - alpha0 * halo_qb
    coarse_r = coarse_r - alpha0 * coarse_q
    box_r = make_box(field_r, halo_ra, halo_rb)
    solved = solve_box(box_r, mean_coef)
    local_rz = jnp.sum(box_r * solved)
    z1 = assemble_boxes(solved) + coarse_field(coarse_r)

    raw = apply_local(z1, coef)
    got = global_sum(
        jnp.concatenate(
            [coarse_share(raw), jnp.stack([local_rz, jnp.sum(z1 * raw), jnp.sum(z1 * raw0)])]
        )
    )
    rz1 = got[coarse_size] + jnp.sum(coarse_r * coarse_r)
    beta0 = rz1 / rz0
    curv1 = got[coarse_size + 1] + beta0 * (2.0 * got[coarse_size + 2] + beta0 * curv0)
    alpha1 = rz1 / curv1
    coarse_r = coarse_r - alpha1 * (got[:coarse_size] + beta0 * coarse_q)
    field_w, halo_wa, halo_wb = assemble_with_halo(raw)
    field_r = field_r - alpha1 * (field_w + beta0 * field_q)
    halo_ra = halo_ra - alpha1 * (halo_wa + beta0 * halo_qa)
    halo_rb = halo_rb - alpha1 * (halo_wb + beta0 * halo_qb)
    box_r = make_box(field_r, halo_ra, halo_rb)
    solved = solve_box(box_r, mean_coef)
    got = global_sum(jnp.sum(box_r * solved)[None])
    rz2 = got[0] + jnp.sum(coarse_r * coarse_r)
    z2 = assemble_boxes(solved) + coarse_field(coarse_r)
    d1 = z1 + beta0 * d0
    pressure = alpha0 * d0 + alpha1 * d1
    direction = z2 + rz2 / rz1 * d1
    shape = diffusivity.shape
    return pressure.reshape(shape), field_r.reshape(shape), direction.reshape(shape)


def solution(mesh):
    split = P(None, None, None, "axial", "azim", None)
    in_specs = (P(None, None, None, None, "axial", "azim", None), split, P(ALL, None))
    return jax.shard_map(
        per_device, mesh=mesh, in_specs=in_specs, out_specs=(split, split, split), check_vma=False
    )
```

```python
import math

import jax
import jax.numpy as jnp
import numpy as np
from jax import lax
from jax.experimental import pallas as pl
from jax.experimental.pallas import tpu as pltpu
from jax.sharding import PartitionSpec as P

ALL = ("axial", "azim")
time_increment = 0.02
mass_shift = 0.05
VMEM_GRANT = 20 << 20
gll_points = [
    -1.0,
    -0.8717401485096066,
    -0.5917001814331423,
    -0.20929921790247888,
    0.20929921790247888,
    0.5917001814331423,
    0.8717401485096066,
    1.0,
]


def legendre_value(order, point):
    before = 1.0
    current = point
    for step_idx in range(1, order):
        after = ((2 * step_idx + 1) * point * current - step_idx * before) / (step_idx + 1)
        before = current
        current = after
    return current


def jacobi_eigen(matrix):
    size_n = len(matrix)
    work = [list(row) for row in matrix]
    vectors = [
        [1.0 if row_idx == col_idx else 0.0 for col_idx in range(size_n)]
        for row_idx in range(size_n)
    ]
    for sweep_idx in range(15):
        for row_idx in range(size_n):
            for col_idx in range(row_idx + 1, size_n):
                off_value = work[row_idx][col_idx]
                if off_value != 0.0:
                    theta = (work[col_idx][col_idx] - work[row_idx][row_idx]) / (2.0 * off_value)
                    root_val = math.sqrt(theta * theta + 1.0)
                    tangent = 1.0 / (theta + root_val) if theta >= 0.0 else 1.0 / (theta - root_val)
                    cosine = 1.0 / math.sqrt(tangent * tangent + 1.0)
                    sine = tangent * cosine
                    for other in range(size_n):
                        left_val = work[other][row_idx]
                        right_val = work[other][col_idx]
                        work[other][row_idx] = cosine * left_val - sine * right_val
                        work[other][col_idx] = sine * left_val + cosine * right_val
                    for other in range(size_n):
                        left_val = work[row_idx][other]
                        right_val = work[col_idx][other]
                        work[row_idx][other] = cosine * left_val - sine * right_val
                        work[col_idx][other] = sine * left_val + cosine * right_val
                    for other in range(size_n):
                        left_val = vectors[other][row_idx]
                        right_val = vectors[other][col_idx]
                        vectors[other][row_idx] = cosine * left_val - sine * right_val
                        vectors[other][col_idx] = sine * left_val + cosine * right_val
    return ([work[row_idx][row_idx] for row_idx in range(size_n)], vectors)


def gll_tables():
    degree = 7
    points = degree + 1
    legendre_at = [legendre_value(degree, node_val) for node_val in gll_points]
    weights = [2.0 / (degree * (degree + 1) * value * value) for value in legendre_at]
    derivative = [[0.0] * points for row_idx in range(points)]
    for row_idx in range(points):
        for col_idx in range(points):
            if row_idx != col_idx:
                derivative[row_idx][col_idx] = legendre_at[row_idx] / (
                    legendre_at[col_idx] * (gll_points[row_idx] - gll_points[col_idx])
                )
    derivative[0][0] = -degree * (degree + 1) / 4.0
    derivative[degree][degree] = degree * (degree + 1) / 4.0
    stiffness = [
        [
            sum(
                (
                    derivative[mid_idx][row_idx] * weights[mid_idx] * derivative[mid_idx][col_idx]
                    for mid_idx in range(points)
                )
            )
            for col_idx in range(points)
        ]
        for row_idx in range(points)
    ]
    line_len = 3 * degree + 1
    big_stiff = [[0.0] * line_len for row_idx in range(line_len)]
    big_mass = [0.0] * line_len
    for element in range(3):
        offset = element * degree
        for row_idx in range(points):
            big_mass[offset + row_idx] += weights[row_idx]
            for col_idx in range(points):
                big_stiff[offset + row_idx][offset + col_idx] += stiffness[row_idx][col_idx]
    start_node = degree - 1
    box_len = degree + 3
    scaling = [1.0 / math.sqrt(big_mass[start_node + row_idx]) for row_idx in range(box_len)]
    symmetric = [
        [
            scaling[row_idx]
            * big_stiff[start_node + row_idx][start_node + col_idx]
            * scaling[col_idx]
            for col_idx in range(box_len)
        ]
        for row_idx in range(box_len)
    ]
    eigval, eigvec = jacobi_eigen(symmetric)
    fdm_basis = [
        [scaling[row_idx] * eigvec[row_idx][col_idx] for col_idx in range(box_len)]
        for row_idx in range(box_len)
    ]
    return (weights, derivative, fdm_basis, eigval)

WEIGHTS, DERIV, BASIS, EIGVAL = (np.asarray(t, np.float64) for t in gll_tables())


def f32(table):
    return jnp.asarray(table, jnp.float32)


F32 = jnp.float32
BF16 = jnp.bfloat16
LANES = 128
INTERPRET = False


def split_terms(table, depth):
    padded = np.zeros((table.shape[0], depth))
    padded[:, : table.shape[1]] = table
    high = padded.astype(jnp.bfloat16)
    low = (padded - high.astype(np.float64)).astype(jnp.bfloat16)
    return jnp.asarray(np.concatenate([high, high, low], axis=1))


def box_tables():
    pairs = [(b + 1, c + 1) for b in range(8) for c in range(8)]
    pairs += [(b + 1, {6: 0, 1: 9}.get(c)) for b in range(8) for c in range(8)]
    pairs += [(0, c + 1) for c in range(8)] + [(9, c + 1) for c in range(8)]
    table = np.zeros((144, 112))
    for row, (b, c) in enumerate(pairs):
        if c is not None:
            table[row, :100] = np.outer(BASIS[b], BASIS[c]).reshape(100)
    sums = np.ones(112)
    sums[:100] = (EIGVAL[:, None] + EIGVAL[None, :]).reshape(100)
    return table, sums


EYE = np.eye(8)
GRAD = np.concatenate([np.kron(DERIV, EYE), np.kron(EYE, DERIV)])
BOX_ROWS, SPECTRUM = box_tables()
EVEN = [bool(abs(BASIS[0, i] - BASIS[9, i]) < abs(BASIS[0, i] + BASIS[9, i])) for i in range(10)]


def constant_tables(radial):
    plane = (WEIGHTS[:, None] * WEIGHTS[None, :]).reshape(64, 1)
    mult_r = np.ones((8, radial))
    mult_r[0, 1:] = 2.0
    mult_r[7, :-1] = 2.0
    ends = np.array([2.0, 1, 1, 1, 1, 1, 1, 2.0])
    mult = (ends[:, None, None] * mult_r[None]).reshape(64, radial)
    return dict(
        plane=f32(np.broadcast_to(plane, (64, radial))),
        over=f32(1.0 / mult),
        spectrum=f32(np.broadcast_to(SPECTRUM[:, None], (112, radial))),
        grad=split_terms(GRAD, 64),
        div=split_terms(GRAD.T, 128),
        into=split_terms(BOX_ROWS.T, 144),
        outof=split_terms(BOX_ROWS, 112),
    )


def product(table_ref, values):
    high = values.astype(BF16)
    low = (values - high.astype(F32)).astype(BF16)
    return jnp.dot(
        table_ref[...], jnp.concatenate([high, low, high], axis=0), preferred_element_type=F32
    )


def combine(coefs, terms):
    total = None
    for coef, term in zip(coefs, terms):
        scaled = float(coef) * term
        total = scaled if total is None else total + scaled
    return total


def skew_apply(matrix, parts):
    plus = [parts[b] + parts[7 - b] for b in range(4)]
    minus = [parts[b] - parts[7 - b] for b in range(4)]
    result = [None] * 8
    for a in range(4):
        even = combine([0.5 * (matrix[a, b] + matrix[a, 7 - b]) for b in range(4)], plus)
        odd = combine([0.5 * (matrix[a, b] - matrix[a, 7 - b]) for b in range(4)], minus)
        result[a] = even + odd
        result[7 - a] = odd - even
    return result


def to_spectral(parts):
    plus = [parts[a] + parts[9 - a] for a in range(5)]
    minus = [parts[a] - parts[9 - a] for a in range(5)]
    return [combine(BASIS[:5, i], plus if EVEN[i] else minus) for i in range(10)]


def from_spectral(parts):
    evens = [i for i in range(10) if EVEN[i]]
    odds = [i for i in range(10) if not EVEN[i]]
    result = [None] * 10
    for a in range(5):
        even = combine(BASIS[a, evens], [parts[i] for i in evens])
        odd = combine(BASIS[a, odds], [parts[i] for i in odds])
        result[a] = even + odd
        result[9 - a] = even - odd
    return result


def masks(rows):
    layer = lax.broadcasted_iota(jnp.int32, (rows, LANES), 0) % 8
    elem = lax.broadcasted_iota(jnp.int32, (rows, LANES), 1)
    return layer, elem > 0, elem < LANES - 1


def spread(values, first, last):
    layer, has_before, has_after = masks(values.shape[0])
    before = pltpu.roll(values, 1, axis=1)
    after = pltpu.roll(values, LANES - 1, axis=1)
    return jnp.where(
        (layer == first) & has_before,
        before,
        jnp.where((layer == last) & has_after, after, 0.0),
    )


def radial_sum(values):
    rows = values.shape[0]
    layer, _, _ = masks(rows)
    cubes = values.reshape(rows // 8, 8, LANES)
    up = pltpu.roll(cubes, 1, axis=1).reshape(rows, LANES)
    down = pltpu.roll(cubes, 7, axis=1).reshape(rows, LANES)
    return values + spread(jnp.where(layer == 0, up, down), 0, 7)


def total(values):
    return jnp.sum(values, axis=(0, 1), keepdims=True)


def add_rows(block, extra):
    pieces = []
    for b in range(8):
        piece = block[8 * b : 8 * b + 8]
        pieces.append(piece + extra[b] if b in extra else piece)
    return jnp.concatenate(pieces, axis=0)


def is_even():
    return lax.axis_index("axial") % 2 == 0


def send_axial(inner_ref, outer_ref, low, high):
    even = is_even()
    row = 0
    for low_piece, high_piece in zip(low, high):
        size = low_piece.shape[0]
        inner_ref[row : row + size] = jnp.where(even, high_piece, low_piece)
        outer_ref[row : row + size] = jnp.where(even, low_piece, high_piece)
        row += size


def got_axial(inner_ref, outer_ref):
    even = is_even()

    def before(start, size):
        return jnp.where(even, outer_ref[start : start + size], inner_ref[start : start + size])

    def after(start, size):
        return jnp.where(even, inner_ref[start : start + size], outer_ref[start : start + size])

    return before, after


def conv_kernel(u_ref, diff_ref, row_ref, plane_ref, grad_ref, conv_ref, kbar_ref, in_ref, out_ref, az_ref):
    plane = plane_ref[...]
    fields = [[u_ref[d, a] for a in range(8)] for d in range(3)]
    low, high = [], []
    for comp in range(3):
        parts = fields[comp]
        flat = product(grad_ref, jnp.concatenate(parts, axis=1))
        along_a = skew_apply(DERIV, parts)
        for a in range(8):
            cols = slice(LANES * a, LANES * a + LANES)
            value = (
                fields[0][a] * along_a[a]
                + fields[1][a] * flat[:64, cols]
                + fields[2][a] * flat[64:, cols]
            )
            value = radial_sum(float(WEIGHTS[a]) * plane * value)
            conv_ref[comp, a] = value
            start = 64 * comp + 8 * a
            az_ref[0, start : start + 8] = value[:8]
            az_ref[1, start : start + 8] = value[56:]
            if a == 0:
                low.append(value)
            if a == 7:
                high.append(value)
    row = row_ref[...]
    send_axial(in_ref, out_ref, low + [row], high + [row])
    mean = diff_ref[0]
    for a in range(1, 8):
        mean = mean + diff_ref[a]
    mean = jnp.sum(mean, axis=0, keepdims=True) * (1.0 / 512.0)
    kbar_ref[...] = jnp.broadcast_to(mean, (8, LANES))


def conv_side_kernel(in_ref, out_ref, az_ref, row_ref, send_ref):
    before, after = got_axial(in_ref, out_ref)
    count = row_ref.shape[0]
    for side, b in ((0, 0), (1, 7)):
        for comp in range(3):
            start = 64 * comp
            send_ref[side, start : start + 8] = az_ref[side, start : start + 8] + before(start + 8 * b, 8)
            send_ref[side, start + 8 : start + 56] = az_ref[side, start + 8 : start + 56]
            send_ref[side, start + 56 : start + 64] = az_ref[side, start + 56 : start + 64] + after(start + 8 * b, 8)
        for place, rows in enumerate((before(192, count), row_ref[...], after(192, count))):
            start = 192 + place * count
            send_ref[side, start : start + count] = rows


def coarse_share(raw, near_ref):
    middle = raw[1]
    for a in range(2, 7):
        middle = middle + raw[a]
    per_axial = (0.5 * raw[0], middle + 0.5 * (raw[0] + raw[7]), 0.5 * raw[7])
    rows = []
    for part in per_axial:
        inner = part[8:16]
        for b in range(2, 7):
            inner = inner + part[8 * b : 8 * b + 8]
        ends = (part[:8], part[56:])
        for piece in (0.5 * ends[0], inner + 0.5 * (ends[0] + ends[1]), 0.5 * ends[1]):
            rows.append(jnp.sum(piece, axis=0, keepdims=True))
    rows = jnp.concatenate(rows + [jnp.zeros((7, LANES), F32)], axis=0)
    shares = jnp.sum(rows, axis=1, keepdims=True)
    return jnp.sum(shares * near_ref[...], axis=0, keepdims=True)


def send_sums(pay_ref, row, scalars):
    width = pay_ref.shape[1]
    place = lax.broadcasted_iota(jnp.int32, (1, width), 1)
    for k, value in enumerate(scalars):
        row = jnp.where(place == width - 1 - k, value, row)
    pay_ref[...] = jnp.broadcast_to(row, pay_ref.shape)


def got_sums(ref, scalars):
    row = jnp.sum(ref[...], axis=0, keepdims=True)
    width = row.shape[1]
    place = lax.broadcasted_iota(jnp.int32, (1, width), 1)
    values = [
        jnp.sum(jnp.where(place == width - 1 - k, row, 0.0), axis=1, keepdims=True)
        for k in range(scalars)
    ]
    return jnp.where(place >= width - 4, 0.0, row), values


def send_raw(raw, g_ref, in_ref, out_ref, az_ref):
    parts = [radial_sum(raw[a]) for a in range(8)]
    for a in range(8):
        g_ref[a] = parts[a]
        for side, (edge, inner) in enumerate(((0, 1), (7, 6))):
            az_ref[side, 8 + 8 * a : 16 + 8 * a] = parts[a][8 * edge : 8 * edge + 8]
            az_ref[side, 80 + 8 * a : 88 + 8 * a] = parts[a][8 * inner : 8 * inner + 8]
    zero = jnp.zeros((8, LANES), F32)
    for side in range(2):
        az_ref[side, :8] = zero
        az_ref[side, 72:80] = zero
    send_axial(in_ref, out_ref, [parts[0], parts[1]], [parts[7], parts[6]])


def raw_side_kernel(in_ref, out_ref, az_ref, send_ref):
    before, after = got_axial(in_ref, out_ref)
    for side, (edge, inner) in enumerate(((0, 1), (7, 6))):
        send_ref[side, :8] = before(64 + 8 * edge, 8)
        send_ref[side, 8:16] = az_ref[side, 8:16] + before(8 * edge, 8)
        send_ref[side, 16:64] = az_ref[side, 16:64]
        send_ref[side, 64:72] = az_ref[side, 64:72] + after(8 * edge, 8)
        send_ref[side, 72:80] = after(64 + 8 * edge, 8)
        send_ref[side, 80:88] = az_ref[side, 80:88] + before(8 * inner, 8)
        send_ref[side, 88:136] = az_ref[side, 88:136]
        send_ref[side, 136:144] = az_ref[side, 136:144] + after(8 * inner, 8)


def divergence_kernel(
    conv_ref, u_ref, in_ref, out_ref, az_ref, row_ref, plane_ref, over_ref, div_ref,
    g_ref, send_in_ref, send_out_ref, send_az_ref, near_ref, pay_ref,
):
    before, after = got_axial(in_ref, out_ref)
    plane, over = plane_ref[...], over_ref[...]
    moved = []
    for comp in range(3):
        parts = []
        for a in range(8):
            value = conv_ref[comp, a]
            if a == 0:
                value = value + before(64 * comp, 64)
            if a == 7:
                value = value + after(64 * comp, 64)
            start = 64 * comp + 8 * a
            value = add_rows(value, {0: az_ref[1, start : start + 8], 7: az_ref[0, start : start + 8]})
            scale = time_increment * (0.5 if a in (0, 7) else 1.0)
            parts.append(float(WEIGHTS[a]) * plane * u_ref[comp, a] - scale * over * value)
        moved.append(parts)
    flat = product(
        div_ref,
        jnp.concatenate([jnp.concatenate(moved[1], axis=1), jnp.concatenate(moved[2], axis=1)], axis=0),
    )
    along_a = skew_apply(DERIV.T, moved[0])
    raw = [along_a[a] + flat[:, LANES * a : LANES * a + LANES] for a in range(8)]
    send_raw(raw, g_ref, send_in_ref, send_out_ref, send_az_ref)
    count = (az_ref.shape[1] - 192) // 3
    width = near_ref.shape[1] // LANES
    near_ref[...] = jnp.zeros(near_ref.shape, F32)
    for i in range(3):
        start = 192 + i * count
        middle = (before(192, count), row_ref[...], after(192, count))[i]
        sides = (az_ref[1, start : start + count], middle, az_ref[0, start : start + count])
        for j, rows in enumerate(sides):
            for k in range(width):
                near_ref[3 * i + j : 3 * i + j + 1, LANES * k : LANES * k + LANES] = rows[k : k + 1]
    send_sums(pay_ref, coarse_share(raw, near_ref), [])


def got_box(g_ref, in_ref, out_ref, az_ref):
    before, after = got_axial(in_ref, out_ref)
    center = []
    for a in range(8):
        value = g_ref[a]
        if a == 0:
            value = value + before(0, 64)
        if a == 7:
            value = value + after(0, 64)
        start = 8 + 8 * a
        center.append(
            add_rows(value, {0: az_ref[1, start : start + 8], 7: az_ref[0, start : start + 8]})
        )
    outer_a = [
        add_rows(before(64, 64), {0: az_ref[1, :8], 7: az_ref[0, :8]}),
        add_rows(after(64, 64), {0: az_ref[1, 72:80], 7: az_ref[0, 72:80]}),
    ]
    outer_b = [
        jnp.concatenate(
            [az_ref[1, 80 + 8 * a : 88 + 8 * a], az_ref[0, 80 + 8 * a : 88 + 8 * a]], axis=0
        )
        for a in range(8)
    ]
    return center, outer_a, outer_b


def put_box(box, center_ref, outer_a_ref, outer_b_ref):
    center, outer_a, outer_b = box
    for a in range(8):
        center_ref[a] = center[a]
        outer_b_ref[a] = outer_b[a]
    for k in range(2):
        outer_a_ref[k] = outer_a[k]


def take_box(center_ref, outer_a_ref, outer_b_ref):
    return (
        [center_ref[a] for a in range(8)],
        [outer_a_ref[k] for k in range(2)],
        [outer_b_ref[a] for a in range(8)],
    )


def add_box(first, scale, second):
    return tuple([x + scale * y for x, y in zip(xs, ys)] for xs, ys in zip(first, second))


def solve(box, kbar_ref, into_ref, outof_ref, spectrum_ref):
    center, outer_a, outer_b = box
    zero = jnp.zeros((80, LANES), F32)
    planes = [jnp.concatenate([outer_a[0], zero], axis=0)]
    for a in range(8):
        planes.append(jnp.concatenate([center[a], spread(center[a], 6, 1), outer_b[a]], axis=0))
    planes.append(jnp.concatenate([outer_a[1], zero], axis=0))
    rows = jnp.concatenate(planes, axis=1)
    flat = product(into_ref, rows)
    parts = to_spectral([flat[:, LANES * a : LANES * a + LANES] for a in range(10)])
    kbar = kbar_ref[0:1, :]
    plane_spectrum = kbar * spectrum_ref[...] + mass_shift
    parts = [parts[i] / (plane_spectrum + float(EIGVAL[i]) * kbar) for i in range(10)]
    parts = from_spectral(parts)
    flat = product(outof_ref, jnp.concatenate(parts, axis=1))
    solved = [flat[:, LANES * a : LANES * a + LANES] for a in range(10)]
    dot = None
    for a in range(10):
        stop = 64 if a in (0, 9) else 144
        term = planes[a][:stop] * solved[a][:stop]
        term = jnp.sum(term.reshape(stop // 8, 8, LANES), axis=0)
        dot = term if dot is None else dot + term
    return solved, dot


def send_solved(solved, part_ref, in_ref, out_ref, az_ref):
    outer_a = [radial_sum(solved[0][:64]), radial_sum(solved[9][:64])]
    edges = []
    for a in range(8):
        rows = solved[a + 1]
        value = radial_sum(rows[:64] + spread(rows[64:128], 1, 6))
        outer_b = radial_sum(rows[128:144])
        part_ref[a] = value
        az_ref[0, 8 * a : 8 * a + 8] = value[:8]
        az_ref[1, 8 * a : 8 * a + 8] = value[56:]
        az_ref[0, 64 + 8 * a : 72 + 8 * a] = outer_b[:8]
        az_ref[1, 64 + 8 * a : 72 + 8 * a] = outer_b[8:]
        if a in (0, 7):
            edges.append((value, outer_b))
    send_axial(
        in_ref,
        out_ref,
        [edges[0][0], outer_a[0], edges[0][1]],
        [edges[1][0], outer_a[1], edges[1][1]],
    )


def solved_side_kernel(in_ref, out_ref, az_ref, send_ref):
    before, after = got_axial(in_ref, out_ref)
    for side, b in ((0, 0), (1, 7)):
        row = 8 * b
        send_ref[side, :8] = az_ref[side, :8] + before(row, 8)
        send_ref[side, 8:16] = az_ref[side, 8:16] + before(64 + row, 8)
        send_ref[side, 16:48] = az_ref[side, 16:48]
        send_ref[side, 48:56] = az_ref[side, 48:56] + after(64 + row, 8)
        send_ref[side, 56:64] = az_ref[side, 56:64] + after(row, 8)
        send_ref[side, 64:72] = az_ref[side, 64:72] + before(128 + 8 * side, 8)
        send_ref[side, 72:120] = az_ref[side, 72:120]
        send_ref[side, 120:128] = az_ref[side, 120:128] + after(128 + 8 * side, 8)


def got_solved(part_ref, in_ref, out_ref, az_ref):
    before, after = got_axial(in_ref, out_ref)
    extra = {0: (before, 0), 1: (before, 64), 6: (after, 64), 7: (after, 0)}
    result = []
    for a in range(8):
        value = part_ref[a]
        if a in extra:
            side, start = extra[a]
            value = value + side(start, 64)
        rows = slice(8 * a, 8 * a + 8)
        faces = slice(64 + 8 * a, 72 + 8 * a)
        result.append(
            add_rows(
                value,
                {0: az_ref[1, rows], 1: az_ref[1, faces], 6: az_ref[0, faces], 7: az_ref[0, rows]},
            )
        )
    return result


def add_coarse(parts, row, near_ref):
    values = jnp.sum(near_ref[...] * row, axis=1, keepdims=True)
    own = [[values[3 * i + j : 3 * i + j + 1] for j in range(3)] for i in range(3)]
    b = lax.broadcasted_iota(jnp.int32, (64, LANES), 0) // 8
    fields = []
    for i in range(3):
        ends = [0.5 * (own[i][1] + own[i][j]) for j in (0, 2)]
        fields.append(jnp.where(b == 0, ends[0], jnp.where(b == 7, ends[1], own[i][1])))
    first, last = 0.5 * (fields[0] + fields[1]), 0.5 * (fields[1] + fields[2])
    return [
        parts[a] + (first if a == 0 else last if a == 7 else fields[1]) for a in range(8)
    ]


def apply_operator(values, diff_ref, plane_ref, grad_ref, div_ref):
    plane = plane_ref[...]
    coef = [float(WEIGHTS[a]) * plane * diff_ref[a] for a in range(8)]
    flat = product(grad_ref, jnp.concatenate(values, axis=1))
    along_a = skew_apply(DERIV, values)
    flux = jnp.concatenate(
        [
            jnp.concatenate([coef[a], coef[a]], axis=0) * flat[:, LANES * a : LANES * a + LANES]
            for a in range(8)
        ],
        axis=1,
    )
    flat = product(div_ref, flux)
    along_a = skew_apply(DERIV.T, [coef[a] * along_a[a] for a in range(8)])
    return [
        along_a[a]
        + flat[:, LANES * a : LANES * a + LANES]
        + (mass_shift * float(WEIGHTS[a])) * plane * values[a]
        for a in range(8)
    ]


def dot_parts(first, second):
    result = first[0] * second[0]
    for a in range(1, 8):
        result = result + first[a] * second[a]
    return total(result)


def norm(row):
    return jnp.sum(row * row, axis=1, keepdims=True)


def keep(ref, row, scalars):
    ref[0:1] = row
    for k, value in enumerate(scalars):
        ref[k + 1 : k + 2] = jnp.broadcast_to(value, row.shape)


def first_solve_kernel(
    g_ref, in_ref, out_ref, az_ref, kbar_ref, into_ref, outof_ref, spectrum_ref,
    center_ref, outer_a_ref, outer_b_ref, part_ref, send_in_ref, send_out_ref, send_az_ref, dot_ref,
):
    box = got_box(g_ref, in_ref, out_ref, az_ref)
    put_box(box, center_ref, outer_a_ref, outer_b_ref)
    solved, dot = solve(box, kbar_ref, into_ref, outof_ref, spectrum_ref)
    dot_ref[...] = dot
    send_solved(solved, part_ref, send_in_ref, send_out_ref, send_az_ref)


def second_solve_kernel(
    g_ref, in_ref, out_ref, az_ref, kbar_ref, into_ref, outof_ref, spectrum_ref,
    old_center_ref, old_a_ref, old_b_ref, sums_ref, state_ref,
    center_ref, outer_a_ref, outer_b_ref, q_center_ref, q_a_ref, q_b_ref,
    part_ref, send_in_ref, send_out_ref, send_az_ref, dot_ref, new_state_ref,
):
    row_q, (local_rz, curv) = got_sums(sums_ref, 2)
    row_r = state_ref[0:1]
    rz = local_rz + norm(row_r)
    alpha = rz / curv
    image = got_box(g_ref, in_ref, out_ref, az_ref)
    put_box(image, q_center_ref, q_a_ref, q_b_ref)
    box = add_box(take_box(old_center_ref, old_a_ref, old_b_ref), -alpha, image)
    put_box(box, center_ref, outer_a_ref, outer_b_ref)
    solved, dot = solve(box, kbar_ref, into_ref, outof_ref, spectrum_ref)
    dot_ref[...] = dot
    keep(new_state_ref, row_r - alpha * row_q, [rz, curv, alpha])
    new_state_ref[4:5] = row_q
    send_solved(solved, part_ref, send_in_ref, send_out_ref, send_az_ref)


def third_solve_kernel(
    g_ref, in_ref, out_ref, az_ref, kbar_ref, into_ref, outof_ref, spectrum_ref,
    old_center_ref, old_a_ref, old_b_ref, q_center_ref, q_a_ref, q_b_ref, sums_ref, state_ref,
    center_ref, part_ref, send_in_ref, send_out_ref, send_az_ref, new_state_ref, pay_ref,
):
    row_w, (local_rz, first_curv, cross) = got_sums(sums_ref, 3)
    row_r, row_q = state_ref[0:1], state_ref[4:5]
    rz_before, curv_before = state_ref[1:2, 0:1], state_ref[2:3, 0:1]
    rz = local_rz + norm(row_r)
    beta = rz / rz_before
    curv = first_curv + beta * (2.0 * cross + beta * curv_before)
    alpha = rz / curv
    image = got_box(g_ref, in_ref, out_ref, az_ref)
    image = add_box(image, beta, take_box(q_center_ref, q_a_ref, q_b_ref))
    box = add_box(take_box(old_center_ref, old_a_ref, old_b_ref), -alpha, image)
    for a in range(8):
        center_ref[a] = box[0][a]
    solved, dot = solve(box, kbar_ref, into_ref, outof_ref, spectrum_ref)
    keep(new_state_ref, row_r - alpha * (row_w + beta * row_q), [rz, beta, alpha])
    send_sums(pay_ref, jnp.zeros((1, pay_ref.shape[1]), F32), [total(dot)])
    send_solved(solved, part_ref, send_in_ref, send_out_ref, send_az_ref)


def first_apply_kernel(
    part_ref, in_ref, out_ref, az_ref, near_ref, diff_ref, plane_ref, grad_ref, div_ref,
    sums_ref, dot_ref,
    z_ref, raw_ref, g_ref, send_in_ref, send_out_ref, send_az_ref, state_ref, pay_ref,
):
    row, _ = got_sums(sums_ref, 0)
    values = add_coarse(got_solved(part_ref, in_ref, out_ref, az_ref), row, near_ref)
    raw = apply_operator(values, diff_ref, plane_ref, grad_ref, div_ref)
    for a in range(8):
        z_ref[a] = values[a]
        raw_ref[a] = raw[a]
    keep(state_ref, row, [])
    send_sums(pay_ref, coarse_share(raw, near_ref), [total(dot_ref[...]), dot_parts(values, raw)])
    send_raw(raw, g_ref, send_in_ref, send_out_ref, send_az_ref)


def second_apply_kernel(
    part_ref, in_ref, out_ref, az_ref, near_ref, diff_ref, plane_ref, grad_ref, div_ref,
    state_ref, dot_ref, old_raw_ref,
    z_ref, g_ref, send_in_ref, send_out_ref, send_az_ref, pay_ref,
):
    row = state_ref[0:1]
    values = add_coarse(got_solved(part_ref, in_ref, out_ref, az_ref), row, near_ref)
    raw = apply_operator(values, diff_ref, plane_ref, grad_ref, div_ref)
    for a in range(8):
        z_ref[a] = values[a]
    scalars = [
        total(dot_ref[...]),
        dot_parts(values, raw),
        dot_parts(values, [old_raw_ref[a] for a in range(8)]),
    ]
    send_sums(pay_ref, coarse_share(raw, near_ref), scalars)
    send_raw(raw, g_ref, send_in_ref, send_out_ref, send_az_ref)


def last_kernel(
    part_ref, in_ref, out_ref, az_ref, near_ref, sums_ref, state_ref, old_state_ref, z0_ref, z1_ref,
    pressure_ref, direction_ref,
):
    _, (local_rz,) = got_sums(sums_ref, 1)
    row = state_ref[0:1]
    rz_before, beta, alpha = (state_ref[k : k + 1, 0:1] for k in (1, 2, 3))
    alpha_before = old_state_ref[3:4, 0:1]
    ratio = (local_rz + norm(row)) / rz_before
    values = add_coarse(got_solved(part_ref, in_ref, out_ref, az_ref), row, near_ref)
    for a in range(8):
        first = z0_ref[a]
        second = z1_ref[a] + beta * first
        pressure_ref[a] = alpha_before * first + alpha * second
        direction_ref[a] = values[a] + ratio * second


def kernel_call(kernel, out_shapes, *args):
    outs = [jax.ShapeDtypeStruct(shape, F32) for shape in out_shapes]
    return pl.pallas_call(
        kernel,
        out_shape=outs,
        compiler_params=pltpu.CompilerParams(vmem_limit_bytes=VMEM_GRANT),
        interpret=INTERPRET,
    )(*args)


def axial_swap(inner_rows, outer_rows):
    count = lax.axis_size("axial")
    inner = [(i, i ^ 1) for i in range(count)]
    outer = [((2 * i + 1) % count, (2 * i + 2) % count) for i in range(count // 2)]
    outer = outer + [(b, a) for a, b in outer]
    from_outer = lax.ppermute(outer_rows, "axial", outer)
    from_inner = lax.ppermute(inner_rows, "axial", inner)
    return from_inner, from_outer


def azim_swap(sides):
    count = lax.axis_size("azim")
    if count == 2:
        return lax.ppermute(sides, "azim", [(0, 1), (1, 0)])
    after = lax.ppermute(sides[0], "azim", [((i + 1) % count, i) for i in range(count)])
    before = lax.ppermute(sides[1], "azim", [(i, (i + 1) % count) for i in range(count)])
    return jnp.stack([after, before])


def gather_sums(rows):
    return lax.all_to_all(rows, ALL, 0, 0, tiled=True)


def per_device(velocity, diffusivity, coarse_factor):
    shape = diffusivity.shape
    devices = lax.axis_size("axial") * lax.axis_size("azim")
    u = velocity.reshape(3, 8, 64, LANES)
    diff = diffusivity.reshape(8, 64, LANES)
    tables = constant_tables(LANES)
    plane, over, spectrum = tables["plane"], tables["over"], tables["spectrum"]
    grad, div, into, outof = tables["grad"], tables["div"], tables["into"], tables["outof"]
    coarse_size = coarse_factor.shape[1]
    width = -(-(coarse_size + 4) // LANES)
    count = 8 * -(-width // 8)
    row = jnp.pad(coarse_factor[0], (0, count * LANES - coarse_size)).reshape(count, LANES)

    field, sums, state = (8, 64, LANES), (devices, width * LANES), (8, width * LANES)
    box = [field, (2, 64, LANES), (8, 16, LANES)]
    raw_sends = [(128, LANES), (128, LANES), (2, 144, LANES)]
    solved_sends = [(144, LANES), (144, LANES), (2, 128, LANES)]

    conv, kbar, inner, outer, azim = kernel_call(
        conv_kernel,
        [(3,) + field, (8, LANES), (192 + count, LANES), (192 + count, LANES), (2, 192, LANES)],
        u, diff, row, plane, grad,
    )
    inner, outer = axial_swap(inner, outer)
    (azim,) = kernel_call(conv_side_kernel, [(2, 192 + 3 * count, LANES)], inner, outer, azim, row)
    azim = azim_swap(azim)
    g, send_in, send_out, send_az, near, pay = kernel_call(
        divergence_kernel,
        [field] + raw_sends + [(16, width * LANES), sums],
        conv, u, inner, outer, azim, row, plane, over, div,
    )

    def finish_raw(send_in, send_out, send_az, pay):
        inner, outer = axial_swap(send_in, send_out)
        pay = gather_sums(pay)
        (azim,) = kernel_call(raw_side_kernel, [(2, 144, LANES)], inner, outer, send_az)
        return inner, outer, azim_swap(azim), pay

    def finish_solved(send_in, send_out, send_az):
        inner, outer = axial_swap(send_in, send_out)
        (azim,) = kernel_call(solved_side_kernel, [(2, 128, LANES)], inner, outer, send_az)
        return inner, outer, azim_swap(azim)

    solver = (kbar, into, outof, spectrum)
    operator = (near, diff, plane, grad, div)
    inner, outer, azim, pay = finish_raw(send_in, send_out, send_az, pay)
    *old, part, send_in, send_out, send_az, dot = kernel_call(
        first_solve_kernel,
        box + [field] + solved_sends + [(8, LANES)],
        g, inner, outer, azim, *solver,
    )
    moved = finish_solved(send_in, send_out, send_az)
    z0, raw0, g, send_in, send_out, send_az, state0, pay = kernel_call(
        first_apply_kernel,
        [field, field, field] + raw_sends + [state, sums],
        part, *moved, *operator, pay, dot,
    )
    inner, outer, azim, pay = finish_raw(send_in, send_out, send_az, pay)
    *new, part, send_in, send_out, send_az, dot, state1 = kernel_call(
        second_solve_kernel,
        box + box + [field] + solved_sends + [(8, LANES), state],
        g, inner, outer, azim, *solver, *old, pay, state0,
    )
    moved = finish_solved(send_in, send_out, send_az)
    z1, g, send_in, send_out, send_az, pay = kernel_call(
        second_apply_kernel,
        [field, field] + raw_sends + [sums],
        part, *moved, *operator, state1, dot, raw0,
    )
    inner, outer, azim, pay = finish_raw(send_in, send_out, send_az, pay)
    residual, part, send_in, send_out, send_az, state2, pay = kernel_call(
        third_solve_kernel,
        [field, field] + solved_sends + [state, sums],
        g, inner, outer, azim, *solver, *new, pay, state1,
    )
    moved = finish_solved(send_in, send_out, send_az)
    pressure, direction = kernel_call(
        last_kernel, [field, field], part, *moved, near, gather_sums(pay), state2, state1, z0, z1
    )
    return pressure.reshape(shape), residual.reshape(shape), direction.reshape(shape)


def solution(mesh):
    split = P(None, None, None, "axial", "azim", None)
    in_specs = (P(None, None, None, None, "axial", "azim", None), split, P(ALL, None))
    return jax.shard_map(
        per_device, mesh=mesh, in_specs=in_specs, out_specs=(split, split, split), check_vma=False
    )
```

```python
import math

import jax
import jax.numpy as jnp
import numpy as np
from jax import lax
from jax.experimental import pallas as pl
from jax.experimental.pallas import tpu as pltpu
from jax.sharding import PartitionSpec as P

ALL = ("axial", "azim")
time_increment = 0.02
mass_shift = 0.05
VMEM_GRANT = 20 << 20
TAIL = 16
gll_points = [
    -1.0,
    -0.8717401485096066,
    -0.5917001814331423,
    -0.20929921790247888,
    0.20929921790247888,
    0.5917001814331423,
    0.8717401485096066,
    1.0,
]


def legendre_value(order, point):
    before = 1.0
    current = point
    for step_idx in range(1, order):
        after = ((2 * step_idx + 1) * point * current - step_idx * before) / (step_idx + 1)
        before = current
        current = after
    return current


def jacobi_eigen(matrix):
    size_n = len(matrix)
    work = [list(row) for row in matrix]
    vectors = [
        [1.0 if row_idx == col_idx else 0.0 for col_idx in range(size_n)]
        for row_idx in range(size_n)
    ]
    for sweep_idx in range(15):
        for row_idx in range(size_n):
            for col_idx in range(row_idx + 1, size_n):
                off_value = work[row_idx][col_idx]
                if off_value != 0.0:
                    theta = (work[col_idx][col_idx] - work[row_idx][row_idx]) / (2.0 * off_value)
                    root_val = math.sqrt(theta * theta + 1.0)
                    tangent = 1.0 / (theta + root_val) if theta >= 0.0 else 1.0 / (theta - root_val)
                    cosine = 1.0 / math.sqrt(tangent * tangent + 1.0)
                    sine = tangent * cosine
                    for other in range(size_n):
                        left_val = work[other][row_idx]
                        right_val = work[other][col_idx]
                        work[other][row_idx] = cosine * left_val - sine * right_val
                        work[other][col_idx] = sine * left_val + cosine * right_val
                    for other in range(size_n):
                        left_val = work[row_idx][other]
                        right_val = work[col_idx][other]
                        work[row_idx][other] = cosine * left_val - sine * right_val
                        work[col_idx][other] = sine * left_val + cosine * right_val
                    for other in range(size_n):
                        left_val = vectors[other][row_idx]
                        right_val = vectors[other][col_idx]
                        vectors[other][row_idx] = cosine * left_val - sine * right_val
                        vectors[other][col_idx] = sine * left_val + cosine * right_val
    return ([work[row_idx][row_idx] for row_idx in range(size_n)], vectors)


def gll_tables():
    degree = 7
    points = degree + 1
    legendre_at = [legendre_value(degree, node_val) for node_val in gll_points]
    weights = [2.0 / (degree * (degree + 1) * value * value) for value in legendre_at]
    derivative = [[0.0] * points for row_idx in range(points)]
    for row_idx in range(points):
        for col_idx in range(points):
            if row_idx != col_idx:
                derivative[row_idx][col_idx] = legendre_at[row_idx] / (
                    legendre_at[col_idx] * (gll_points[row_idx] - gll_points[col_idx])
                )
    derivative[0][0] = -degree * (degree + 1) / 4.0
    derivative[degree][degree] = degree * (degree + 1) / 4.0
    stiffness = [
        [
            sum(
                (
                    derivative[mid_idx][row_idx] * weights[mid_idx] * derivative[mid_idx][col_idx]
                    for mid_idx in range(points)
                )
            )
            for col_idx in range(points)
        ]
        for row_idx in range(points)
    ]
    line_len = 3 * degree + 1
    big_stiff = [[0.0] * line_len for row_idx in range(line_len)]
    big_mass = [0.0] * line_len
    for element in range(3):
        offset = element * degree
        for row_idx in range(points):
            big_mass[offset + row_idx] += weights[row_idx]
            for col_idx in range(points):
                big_stiff[offset + row_idx][offset + col_idx] += stiffness[row_idx][col_idx]
    start_node = degree - 1
    box_len = degree + 3
    scaling = [1.0 / math.sqrt(big_mass[start_node + row_idx]) for row_idx in range(box_len)]
    symmetric = [
        [
            scaling[row_idx]
            * big_stiff[start_node + row_idx][start_node + col_idx]
            * scaling[col_idx]
            for col_idx in range(box_len)
        ]
        for row_idx in range(box_len)
    ]
    eigval, eigvec = jacobi_eigen(symmetric)
    fdm_basis = [
        [scaling[row_idx] * eigvec[row_idx][col_idx] for col_idx in range(box_len)]
        for row_idx in range(box_len)
    ]
    return (weights, derivative, fdm_basis, eigval)

WEIGHTS, DERIV, BASIS, EIGVAL = (np.asarray(t, np.float64) for t in gll_tables())


def f32(table):
    return jnp.asarray(table, jnp.float32)


F32 = jnp.float32
BF16 = jnp.bfloat16
LANES = 128
INTERPRET = False


def split_terms(table, depth):
    padded = np.zeros((table.shape[0], depth))
    padded[:, : table.shape[1]] = table
    high = padded.astype(jnp.bfloat16)
    low = (padded - high.astype(np.float64)).astype(jnp.bfloat16)
    return jnp.asarray(np.concatenate([high, high, low], axis=1))


def box_tables():
    pairs = [(b + 1, c + 1) for b in range(8) for c in range(8)]
    pairs += [(b + 1, {6: 0, 1: 9}.get(c)) for b in range(8) for c in range(8)]
    pairs += [(0, c + 1) for c in range(8)] + [(9, c + 1) for c in range(8)]
    table = np.zeros((144, 112))
    for row, (b, c) in enumerate(pairs):
        if c is not None:
            table[row, :100] = np.outer(BASIS[b], BASIS[c]).reshape(100)
    sums = np.ones(112)
    sums[:100] = (EIGVAL[:, None] + EIGVAL[None, :]).reshape(100)
    return table, sums


EYE = np.eye(8)
GRAD = np.concatenate([np.kron(DERIV, EYE), np.kron(EYE, DERIV)])
BOX_ROWS, SPECTRUM = box_tables()
EVEN = [bool(abs(BASIS[0, i] - BASIS[9, i]) < abs(BASIS[0, i] + BASIS[9, i])) for i in range(10)]


def constant_tables(radial):
    plane = (WEIGHTS[:, None] * WEIGHTS[None, :]).reshape(64, 1)
    mult_r = np.ones((8, radial))
    mult_r[0, 1:] = 2.0
    mult_r[7, :-1] = 2.0
    ends = np.array([2.0, 1, 1, 1, 1, 1, 1, 2.0])
    mult = (ends[:, None, None] * mult_r[None]).reshape(64, radial)
    return dict(
        plane=f32(np.broadcast_to(plane, (64, radial))),
        over=f32(1.0 / mult),
        spectrum=f32(np.broadcast_to(SPECTRUM[:, None], (112, radial))),
        grad=split_terms(GRAD, 64),
        div=split_terms(GRAD.T, 128),
        into=split_terms(BOX_ROWS.T, 144),
        outof=split_terms(BOX_ROWS, 112),
    )


def product(table_ref, values):
    high = values.astype(BF16)
    low = (values - high.astype(F32)).astype(BF16)
    return jnp.dot(
        table_ref[...], jnp.concatenate([high, low, high], axis=0), preferred_element_type=F32
    )


def combine(coefs, terms):
    total = None
    for coef, term in zip(coefs, terms):
        scaled = float(coef) * term
        total = scaled if total is None else total + scaled
    return total


def skew_apply(matrix, parts):
    plus = [parts[b] + parts[7 - b] for b in range(4)]
    minus = [parts[b] - parts[7 - b] for b in range(4)]
    result = [None] * 8
    for a in range(4):
        even = combine([0.5 * (matrix[a, b] + matrix[a, 7 - b]) for b in range(4)], plus)
        odd = combine([0.5 * (matrix[a, b] - matrix[a, 7 - b]) for b in range(4)], minus)
        result[a] = even + odd
        result[7 - a] = odd - even
    return result


def to_spectral(parts):
    plus = [parts[a] + parts[9 - a] for a in range(5)]
    minus = [parts[a] - parts[9 - a] for a in range(5)]
    return [combine(BASIS[:5, i], plus if EVEN[i] else minus) for i in range(10)]


def from_spectral(parts):
    evens = [i for i in range(10) if EVEN[i]]
    odds = [i for i in range(10) if not EVEN[i]]
    result = [None] * 10
    for a in range(5):
        even = combine(BASIS[a, evens], [parts[i] for i in evens])
        odd = combine(BASIS[a, odds], [parts[i] for i in odds])
        result[a] = even + odd
        result[9 - a] = even - odd
    return result


def masks(rows):
    layer = lax.broadcasted_iota(jnp.int32, (rows, LANES), 0) % 8
    elem = lax.broadcasted_iota(jnp.int32, (rows, LANES), 1)
    return layer, elem > 0, elem < LANES - 1


def spread(values, first, last):
    layer, has_before, has_after = masks(values.shape[0])
    before = pltpu.roll(values, 1, axis=1)
    after = pltpu.roll(values, LANES - 1, axis=1)
    return jnp.where(
        (layer == first) & has_before,
        before,
        jnp.where((layer == last) & has_after, after, 0.0),
    )


def radial_sum(values):
    rows = values.shape[0]
    layer, _, _ = masks(rows)
    cubes = values.reshape(rows // 8, 8, LANES)
    up = pltpu.roll(cubes, 1, axis=1).reshape(rows, LANES)
    down = pltpu.roll(cubes, 7, axis=1).reshape(rows, LANES)
    return values + spread(jnp.where(layer == 0, up, down), 0, 7)


def total(values):
    return jnp.sum(values, axis=(0, 1), keepdims=True)


def add_rows(block, extra):
    pieces = []
    for b in range(8):
        piece = block[8 * b : 8 * b + 8]
        pieces.append(piece + extra[b] if b in extra else piece)
    return jnp.concatenate(pieces, axis=0)


def is_even():
    return lax.axis_index("axial") % 2 == 0


def send_axial(inner_ref, outer_ref, low, high):
    even = is_even()
    row = 0
    for low_piece, high_piece in zip(low, high):
        size = low_piece.shape[0]
        inner_ref[row : row + size] = jnp.where(even, high_piece, low_piece)
        outer_ref[row : row + size] = jnp.where(even, low_piece, high_piece)
        row += size


def got_axial(inner_ref, outer_ref):
    even = is_even()

    def before(start, size):
        return jnp.where(even, outer_ref[start : start + size], inner_ref[start : start + size])

    def after(start, size):
        return jnp.where(even, inner_ref[start : start + size], outer_ref[start : start + size])

    return before, after


def conv_kernel(
    u_hbm, row_hbm, plane_hbm, grad_hbm,
    conv_ref, row_ref, in_ref, out_ref, early_ref, late_ref,
    u_ref, small_ref, plane_ref, grad_ref, sems,
):
    copies = [
        pltpu.make_async_copy(source, target, sems.at[k])
        for k, (source, target) in enumerate(
            ((u_hbm, u_ref), (plane_hbm, plane_ref), (grad_hbm, grad_ref), (row_hbm, small_ref))
        )
    ]
    for copy in copies:
        copy.start()
    row_ref[...] = jnp.zeros(row_ref.shape, F32)
    for copy in copies:
        copy.wait()
    size = small_ref.shape[1]
    for k in range(-(-size // LANES)):
        stop = min(LANES, size - LANES * k)
        row_ref[k : k + 1, :stop] = small_ref[:, LANES * k : LANES * k + stop]
    plane = plane_ref[...]
    fields = [[u_ref[d, a] for a in range(8)] for d in range(3)]
    low, high = [], []
    for comp in range(3):
        parts = fields[comp]
        flat = product(grad_ref, jnp.concatenate(parts, axis=1))
        along_a = skew_apply(DERIV, parts)
        for a in range(8):
            cols = slice(LANES * a, LANES * a + LANES)
            value = (
                fields[0][a] * along_a[a]
                + fields[1][a] * flat[:64, cols]
                + fields[2][a] * flat[64:, cols]
            )
            value = radial_sum(float(WEIGHTS[a]) * plane * value)
            conv_ref[comp, a] = value
            for side, rows in enumerate((value[:8], value[56:])):
                if a in (0, 7):
                    start = 16 * comp + (8 if a else 0)
                    late_ref[side, start : start + 8] = rows
                else:
                    start = 48 * comp + 8 * (a - 1)
                    early_ref[side, start : start + 8] = rows
            if a == 0:
                low.append(value)
            if a == 7:
                high.append(value)
    row = row_ref[...]
    send_axial(in_ref, out_ref, low + [row], high + [row])


def mean_kernel(diff_ref, kbar_ref):
    mean = diff_ref[0]
    for a in range(1, 8):
        mean = mean + diff_ref[a]
    mean = jnp.sum(mean, axis=0, keepdims=True) * (1.0 / 512.0)
    kbar_ref[...] = jnp.broadcast_to(mean, (8, LANES))


def conv_side_kernel(in_ref, out_ref, late_ref, row_ref, send_ref):
    before, after = got_axial(in_ref, out_ref)
    count = row_ref.shape[0]
    for side, b in ((0, 0), (1, 7)):
        for comp in range(3):
            first = slice(16 * comp, 16 * comp + 8)
            last = slice(16 * comp + 8, 16 * comp + 16)
            row = 64 * comp + 8 * b
            send_ref[side, first] = late_ref[side, first] + before(row, 8)
            send_ref[side, last] = late_ref[side, last] + after(row, 8)
        for place, rows in enumerate((before(192, count), row_ref[...], after(192, count))):
            start = 48 + place * count
            send_ref[side, start : start + count] = rows


def coarse_share(raw, near_ref):
    middle = raw[1]
    for a in range(2, 7):
        middle = middle + raw[a]
    per_axial = (0.5 * raw[0], middle + 0.5 * (raw[0] + raw[7]), 0.5 * raw[7])
    rows = []
    for part in per_axial:
        inner = part[8:16]
        for b in range(2, 7):
            inner = inner + part[8 * b : 8 * b + 8]
        ends = (part[:8], part[56:])
        for piece in (0.5 * ends[0], inner + 0.5 * (ends[0] + ends[1]), 0.5 * ends[1]):
            rows.append(jnp.sum(piece, axis=0, keepdims=True))
    rows = jnp.concatenate(rows + [jnp.zeros((7, LANES), F32)], axis=0)
    shares = jnp.sum(rows, axis=1, keepdims=True)
    return jnp.sum(shares * near_ref[...], axis=0, keepdims=True)


def send_sums(pay_ref, row, scalars):
    width = pay_ref.shape[1]
    place = lax.broadcasted_iota(jnp.int32, (1, width), 1)
    for k, value in enumerate(scalars):
        row = jnp.where(place == width - 1 - k, value, row)
    pay_ref[...] = jnp.broadcast_to(row, pay_ref.shape)


def got_sums(ref, scalars):
    row = jnp.sum(ref[...], axis=0, keepdims=True)
    width = row.shape[1]
    place = lax.broadcasted_iota(jnp.int32, (1, width), 1)
    values = [
        jnp.sum(jnp.where(place == width - 1 - k, row, 0.0), axis=1, keepdims=True)
        for k in range(scalars)
    ]
    return jnp.where(place >= width - TAIL, 0.0, row), values


def send_raw(raw, g_ref, in_ref, out_ref, early_ref, late_ref):
    parts = [radial_sum(raw[a]) for a in range(8)]
    for a in range(8):
        g_ref[a] = parts[a]
    send_axial(in_ref, out_ref, [parts[0], parts[1]], [parts[7], parts[6]])
    for side, (edge, inner) in enumerate(((0, 1), (7, 6))):
        edges = [part[8 * edge : 8 * edge + 8] for part in parts]
        inners = [part[8 * inner : 8 * inner + 8] for part in parts]
        for a in range(1, 7):
            early_ref[side, 8 * a - 8 : 8 * a] = edges[a]
            early_ref[side, 40 + 8 * a : 48 + 8 * a] = inners[a]
        late_ref[side, :8] = edges[0]
        late_ref[side, 8:16] = edges[7]
        late_ref[side, 16:24] = inners[0]
        late_ref[side, 24:32] = inners[7]


def raw_side_kernel(in_ref, out_ref, late_ref, send_ref):
    before, after = got_axial(in_ref, out_ref)
    for side, (edge, inner) in enumerate(((0, 1), (7, 6))):
        send_ref[side, :8] = before(64 + 8 * edge, 8)
        send_ref[side, 8:16] = late_ref[side, :8] + before(8 * edge, 8)
        send_ref[side, 16:24] = late_ref[side, 8:16] + after(8 * edge, 8)
        send_ref[side, 24:32] = after(64 + 8 * edge, 8)
        send_ref[side, 32:40] = late_ref[side, 16:24] + before(8 * inner, 8)
        send_ref[side, 40:48] = late_ref[side, 24:32] + after(8 * inner, 8)


def divergence_kernel(
    conv_ref, u_ref, in_ref, out_ref, early_ref, late_ref, row_ref, plane_ref, over_ref, div_ref,
    g_ref, send_in_ref, send_out_ref, send_early_ref, send_late_ref, near_ref, pay_ref,
):
    before, after = got_axial(in_ref, out_ref)
    plane, over = plane_ref[...], over_ref[...]

    def side_rows(side, comp, a):
        if a in (0, 7):
            start = 16 * comp + (8 if a else 0)
            return late_ref[side, start : start + 8]
        start = 48 * comp + 8 * (a - 1)
        return early_ref[side, start : start + 8]

    moved = []
    for comp in range(3):
        parts = []
        for a in range(8):
            value = conv_ref[comp, a]
            if a == 0:
                value = value + before(64 * comp, 64)
            if a == 7:
                value = value + after(64 * comp, 64)
            value = add_rows(value, {0: side_rows(1, comp, a), 7: side_rows(0, comp, a)})
            scale = time_increment * (0.5 if a in (0, 7) else 1.0)
            parts.append(float(WEIGHTS[a]) * plane * u_ref[comp, a] - scale * over * value)
        moved.append(parts)
    flat = product(
        div_ref,
        jnp.concatenate([jnp.concatenate(moved[1], axis=1), jnp.concatenate(moved[2], axis=1)], axis=0),
    )
    along_a = skew_apply(DERIV.T, moved[0])
    raw = [along_a[a] + flat[:, LANES * a : LANES * a + LANES] for a in range(8)]
    send_raw(raw, g_ref, send_in_ref, send_out_ref, send_early_ref, send_late_ref)
    count = row_ref.shape[0]
    width = near_ref.shape[1] // LANES
    near_ref[...] = jnp.zeros(near_ref.shape, F32)
    for i in range(3):
        start = 48 + i * count
        middle = (before(192, count), row_ref[...], after(192, count))[i]
        sides = (late_ref[1, start : start + count], middle, late_ref[0, start : start + count])
        for j, rows in enumerate(sides):
            for k in range(width):
                near_ref[3 * i + j : 3 * i + j + 1, LANES * k : LANES * k + LANES] = rows[k : k + 1]
    send_sums(pay_ref, coarse_share(raw, near_ref), [])


def got_planes(g_ref, in_ref, out_ref, early_ref, late_ref):
    before, after = got_axial(in_ref, out_ref)

    def edge_rows(side, e):
        if e in (0, 1, 8, 9):
            start = 8 * (0, 1, 8, 9).index(e)
            return late_ref[side, start : start + 8]
        return early_ref[side, 8 * e - 16 : 8 * e - 8]

    def inner_rows(side, a):
        if a in (0, 7):
            start = 40 if a else 32
            return late_ref[side, start : start + 8]
        return early_ref[side, 40 + 8 * a : 48 + 8 * a]

    zero = jnp.zeros((80, LANES), F32)
    planes = []
    for e in range(10):
        if e == 0:
            value = before(64, 64)
        elif e == 9:
            value = after(64, 64)
        else:
            value = g_ref[e - 1]
        if e == 1:
            value = value + before(0, 64)
        if e == 8:
            value = value + after(0, 64)
        value = add_rows(value, {0: edge_rows(1, e), 7: edge_rows(0, e)})
        if e in (0, 9):
            rows = [value, zero]
        else:
            rows = [value, spread(value, 6, 1), inner_rows(1, e - 1), inner_rows(0, e - 1)]
        planes.append(jnp.concatenate(rows, axis=0))
    return planes


def solve_kernel(
    g_ref, in_ref, out_ref, early_ref, late_ref, kbar_ref, into_ref, outof_ref, spectrum_ref,
    planes_ref, solved_ref, part_ref, send_in_ref, send_out_ref, send_early_ref, send_late_ref,
):
    planes = got_planes(g_ref, in_ref, out_ref, early_ref, late_ref)
    for e in range(10):
        planes_ref[e] = planes[e]
    flat = product(into_ref, jnp.concatenate(planes, axis=1))
    parts = to_spectral([flat[:, LANES * e : LANES * e + LANES] for e in range(10)])
    kbar = kbar_ref[0:1, :]
    plane_spectrum = kbar * spectrum_ref[...] + mass_shift
    parts = [parts[i] / (plane_spectrum + float(EIGVAL[i]) * kbar) for i in range(10)]
    parts = from_spectral(parts)
    flat = product(outof_ref, jnp.concatenate(parts, axis=1))
    solved = [flat[:, LANES * e : LANES * e + LANES] for e in range(10)]
    for e in range(10):
        solved_ref[e] = solved[e]
    outer_a = [radial_sum(solved[0][:64]), radial_sum(solved[9][:64])]
    edges = []
    for a in range(8):
        rows = solved[a + 1]
        value = radial_sum(rows[:64] + spread(rows[64:128], 1, 6))
        outer_b = radial_sum(rows[128:144])
        part_ref[a] = value
        for side in range(2):
            edge = value[56 * side : 56 * side + 8]
            face = outer_b[8 * side : 8 * side + 8]
            if a in (0, 1, 6, 7):
                start = 8 * (0, 1, 6, 7).index(a)
                send_late_ref[side, start : start + 8] = edge
            else:
                send_early_ref[side, 8 * a - 16 : 8 * a - 8] = edge
            if a in (0, 7):
                start = 40 if a else 32
                send_late_ref[side, start : start + 8] = face
            else:
                send_early_ref[side, 24 + 8 * a : 32 + 8 * a] = face
        if a in (0, 7):
            edges.append((value, outer_b))
    send_axial(
        send_in_ref,
        send_out_ref,
        [edges[0][0], outer_a[0], edges[0][1]],
        [edges[1][0], outer_a[1], edges[1][1]],
    )


def solved_side_kernel(in_ref, out_ref, late_ref, send_ref):
    before, after = got_axial(in_ref, out_ref)
    for side, b in ((0, 0), (1, 7)):
        row = 8 * b
        send_ref[side, :8] = late_ref[side, :8] + before(row, 8)
        send_ref[side, 8:16] = late_ref[side, 8:16] + before(64 + row, 8)
        send_ref[side, 16:24] = late_ref[side, 16:24] + after(64 + row, 8)
        send_ref[side, 24:32] = late_ref[side, 24:32] + after(row, 8)
        send_ref[side, 32:40] = late_ref[side, 32:40] + before(128 + 8 * side, 8)
        send_ref[side, 40:48] = late_ref[side, 40:48] + after(128 + 8 * side, 8)


def got_solved(part_ref, in_ref, out_ref, early_ref, late_ref):
    before, after = got_axial(in_ref, out_ref)
    extra = {0: (before, 0), 1: (before, 64), 6: (after, 64), 7: (after, 0)}

    def edge_rows(side, a):
        if a in extra:
            start = 8 * (0, 1, 6, 7).index(a)
            return late_ref[side, start : start + 8]
        return early_ref[side, 8 * a - 16 : 8 * a - 8]

    def face_rows(side, a):
        if a in (0, 7):
            start = 40 if a else 32
            return late_ref[side, start : start + 8]
        return early_ref[side, 24 + 8 * a : 32 + 8 * a]

    result = []
    for a in range(8):
        value = part_ref[a]
        if a in extra:
            side, start = extra[a]
            value = value + side(start, 64)
        result.append(
            add_rows(
                value,
                {0: edge_rows(1, a), 1: face_rows(1, a), 6: face_rows(0, a), 7: edge_rows(0, a)},
            )
        )
    return result


def add_coarse(parts, row, near_ref):
    values = jnp.sum(near_ref[...] * row, axis=1, keepdims=True)
    own = [[values[3 * i + j : 3 * i + j + 1] for j in range(3)] for i in range(3)]
    b = lax.broadcasted_iota(jnp.int32, (64, LANES), 0) // 8
    fields = []
    for i in range(3):
        ends = [0.5 * (own[i][1] + own[i][j]) for j in (0, 2)]
        fields.append(jnp.where(b == 0, ends[0], jnp.where(b == 7, ends[1], own[i][1])))
    first, last = 0.5 * (fields[0] + fields[1]), 0.5 * (fields[1] + fields[2])
    return [
        parts[a] + (first if a == 0 else last if a == 7 else fields[1]) for a in range(8)
    ]


def apply_operator(values, diff_ref, plane_ref, grad_ref, div_ref):
    plane = plane_ref[...]
    coef = [float(WEIGHTS[a]) * plane * diff_ref[a] for a in range(8)]
    flat = product(grad_ref, jnp.concatenate(values, axis=1))
    along_a = skew_apply(DERIV, values)
    flux = jnp.concatenate(
        [
            jnp.concatenate([coef[a], coef[a]], axis=0) * flat[:, LANES * a : LANES * a + LANES]
            for a in range(8)
        ],
        axis=1,
    )
    flat = product(div_ref, flux)
    along_a = skew_apply(DERIV.T, [coef[a] * along_a[a] for a in range(8)])
    return [
        along_a[a]
        + flat[:, LANES * a : LANES * a + LANES]
        + (mass_shift * float(WEIGHTS[a])) * plane * values[a]
        for a in range(8)
    ]


def dot_parts(first, second):
    result = first[0] * second[0]
    for a in range(1, 8):
        result = result + first[a] * second[a]
    return total(result)


def norm(row):
    return jnp.sum(row * row, axis=1, keepdims=True)


def dot_planes(first, second):
    result = None
    for e in range(10):
        stop = 64 if e in (0, 9) else 144
        term = first[e][:stop] * second[e][:stop]
        term = jnp.sum(term.reshape(stop // 8, 8, LANES), axis=0)
        result = term if result is None else result + term
    return total(result)


def first_apply_kernel(
    part_ref, in_ref, out_ref, early_ref, late_ref, near_ref, diff_ref, plane_ref, grad_ref, div_ref,
    sums_ref, planes_ref, solved_ref,
    z_ref, raw_ref, g_ref, send_in_ref, send_out_ref, send_early_ref, send_late_ref, row_ref, pay_ref,
):
    row, _ = got_sums(sums_ref, 0)
    values = got_solved(part_ref, in_ref, out_ref, early_ref, late_ref)
    values = add_coarse(values, row, near_ref)
    raw = apply_operator(values, diff_ref, plane_ref, grad_ref, div_ref)
    send_raw(raw, g_ref, send_in_ref, send_out_ref, send_early_ref, send_late_ref)
    for a in range(8):
        z_ref[a] = values[a]
        raw_ref[a] = raw[a]
    row_ref[0:1] = row
    scalars = [dot_planes(planes_ref, solved_ref), dot_parts(values, raw)]
    send_sums(pay_ref, coarse_share(raw, near_ref), scalars)


def first_step(sums_ref, row_ref):
    row_q, (local_rz, curv) = got_sums(sums_ref, 2)
    row_r = row_ref[0:1]
    rz = local_rz + norm(row_r)
    return row_r, row_q, rz, curv, rz / curv


def second_apply_kernel(
    part_ref, in_ref, out_ref, early_ref, late_ref, near_ref, diff_ref, plane_ref, grad_ref, div_ref,
    sums_ref, row_ref, z0_ref,
    y_ref, z_ref, raw_ref, g_ref, send_in_ref, send_out_ref, send_early_ref, send_late_ref,
):
    _, row_q, _, _, alpha = first_step(sums_ref, row_ref)
    change = got_solved(part_ref, in_ref, out_ref, early_ref, late_ref)
    change = add_coarse(change, row_q, near_ref)
    values = [z0_ref[a] - alpha * change[a] for a in range(8)]
    raw = apply_operator(values, diff_ref, plane_ref, grad_ref, div_ref)
    send_raw(raw, g_ref, send_in_ref, send_out_ref, send_early_ref, send_late_ref)
    for a in range(8):
        y_ref[a] = change[a]
        z_ref[a] = values[a]
        raw_ref[a] = raw[a]


def first_dots_kernel(
    sums_ref, row_ref, near_ref, planes_r_ref, planes_q_ref, solved_r_ref, solved_q_ref,
    z_ref, raw_ref, old_raw_ref,
    planes_ref, solved_ref, pay_ref,
):
    alpha = first_step(sums_ref, row_ref)[4]
    planes, solved = [], []
    for e in range(10):
        planes.append(planes_r_ref[e] - alpha * planes_q_ref[e])
        solved.append(solved_r_ref[e] - alpha * solved_q_ref[e])
        planes_ref[e] = planes[e]
        solved_ref[e] = solved[e]
    values = [z_ref[a] for a in range(8)]
    raw = [raw_ref[a] for a in range(8)]
    scalars = [
        dot_planes(planes, solved),
        dot_planes(planes, solved_q_ref),
        dot_planes(planes_q_ref, solved),
        dot_planes(planes_q_ref, solved_q_ref),
        dot_parts(values, raw),
        dot_parts(values, [old_raw_ref[a] for a in range(8)]),
    ]
    send_sums(pay_ref, coarse_share(raw, near_ref), scalars)


def second_dots_kernel(
    pay_in_ref, planes_r_ref, planes_q_ref, planes_w_ref, solved_r_ref, solved_q_ref, solved_w_ref,
    pay_ref,
):
    scalars = [
        dot_planes(planes_r_ref, solved_w_ref),
        dot_planes(planes_q_ref, solved_w_ref),
        dot_planes(planes_w_ref, solved_r_ref),
        dot_planes(planes_w_ref, solved_q_ref),
        dot_planes(planes_w_ref, solved_w_ref),
    ]
    row = pay_in_ref[0:1]
    width = row.shape[1]
    place = lax.broadcasted_iota(jnp.int32, (1, width), 1)
    for k, value in enumerate(scalars):
        row = jnp.where(place == width - 7 - k, value, row)
    pay_ref[...] = jnp.broadcast_to(row, pay_ref.shape)


def last_kernel(
    part_ref, in_ref, out_ref, early_ref, late_ref, near_ref, sums_ref, old_sums_ref, row_ref,
    y_ref, z0_ref, z1_ref, planes_r_ref, planes_q_ref, planes_w_ref,
    pressure_ref, residual_ref, direction_ref,
):
    row_r, row_q, rz0, curv0, alpha0 = first_step(old_sums_ref, row_ref)
    row_w, scalars = got_sums(sums_ref, 11)
    rr, rq, qr, qq, first_curv, cross, rw, qw, wr, wq, ww = scalars
    row_r = row_r - alpha0 * row_q
    rz1 = rr + norm(row_r)
    beta0 = rz1 / rz0
    curv1 = first_curv + beta0 * (2.0 * cross + beta0 * curv0)
    alpha1 = rz1 / curv1
    row = row_w + beta0 * row_q
    row_r = row_r - alpha1 * row
    step = -alpha1 * beta0
    rz2 = (
        rr
        - alpha1 * (rw + wr)
        + step * (rq + qr)
        + alpha1 * alpha1 * ww
        - alpha1 * step * (wq + qw)
        + step * step * qq
        + norm(row_r)
    )
    beta1 = rz2 / rz1
    change = got_solved(part_ref, in_ref, out_ref, early_ref, late_ref)
    change = add_coarse(change, row_w, near_ref)
    for a in range(8):
        first = z0_ref[a]
        second = z1_ref[a] + beta0 * first
        image = planes_w_ref[a + 1, :64] + beta0 * planes_q_ref[a + 1, :64]
        residual_ref[a] = planes_r_ref[a + 1, :64] - alpha1 * image
        pressure_ref[a] = alpha0 * first + alpha1 * second
        direction_ref[a] = (
            z1_ref[a] - alpha1 * (change[a] + beta0 * y_ref[a]) + beta1 * second
        )


def kernel_call(kernel, out_shapes, *args, **options):
    outs = [jax.ShapeDtypeStruct(shape, F32) for shape in out_shapes]
    return pl.pallas_call(
        kernel,
        out_shape=outs,
        compiler_params=pltpu.CompilerParams(vmem_limit_bytes=VMEM_GRANT),
        interpret=INTERPRET,
        **options,
    )(*args)


def axial_swap(inner_rows, outer_rows):
    count = lax.axis_size("axial")
    inner = [(i, i ^ 1) for i in range(count)]
    outer = [((2 * i + 1) % count, (2 * i + 2) % count) for i in range(count // 2)]
    outer = outer + [(b, a) for a, b in outer]
    from_outer = lax.ppermute(outer_rows, "axial", outer)
    from_inner = lax.ppermute(inner_rows, "axial", inner)
    return from_inner, from_outer


def azim_swap(sides):
    count = lax.axis_size("azim")
    if count == 2:
        return lax.ppermute(sides, "azim", [(0, 1), (1, 0)])
    after = lax.ppermute(sides[0], "azim", [((i + 1) % count, i) for i in range(count)])
    before = lax.ppermute(sides[1], "azim", [(i, (i + 1) % count) for i in range(count)])
    return jnp.stack([after, before])


def gather_sums(rows):
    return lax.all_to_all(rows, ALL, 0, 0, tiled=True)


def per_device(velocity, diffusivity, coarse_factor):
    shape = diffusivity.shape
    devices = lax.axis_size("axial") * lax.axis_size("azim")
    u = velocity.reshape(3, 8, 64, LANES)
    diff = diffusivity.reshape(8, 64, LANES)
    tables = constant_tables(LANES)
    plane, over, spectrum = tables["plane"], tables["over"], tables["spectrum"]
    grad, div, into, outof = tables["grad"], tables["div"], tables["into"], tables["outof"]
    coarse_size = coarse_factor.shape[1]
    width = -(-(coarse_size + TAIL) // LANES)
    count = 8 * -(-width // 8)

    field, sums, row_shape = (8, 64, LANES), (devices, width * LANES), (8, width * LANES)
    boxes = [(10, 144, LANES), (10, 144, LANES)]
    raw_sends = [(128, LANES), (128, LANES), (2, 96, LANES), (2, 32, LANES)]
    solved_sends = [(144, LANES), (144, LANES), (2, 80, LANES), (2, 48, LANES)]

    far = pl.BlockSpec(memory_space=pltpu.HBM)
    conv, row, *sends = kernel_call(
        conv_kernel,
        [(3,) + field, (count, LANES), (192 + count, LANES), (192 + count, LANES)]
        + [(2, 144, LANES), (2, 48, LANES)],
        u, coarse_factor, plane, grad,
        in_specs=[far] * 4,
        scratch_shapes=[
            pltpu.VMEM((3,) + field, F32),
            pltpu.VMEM((1, coarse_size), F32),
            pltpu.VMEM(plane.shape, F32),
            pltpu.VMEM(grad.shape, BF16),
            pltpu.SemaphoreType.DMA((4,)),
        ],
    )
    (kbar,) = kernel_call(mean_kernel, [(8, LANES)], diff)

    def exchange(side_kernel, late_rows, send_in, send_out, send_early, send_late, *more):
        inner, outer = axial_swap(send_in, send_out)
        early = azim_swap(send_early)
        (late,) = kernel_call(side_kernel, [(2, late_rows, LANES)], inner, outer, send_late, *more)
        return inner, outer, early, azim_swap(late)

    moved = exchange(conv_side_kernel, 48 + 3 * count, *sends, row)
    g, *sends, near, pay = kernel_call(
        divergence_kernel,
        [field] + raw_sends + [(16, width * LANES), sums],
        conv, u, *moved, row, plane, over, div,
    )
    solver = (kbar, into, outof, spectrum)
    operator = (near, diff, plane, grad, div)
    solve_shapes = boxes + [field] + solved_sends

    moved = exchange(raw_side_kernel, 48, *sends)
    pay = gather_sums(pay)
    planes_r, solved_r, part, *sends = kernel_call(solve_kernel, solve_shapes, g, *moved, *solver)
    moved = exchange(solved_side_kernel, 48, *sends)
    z0, raw0, g, *sends, row_r, pay = kernel_call(
        first_apply_kernel,
        [field, field, field] + raw_sends + [row_shape, sums],
        part, *moved, *operator, pay, planes_r, solved_r,
    )
    moved = exchange(raw_side_kernel, 48, *sends)
    first_sums = gather_sums(pay)
    planes_q, solved_q, part, *sends = kernel_call(solve_kernel, solve_shapes, g, *moved, *solver)
    moved = exchange(solved_side_kernel, 48, *sends)
    y, z1, raw1, g, *sends = kernel_call(
        second_apply_kernel,
        [field, field, field, field] + raw_sends,
        part, *moved, *operator, first_sums, row_r, z0,
    )
    planes_r, solved_r, pay = kernel_call(
        first_dots_kernel,
        boxes + [sums],
        first_sums, row_r, near, planes_r, planes_q, solved_r, solved_q, z1, raw1, raw0,
    )
    moved = exchange(raw_side_kernel, 48, *sends)
    planes_w, solved_w, part, *sends = kernel_call(solve_kernel, solve_shapes, g, *moved, *solver)
    (pay,) = kernel_call(
        second_dots_kernel, [sums], pay, planes_r, planes_q, planes_w, solved_r, solved_q, solved_w
    )
    moved = exchange(solved_side_kernel, 48, *sends)
    pressure, residual, direction = kernel_call(
        last_kernel,
        [field, field, field],
        part, *moved, near, gather_sums(pay), first_sums, row_r,
        y, z0, z1, planes_r, planes_q, planes_w,
    )
    return pressure.reshape(shape), residual.reshape(shape), direction.reshape(shape)


def solution(mesh):
    split = P(None, None, None, "axial", "azim", None)
    in_specs = (P(None, None, None, None, "axial", "azim", None), split, P(ALL, None))
    return jax.shard_map(
        per_device, mesh=mesh, in_specs=in_specs, out_specs=(split, split, split), check_vma=False
    )
```

```python
import math

import jax
import jax.numpy as jnp
import numpy as np
from jax import lax
from jax.experimental import pallas as pl
from jax.experimental.pallas import tpu as pltpu
from jax.sharding import PartitionSpec as P

ALL = ("axial", "azim")
time_increment = 0.02
mass_shift = 0.05
VMEM_GRANT = 20 << 20
TAIL = 16
gll_points = [
    -1.0,
    -0.8717401485096066,
    -0.5917001814331423,
    -0.20929921790247888,
    0.20929921790247888,
    0.5917001814331423,
    0.8717401485096066,
    1.0,
]


def legendre_value(order, point):
    before = 1.0
    current = point
    for step_idx in range(1, order):
        after = ((2 * step_idx + 1) * point * current - step_idx * before) / (step_idx + 1)
        before = current
        current = after
    return current


def jacobi_eigen(matrix):
    size_n = len(matrix)
    work = [list(row) for row in matrix]
    vectors = [
        [1.0 if row_idx == col_idx else 0.0 for col_idx in range(size_n)]
        for row_idx in range(size_n)
    ]
    for sweep_idx in range(15):
        for row_idx in range(size_n):
            for col_idx in range(row_idx + 1, size_n):
                off_value = work[row_idx][col_idx]
                if off_value != 0.0:
                    theta = (work[col_idx][col_idx] - work[row_idx][row_idx]) / (2.0 * off_value)
                    root_val = math.sqrt(theta * theta + 1.0)
                    tangent = 1.0 / (theta + root_val) if theta >= 0.0 else 1.0 / (theta - root_val)
                    cosine = 1.0 / math.sqrt(tangent * tangent + 1.0)
                    sine = tangent * cosine
                    for other in range(size_n):
                        left_val = work[other][row_idx]
                        right_val = work[other][col_idx]
                        work[other][row_idx] = cosine * left_val - sine * right_val
                        work[other][col_idx] = sine * left_val + cosine * right_val
                    for other in range(size_n):
                        left_val = work[row_idx][other]
                        right_val = work[col_idx][other]
                        work[row_idx][other] = cosine * left_val - sine * right_val
                        work[col_idx][other] = sine * left_val + cosine * right_val
                    for other in range(size_n):
                        left_val = vectors[other][row_idx]
                        right_val = vectors[other][col_idx]
                        vectors[other][row_idx] = cosine * left_val - sine * right_val
                        vectors[other][col_idx] = sine * left_val + cosine * right_val
    return ([work[row_idx][row_idx] for row_idx in range(size_n)], vectors)


def gll_tables():
    degree = 7
    points = degree + 1
    legendre_at = [legendre_value(degree, node_val) for node_val in gll_points]
    weights = [2.0 / (degree * (degree + 1) * value * value) for value in legendre_at]
    derivative = [[0.0] * points for row_idx in range(points)]
    for row_idx in range(points):
        for col_idx in range(points):
            if row_idx != col_idx:
                derivative[row_idx][col_idx] = legendre_at[row_idx] / (
                    legendre_at[col_idx] * (gll_points[row_idx] - gll_points[col_idx])
                )
    derivative[0][0] = -degree * (degree + 1) / 4.0
    derivative[degree][degree] = degree * (degree + 1) / 4.0
    stiffness = [
        [
            sum(
                (
                    derivative[mid_idx][row_idx] * weights[mid_idx] * derivative[mid_idx][col_idx]
                    for mid_idx in range(points)
                )
            )
            for col_idx in range(points)
        ]
        for row_idx in range(points)
    ]
    line_len = 3 * degree + 1
    big_stiff = [[0.0] * line_len for row_idx in range(line_len)]
    big_mass = [0.0] * line_len
    for element in range(3):
        offset = element * degree
        for row_idx in range(points):
            big_mass[offset + row_idx] += weights[row_idx]
            for col_idx in range(points):
                big_stiff[offset + row_idx][offset + col_idx] += stiffness[row_idx][col_idx]
    start_node = degree - 1
    box_len = degree + 3
    scaling = [1.0 / math.sqrt(big_mass[start_node + row_idx]) for row_idx in range(box_len)]
    symmetric = [
        [
            scaling[row_idx]
            * big_stiff[start_node + row_idx][start_node + col_idx]
            * scaling[col_idx]
            for col_idx in range(box_len)
        ]
        for row_idx in range(box_len)
    ]
    eigval, eigvec = jacobi_eigen(symmetric)
    fdm_basis = [
        [scaling[row_idx] * eigvec[row_idx][col_idx] for col_idx in range(box_len)]
        for row_idx in range(box_len)
    ]
    return (weights, derivative, fdm_basis, eigval)

WEIGHTS, DERIV, BASIS, EIGVAL = (np.asarray(t, np.float64) for t in gll_tables())


def f32(table):
    return jnp.asarray(table, jnp.float32)


F32 = jnp.float32
BF16 = jnp.bfloat16
LANES = 128
INTERPRET = False


def split_terms(table, depth):
    padded = np.zeros((table.shape[0], depth))
    padded[:, : table.shape[1]] = table
    high = padded.astype(jnp.bfloat16)
    low = (padded - high.astype(np.float64)).astype(jnp.bfloat16)
    return jnp.asarray(np.concatenate([high, high, low], axis=1))


def box_tables():
    pairs = [(b + 1, c + 1) for b in range(8) for c in range(8)]
    pairs += [(b + 1, {6: 0, 1: 9}.get(c)) for b in range(8) for c in range(8)]
    pairs += [(0, c + 1) for c in range(8)] + [(9, c + 1) for c in range(8)]
    table = np.zeros((144, 112))
    for row, (b, c) in enumerate(pairs):
        if c is not None:
            table[row, :100] = np.outer(BASIS[b], BASIS[c]).reshape(100)
    sums = np.ones(112)
    sums[:100] = (EIGVAL[:, None] + EIGVAL[None, :]).reshape(100)
    return table, sums


EYE = np.eye(8)
GRAD = np.concatenate([np.kron(DERIV, EYE), np.kron(EYE, DERIV)])
BOX_ROWS, SPECTRUM = box_tables()
EVEN = [bool(abs(BASIS[0, i] - BASIS[9, i]) < abs(BASIS[0, i] + BASIS[9, i])) for i in range(10)]


def constant_tables(radial):
    plane = (WEIGHTS[:, None] * WEIGHTS[None, :]).reshape(64, 1)
    mult_r = np.ones((8, radial))
    mult_r[0, 1:] = 2.0
    mult_r[7, :-1] = 2.0
    ends = np.array([2.0, 1, 1, 1, 1, 1, 1, 2.0])
    mult = (ends[:, None, None] * mult_r[None]).reshape(64, radial)
    return dict(
        plane=f32(np.broadcast_to(plane, (64, radial))),
        over=f32(1.0 / mult),
        spectrum=f32(np.broadcast_to(SPECTRUM[:, None], (112, radial))),
        grad=split_terms(GRAD, 64),
        div=split_terms(GRAD.T, 128),
        into=split_terms(BOX_ROWS.T, 144),
        outof=split_terms(BOX_ROWS, 112),
    )


def product(table_ref, values):
    high = values.astype(BF16)
    low = (values - high.astype(F32)).astype(BF16)
    return jnp.dot(
        table_ref[...], jnp.concatenate([high, low, high], axis=0), preferred_element_type=F32
    )


def combine(coefs, terms):
    total = None
    for coef, term in zip(coefs, terms):
        scaled = float(coef) * term
        total = scaled if total is None else total + scaled
    return total


def skew_apply(matrix, parts):
    plus = [parts[b] + parts[7 - b] for b in range(4)]
    minus = [parts[b] - parts[7 - b] for b in range(4)]
    result = [None] * 8
    for a in range(4):
        even = combine([0.5 * (matrix[a, b] + matrix[a, 7 - b]) for b in range(4)], plus)
        odd = combine([0.5 * (matrix[a, b] - matrix[a, 7 - b]) for b in range(4)], minus)
        result[a] = even + odd
        result[7 - a] = odd - even
    return result


def to_spectral(parts):
    plus = [parts[a] + parts[9 - a] for a in range(5)]
    minus = [parts[a] - parts[9 - a] for a in range(5)]
    return [combine(BASIS[:5, i], plus if EVEN[i] else minus) for i in range(10)]


def from_spectral(parts):
    evens = [i for i in range(10) if EVEN[i]]
    odds = [i for i in range(10) if not EVEN[i]]
    result = [None] * 10
    for a in range(5):
        even = combine(BASIS[a, evens], [parts[i] for i in evens])
        odd = combine(BASIS[a, odds], [parts[i] for i in odds])
        result[a] = even + odd
        result[9 - a] = even - odd
    return result


def masks(rows):
    layer = lax.broadcasted_iota(jnp.int32, (rows, LANES), 0) % 8
    elem = lax.broadcasted_iota(jnp.int32, (rows, LANES), 1)
    return layer, elem > 0, elem < LANES - 1


def spread(values, first, last):
    layer, has_before, has_after = masks(values.shape[0])
    before = pltpu.roll(values, 1, axis=1)
    after = pltpu.roll(values, LANES - 1, axis=1)
    return jnp.where(
        (layer == first) & has_before,
        before,
        jnp.where((layer == last) & has_after, after, 0.0),
    )


def radial_sum(values):
    rows = values.shape[0]
    layer, _, _ = masks(rows)
    cubes = values.reshape(rows // 8, 8, LANES)
    up = pltpu.roll(cubes, 1, axis=1).reshape(rows, LANES)
    down = pltpu.roll(cubes, 7, axis=1).reshape(rows, LANES)
    return values + spread(jnp.where(layer == 0, up, down), 0, 7)


def total(values):
    return jnp.sum(values, axis=(0, 1), keepdims=True)


def add_rows(block, extra):
    pieces = []
    for b in range(8):
        piece = block[8 * b : 8 * b + 8]
        pieces.append(piece + extra[b] if b in extra else piece)
    return jnp.concatenate(pieces, axis=0)


def is_even():
    return lax.axis_index("axial") % 2 == 0


def send_axial(inner_ref, outer_ref, low, high):
    even = is_even()
    row = 0
    for low_piece, high_piece in zip(low, high):
        size = low_piece.shape[0]
        inner_ref[row : row + size] = jnp.where(even, high_piece, low_piece)
        outer_ref[row : row + size] = jnp.where(even, low_piece, high_piece)
        row += size


def got_axial(inner_ref, outer_ref):
    even = is_even()

    def before(start, size):
        return jnp.where(even, outer_ref[start : start + size], inner_ref[start : start + size])

    def after(start, size):
        return jnp.where(even, inner_ref[start : start + size], outer_ref[start : start + size])

    return before, after


def conv_kernel(
    u_hbm, row_hbm, plane_hbm, grad_hbm,
    conv_ref, row_ref, in_ref, out_ref, early_ref, late_ref,
    u_ref, small_ref, plane_ref, grad_ref, sems,
):
    copies = [
        pltpu.make_async_copy(source, target, sems.at[k])
        for k, (source, target) in enumerate(
            ((u_hbm, u_ref), (plane_hbm, plane_ref), (grad_hbm, grad_ref), (row_hbm, small_ref))
        )
    ]
    for copy in copies:
        copy.start()
    row_ref[...] = jnp.zeros(row_ref.shape, F32)
    for copy in copies:
        copy.wait()
    size = small_ref.shape[1]
    for k in range(-(-size // LANES)):
        stop = min(LANES, size - LANES * k)
        row_ref[k : k + 1, :stop] = small_ref[:, LANES * k : LANES * k + stop]
    plane = plane_ref[...]
    fields = [[u_ref[d, a] for a in range(8)] for d in range(3)]
    low, high = [], []
    for comp in range(3):
        parts = fields[comp]
        flat = product(grad_ref, jnp.concatenate(parts, axis=1))
        along_a = skew_apply(DERIV, parts)
        for a in range(8):
            cols = slice(LANES * a, LANES * a + LANES)
            value = (
                fields[0][a] * along_a[a]
                + fields[1][a] * flat[:64, cols]
                + fields[2][a] * flat[64:, cols]
            )
            value = radial_sum(float(WEIGHTS[a]) * plane * value)
            conv_ref[comp, a] = value
            for side, rows in enumerate((value[:8], value[56:])):
                if a in (0, 7):
                    start = 16 * comp + (8 if a else 0)
                    late_ref[side, start : start + 8] = rows
                else:
                    start = 48 * comp + 8 * (a - 1)
                    early_ref[side, start : start + 8] = rows
            if a == 0:
                low.append(value)
            if a == 7:
                high.append(value)
    row = row_ref[...]
    send_axial(in_ref, out_ref, low + [row], high + [row])


def mean_kernel(diff_ref, kbar_ref):
    mean = diff_ref[0]
    for a in range(1, 8):
        mean = mean + diff_ref[a]
    mean = jnp.sum(mean, axis=0, keepdims=True) * (1.0 / 512.0)
    kbar_ref[...] = jnp.broadcast_to(mean, (8, LANES))


def conv_side_kernel(in_ref, out_ref, late_ref, row_ref, send_ref):
    before, after = got_axial(in_ref, out_ref)
    count = row_ref.shape[0]
    for side, b in ((0, 0), (1, 7)):
        for comp in range(3):
            first = slice(16 * comp, 16 * comp + 8)
            last = slice(16 * comp + 8, 16 * comp + 16)
            row = 64 * comp + 8 * b
            send_ref[side, first] = late_ref[side, first] + before(row, 8)
            send_ref[side, last] = late_ref[side, last] + after(row, 8)
        for place, rows in enumerate((before(192, count), row_ref[...], after(192, count))):
            start = 48 + place * count
            send_ref[side, start : start + count] = rows


def coarse_share(raw, near_ref):
    middle = raw[1]
    for a in range(2, 7):
        middle = middle + raw[a]
    per_axial = (0.5 * raw[0], middle + 0.5 * (raw[0] + raw[7]), 0.5 * raw[7])
    rows = []
    for part in per_axial:
        inner = part[8:16]
        for b in range(2, 7):
            inner = inner + part[8 * b : 8 * b + 8]
        ends = (part[:8], part[56:])
        for piece in (0.5 * ends[0], inner + 0.5 * (ends[0] + ends[1]), 0.5 * ends[1]):
            rows.append(jnp.sum(piece, axis=0, keepdims=True))
    rows = jnp.concatenate(rows + [jnp.zeros((7, LANES), F32)], axis=0)
    shares = jnp.sum(rows, axis=1, keepdims=True)
    return jnp.sum(shares * near_ref[...], axis=0, keepdims=True)


def send_sums(pay_ref, row, scalars):
    width = pay_ref.shape[1]
    place = lax.broadcasted_iota(jnp.int32, (1, width), 1)
    for k, value in enumerate(scalars):
        row = jnp.where(place == width - 1 - k, value, row)
    pay_ref[...] = jnp.broadcast_to(row, pay_ref.shape)


def got_sums(ref, scalars):
    row = jnp.sum(ref[...], axis=0, keepdims=True)
    width = row.shape[1]
    place = lax.broadcasted_iota(jnp.int32, (1, width), 1)
    values = [
        jnp.sum(jnp.where(place == width - 1 - k, row, 0.0), axis=1, keepdims=True)
        for k in range(scalars)
    ]
    return jnp.where(place >= width - TAIL, 0.0, row), values


def send_raw(raw, g_ref, in_ref, out_ref, early_ref, late_ref):
    parts = [radial_sum(raw[a]) for a in range(8)]
    for a in range(8):
        g_ref[a] = parts[a]
    send_axial(in_ref, out_ref, [parts[0], parts[1]], [parts[7], parts[6]])
    for side, (edge, inner) in enumerate(((0, 1), (7, 6))):
        edges = [part[8 * edge : 8 * edge + 8] for part in parts]
        inners = [part[8 * inner : 8 * inner + 8] for part in parts]
        for a in range(1, 7):
            early_ref[side, 8 * a - 8 : 8 * a] = edges[a]
            early_ref[side, 40 + 8 * a : 48 + 8 * a] = inners[a]
        late_ref[side, :8] = edges[0]
        late_ref[side, 8:16] = edges[7]
        late_ref[side, 16:24] = inners[0]
        late_ref[side, 24:32] = inners[7]


def raw_side_kernel(in_ref, out_ref, late_ref, row_ref, send_ref, pass_ref):
    pass_ref[...] = row_ref[...]
    before, after = got_axial(in_ref, out_ref)
    for side, (edge, inner) in enumerate(((0, 1), (7, 6))):
        send_ref[side, :8] = before(64 + 8 * edge, 8)
        send_ref[side, 8:16] = late_ref[side, :8] + before(8 * edge, 8)
        send_ref[side, 16:24] = late_ref[side, 8:16] + after(8 * edge, 8)
        send_ref[side, 24:32] = after(64 + 8 * edge, 8)
        send_ref[side, 32:40] = late_ref[side, 16:24] + before(8 * inner, 8)
        send_ref[side, 40:48] = late_ref[side, 24:32] + after(8 * inner, 8)


def divergence_kernel(
    conv_ref, u_ref, in_ref, out_ref, early_ref, late_ref, row_ref, plane_ref, over_ref, div_ref,
    g_ref, send_in_ref, send_out_ref, send_early_ref, send_late_ref, near_ref, pay_ref,
):
    before, after = got_axial(in_ref, out_ref)
    plane, over = plane_ref[...], over_ref[...]

    def side_rows(side, comp, a):
        if a in (0, 7):
            start = 16 * comp + (8 if a else 0)
            return late_ref[side, start : start + 8]
        start = 48 * comp + 8 * (a - 1)
        return early_ref[side, start : start + 8]

    moved = []
    for comp in range(3):
        parts = []
        for a in range(8):
            value = conv_ref[comp, a]
            if a == 0:
                value = value + before(64 * comp, 64)
            if a == 7:
                value = value + after(64 * comp, 64)
            value = add_rows(value, {0: side_rows(1, comp, a), 7: side_rows(0, comp, a)})
            scale = time_increment * (0.5 if a in (0, 7) else 1.0)
            parts.append(float(WEIGHTS[a]) * plane * u_ref[comp, a] - scale * over * value)
        moved.append(parts)
    flat = product(
        div_ref,
        jnp.concatenate([jnp.concatenate(moved[1], axis=1), jnp.concatenate(moved[2], axis=1)], axis=0),
    )
    along_a = skew_apply(DERIV.T, moved[0])
    raw = [along_a[a] + flat[:, LANES * a : LANES * a + LANES] for a in range(8)]
    send_raw(raw, g_ref, send_in_ref, send_out_ref, send_early_ref, send_late_ref)
    count = row_ref.shape[0]
    width = near_ref.shape[1] // LANES
    near_ref[...] = jnp.zeros(near_ref.shape, F32)
    for i in range(3):
        start = 48 + i * count
        middle = (before(192, count), row_ref[...], after(192, count))[i]
        sides = (late_ref[1, start : start + count], middle, late_ref[0, start : start + count])
        for j, rows in enumerate(sides):
            for k in range(width):
                near_ref[3 * i + j : 3 * i + j + 1, LANES * k : LANES * k + LANES] = rows[k : k + 1]
    send_sums(pay_ref, coarse_share(raw, near_ref), [])


def got_planes(g_ref, in_ref, out_ref, early_ref, late_ref):
    before, after = got_axial(in_ref, out_ref)

    def edge_rows(side, e):
        if e in (0, 1, 8, 9):
            start = 8 * (0, 1, 8, 9).index(e)
            return late_ref[side, start : start + 8]
        return early_ref[side, 8 * e - 16 : 8 * e - 8]

    def inner_rows(side, a):
        if a in (0, 7):
            start = 40 if a else 32
            return late_ref[side, start : start + 8]
        return early_ref[side, 40 + 8 * a : 48 + 8 * a]

    zero = jnp.zeros((80, LANES), F32)
    planes = []
    for e in range(10):
        if e == 0:
            value = before(64, 64)
        elif e == 9:
            value = after(64, 64)
        else:
            value = g_ref[e - 1]
        if e == 1:
            value = value + before(0, 64)
        if e == 8:
            value = value + after(0, 64)
        value = add_rows(value, {0: edge_rows(1, e), 7: edge_rows(0, e)})
        if e in (0, 9):
            rows = [value, zero]
        else:
            rows = [value, spread(value, 6, 1), inner_rows(1, e - 1), inner_rows(0, e - 1)]
        planes.append(jnp.concatenate(rows, axis=0))
    return planes


def solve_kernel(
    g_ref, in_ref, out_ref, early_ref, late_ref, row_ref,
    kbar_ref, into_ref, outof_ref, spectrum_ref,
    planes_ref, solved_ref, part_ref, send_in_ref, send_out_ref, send_early_ref, send_late_ref,
    pass_ref,
):
    pass_ref[...] = row_ref[...]
    planes = got_planes(g_ref, in_ref, out_ref, early_ref, late_ref)
    for e in range(10):
        planes_ref[e] = planes[e]
    flat = product(into_ref, jnp.concatenate(planes, axis=1))
    parts = to_spectral([flat[:, LANES * e : LANES * e + LANES] for e in range(10)])
    kbar = kbar_ref[0:1, :]
    plane_spectrum = kbar * spectrum_ref[...] + mass_shift
    parts = [parts[i] / (plane_spectrum + float(EIGVAL[i]) * kbar) for i in range(10)]
    parts = from_spectral(parts)
    flat = product(outof_ref, jnp.concatenate(parts, axis=1))
    solved = [flat[:, LANES * e : LANES * e + LANES] for e in range(10)]
    for e in range(10):
        solved_ref[e] = solved[e]
    outer_a = [radial_sum(solved[0][:64]), radial_sum(solved[9][:64])]
    edges = []
    for a in range(8):
        rows = solved[a + 1]
        value = radial_sum(rows[:64] + spread(rows[64:128], 1, 6))
        outer_b = radial_sum(rows[128:144])
        part_ref[a] = value
        for side in range(2):
            edge = value[56 * side : 56 * side + 8]
            face = outer_b[8 * side : 8 * side + 8]
            if a in (0, 1, 6, 7):
                start = 8 * (0, 1, 6, 7).index(a)
                send_late_ref[side, start : start + 8] = edge
            else:
                send_early_ref[side, 8 * a - 16 : 8 * a - 8] = edge
            if a in (0, 7):
                start = 40 if a else 32
                send_late_ref[side, start : start + 8] = face
            else:
                send_early_ref[side, 24 + 8 * a : 32 + 8 * a] = face
        if a in (0, 7):
            edges.append((value, outer_b))
    send_axial(
        send_in_ref,
        send_out_ref,
        [edges[0][0], outer_a[0], edges[0][1]],
        [edges[1][0], outer_a[1], edges[1][1]],
    )


def solved_side_kernel(in_ref, out_ref, late_ref, row_ref, send_ref, pass_ref):
    pass_ref[...] = row_ref[...]
    before, after = got_axial(in_ref, out_ref)
    for side, b in ((0, 0), (1, 7)):
        row = 8 * b
        send_ref[side, :8] = late_ref[side, :8] + before(row, 8)
        send_ref[side, 8:16] = late_ref[side, 8:16] + before(64 + row, 8)
        send_ref[side, 16:24] = late_ref[side, 16:24] + after(64 + row, 8)
        send_ref[side, 24:32] = late_ref[side, 24:32] + after(row, 8)
        send_ref[side, 32:40] = late_ref[side, 32:40] + before(128 + 8 * side, 8)
        send_ref[side, 40:48] = late_ref[side, 40:48] + after(128 + 8 * side, 8)


def got_solved(part_ref, in_ref, out_ref, early_ref, late_ref):
    before, after = got_axial(in_ref, out_ref)
    extra = {0: (before, 0), 1: (before, 64), 6: (after, 64), 7: (after, 0)}

    def edge_rows(side, a):
        if a in extra:
            start = 8 * (0, 1, 6, 7).index(a)
            return late_ref[side, start : start + 8]
        return early_ref[side, 8 * a - 16 : 8 * a - 8]

    def face_rows(side, a):
        if a in (0, 7):
            start = 40 if a else 32
            return late_ref[side, start : start + 8]
        return early_ref[side, 24 + 8 * a : 32 + 8 * a]

    result = []
    for a in range(8):
        value = part_ref[a]
        if a in extra:
            side, start = extra[a]
            value = value + side(start, 64)
        result.append(
            add_rows(
                value,
                {0: edge_rows(1, a), 1: face_rows(1, a), 6: face_rows(0, a), 7: edge_rows(0, a)},
            )
        )
    return result


def add_coarse(parts, row, near_ref):
    values = jnp.sum(near_ref[...] * row, axis=1, keepdims=True)
    own = [[values[3 * i + j : 3 * i + j + 1] for j in range(3)] for i in range(3)]
    b = lax.broadcasted_iota(jnp.int32, (64, LANES), 0) // 8
    fields = []
    for i in range(3):
        ends = [0.5 * (own[i][1] + own[i][j]) for j in (0, 2)]
        fields.append(jnp.where(b == 0, ends[0], jnp.where(b == 7, ends[1], own[i][1])))
    first, last = 0.5 * (fields[0] + fields[1]), 0.5 * (fields[1] + fields[2])
    return [
        parts[a] + (first if a == 0 else last if a == 7 else fields[1]) for a in range(8)
    ]


def apply_operator(values, diff_ref, plane_ref, grad_ref, div_ref):
    plane = plane_ref[...]
    coef = [float(WEIGHTS[a]) * plane * diff_ref[a] for a in range(8)]
    flat = product(grad_ref, jnp.concatenate(values, axis=1))
    along_a = skew_apply(DERIV, values)
    flux = jnp.concatenate(
        [
            jnp.concatenate([coef[a], coef[a]], axis=0) * flat[:, LANES * a : LANES * a + LANES]
            for a in range(8)
        ],
        axis=1,
    )
    flat = product(div_ref, flux)
    along_a = skew_apply(DERIV.T, [coef[a] * along_a[a] for a in range(8)])
    return [
        along_a[a]
        + flat[:, LANES * a : LANES * a + LANES]
        + (mass_shift * float(WEIGHTS[a])) * plane * values[a]
        for a in range(8)
    ]


def dot_parts(first, second):
    result = first[0] * second[0]
    for a in range(1, 8):
        result = result + first[a] * second[a]
    return total(result)


def norm(row):
    return jnp.sum(row * row, axis=1, keepdims=True)


def dot_planes(first, second):
    result = None
    for e in range(10):
        stop = 64 if e in (0, 9) else 144
        term = first[e][:stop] * second[e][:stop]
        term = jnp.sum(term.reshape(stop // 8, 8, LANES), axis=0)
        result = term if result is None else result + term
    return total(result)


def first_apply_kernel(
    part_ref, in_ref, out_ref, early_ref, late_ref, near_ref, diff_ref, plane_ref, grad_ref, div_ref,
    sums_ref, planes_ref, solved_ref,
    z_ref, raw_ref, g_ref, send_in_ref, send_out_ref, send_early_ref, send_late_ref, row_ref, pay_ref,
):
    row, _ = got_sums(sums_ref, 0)
    values = got_solved(part_ref, in_ref, out_ref, early_ref, late_ref)
    values = add_coarse(values, row, near_ref)
    raw = apply_operator(values, diff_ref, plane_ref, grad_ref, div_ref)
    send_raw(raw, g_ref, send_in_ref, send_out_ref, send_early_ref, send_late_ref)
    for a in range(8):
        z_ref[a] = values[a]
        raw_ref[a] = raw[a]
    row_ref[0:1] = row
    scalars = [dot_planes(planes_ref, solved_ref), dot_parts(values, raw)]
    send_sums(pay_ref, coarse_share(raw, near_ref), scalars)


def first_step(sums_ref, row_ref):
    row_q, (local_rz, curv) = got_sums(sums_ref, 2)
    row_r = row_ref[0:1]
    rz = local_rz + norm(row_r)
    return row_r, row_q, rz, curv, rz / curv


def second_apply_kernel(
    part_ref, in_ref, out_ref, early_ref, late_ref, near_ref, diff_ref, plane_ref, grad_ref, div_ref,
    sums_ref, row_ref, z0_ref,
    y_ref, z_ref, raw_ref, g_ref, send_in_ref, send_out_ref, send_early_ref, send_late_ref,
):
    _, row_q, _, _, alpha = first_step(sums_ref, row_ref)
    change = got_solved(part_ref, in_ref, out_ref, early_ref, late_ref)
    change = add_coarse(change, row_q, near_ref)
    values = [z0_ref[a] - alpha * change[a] for a in range(8)]
    raw = apply_operator(values, diff_ref, plane_ref, grad_ref, div_ref)
    send_raw(raw, g_ref, send_in_ref, send_out_ref, send_early_ref, send_late_ref)
    for a in range(8):
        y_ref[a] = change[a]
        z_ref[a] = values[a]
        raw_ref[a] = raw[a]


def first_dots_kernel(
    sums_ref, row_ref, near_ref, planes_r_ref, planes_q_ref, solved_r_ref, solved_q_ref,
    z_ref, raw_ref, old_raw_ref,
    planes_ref, solved_ref, pay_ref,
):
    alpha = first_step(sums_ref, row_ref)[4]
    planes, solved = [], []
    for e in range(10):
        planes.append(planes_r_ref[e] - alpha * planes_q_ref[e])
        solved.append(solved_r_ref[e] - alpha * solved_q_ref[e])
        planes_ref[e] = planes[e]
        solved_ref[e] = solved[e]
    values = [z_ref[a] for a in range(8)]
    raw = [raw_ref[a] for a in range(8)]
    scalars = [
        dot_planes(planes, solved),
        dot_planes(planes, solved_q_ref),
        dot_planes(planes_q_ref, solved),
        dot_planes(planes_q_ref, solved_q_ref),
        dot_parts(values, raw),
        dot_parts(values, [old_raw_ref[a] for a in range(8)]),
    ]
    send_sums(pay_ref, coarse_share(raw, near_ref), scalars)


def second_dots_kernel(
    row_ref, planes_r_ref, planes_q_ref, planes_w_ref, solved_r_ref, solved_q_ref, solved_w_ref,
    pay_ref,
):
    scalars = [
        dot_planes(planes_r_ref, solved_w_ref),
        dot_planes(planes_q_ref, solved_w_ref),
        dot_planes(planes_w_ref, solved_r_ref),
        dot_planes(planes_w_ref, solved_q_ref),
        dot_planes(planes_w_ref, solved_w_ref),
    ]
    row = row_ref[...]
    width = row.shape[1]
    place = lax.broadcasted_iota(jnp.int32, (1, width), 1)
    for k, value in enumerate(scalars):
        row = jnp.where(place == width - 7 - k, value, row)
    pay_ref[...] = jnp.broadcast_to(row, pay_ref.shape)


def last_kernel(
    part_ref, in_ref, out_ref, early_ref, late_ref, near_ref, sums_ref, old_sums_ref, row_ref,
    y_ref, z0_ref, z1_ref, planes_r_ref, planes_q_ref, planes_w_ref,
    pressure_ref, residual_ref, direction_ref,
):
    row_r, row_q, rz0, curv0, alpha0 = first_step(old_sums_ref, row_ref)
    row_w, scalars = got_sums(sums_ref, 11)
    rr, rq, qr, qq, first_curv, cross, rw, qw, wr, wq, ww = scalars
    row_r = row_r - alpha0 * row_q
    rz1 = rr + norm(row_r)
    beta0 = rz1 / rz0
    curv1 = first_curv + beta0 * (2.0 * cross + beta0 * curv0)
    alpha1 = rz1 / curv1
    row = row_w + beta0 * row_q
    row_r = row_r - alpha1 * row
    step = -alpha1 * beta0
    rz2 = (
        rr
        - alpha1 * (rw + wr)
        + step * (rq + qr)
        + alpha1 * alpha1 * ww
        - alpha1 * step * (wq + qw)
        + step * step * qq
        + norm(row_r)
    )
    beta1 = rz2 / rz1
    change = got_solved(part_ref, in_ref, out_ref, early_ref, late_ref)
    change = add_coarse(change, row_w, near_ref)
    for a in range(8):
        first = z0_ref[a]
        second = z1_ref[a] + beta0 * first
        image = planes_w_ref[a + 1, :64] + beta0 * planes_q_ref[a + 1, :64]
        residual_ref[a] = planes_r_ref[a + 1, :64] - alpha1 * image
        pressure_ref[a] = alpha0 * first + alpha1 * second
        direction_ref[a] = (
            z1_ref[a] - alpha1 * (change[a] + beta0 * y_ref[a]) + beta1 * second
        )


def kernel_call(kernel, out_shapes, *args, **options):
    outs = [jax.ShapeDtypeStruct(shape, F32) for shape in out_shapes]
    return pl.pallas_call(
        kernel,
        out_shape=outs,
        compiler_params=pltpu.CompilerParams(vmem_limit_bytes=VMEM_GRANT),
        interpret=INTERPRET,
        **options,
    )(*args)


def axial_swap(inner_rows, outer_rows):
    count = lax.axis_size("axial")
    inner = [(i, i ^ 1) for i in range(count)]
    outer = [((2 * i + 1) % count, (2 * i + 2) % count) for i in range(count // 2)]
    outer = outer + [(b, a) for a, b in outer]
    from_outer = lax.ppermute(outer_rows, "axial", outer)
    from_inner = lax.ppermute(inner_rows, "axial", inner)
    return from_inner, from_outer


def azim_swap(sides):
    count = lax.axis_size("azim")
    if count == 2:
        return lax.ppermute(sides, "azim", [(0, 1), (1, 0)])
    after = lax.ppermute(sides[0], "azim", [((i + 1) % count, i) for i in range(count)])
    before = lax.ppermute(sides[1], "azim", [(i, (i + 1) % count) for i in range(count)])
    return jnp.stack([after, before])


def sum_steps():
    azim = lax.axis_size("azim")
    count = lax.axis_size("axial") * azim
    steps, step = [], 2 * azim
    while step < count:
        steps.append(step)
        step *= 2
    step = 1
    while step < azim:
        steps.append(step)
        step *= 2
    groups = [steps[k::4] for k in range(4)]
    groups[0] = groups[0] + [azim]
    return groups


def partial_sum(row, steps):
    count = lax.axis_size("axial") * lax.axis_size("azim")
    for step in steps:
        row = row + lax.ppermute(row, ALL, [(i, i ^ step) for i in range(count)])
    return row


def gather_sums(rows):
    return lax.all_to_all(rows, ALL, 0, 0, tiled=True)


def per_device(velocity, diffusivity, coarse_factor):
    shape = diffusivity.shape
    devices = lax.axis_size("axial") * lax.axis_size("azim")
    u = velocity.reshape(3, 8, 64, LANES)
    diff = diffusivity.reshape(8, 64, LANES)
    tables = constant_tables(LANES)
    plane, over, spectrum = tables["plane"], tables["over"], tables["spectrum"]
    grad, div, into, outof = tables["grad"], tables["div"], tables["into"], tables["outof"]
    coarse_size = coarse_factor.shape[1]
    width = -(-(coarse_size + TAIL) // LANES)
    count = 8 * -(-width // 8)

    field, sums, row_shape = (8, 64, LANES), (devices, width * LANES), (8, width * LANES)
    boxes = [(10, 144, LANES), (10, 144, LANES)]
    raw_sends = [(128, LANES), (128, LANES), (2, 96, LANES), (2, 32, LANES)]
    solved_sends = [(144, LANES), (144, LANES), (2, 80, LANES), (2, 48, LANES)]

    far = pl.BlockSpec(memory_space=pltpu.HBM)
    conv, row, *sends = kernel_call(
        conv_kernel,
        [(3,) + field, (count, LANES), (192 + count, LANES), (192 + count, LANES)]
        + [(2, 144, LANES), (2, 48, LANES)],
        *(pltpu.with_memory_space_constraint(x, pltpu.HBM) for x in (u, coarse_factor, plane, grad)),
        in_specs=[far] * 4,
        scratch_shapes=[
            pltpu.VMEM((3,) + field, F32),
            pltpu.VMEM((1, coarse_size), F32),
            pltpu.VMEM(plane.shape, F32),
            pltpu.VMEM(grad.shape, BF16),
            pltpu.SemaphoreType.DMA((4,)),
        ],
    )
    (kbar,) = kernel_call(mean_kernel, [(8, LANES)], diff)

    def exchange(side_kernel, late_rows, sends, extra, extra_shape=None):
        send_in, send_out, send_early, send_late = sends
        inner, outer = axial_swap(send_in, send_out)
        early = azim_swap(send_early)
        shapes = [(2, late_rows, LANES)]
        shapes = shapes if extra_shape is None else shapes + [extra_shape]
        late, *passed = kernel_call(side_kernel, shapes, inner, outer, send_late, extra)
        return [inner, outer, early, azim_swap(late)] + passed

    one = (1, width * LANES)
    groups = sum_steps()
    moved = exchange(conv_side_kernel, 48 + 3 * count, sends, row)
    g, *sends, near, pay = kernel_call(
        divergence_kernel,
        [field] + raw_sends + [(16, width * LANES), one],
        conv, u, *moved, row, plane, over, div,
    )
    solver = (kbar, into, outof, spectrum)
    operator = (near, diff, plane, grad, div)
    solve_shapes = boxes + [field] + solved_sends + [one]

    *moved, pay = exchange(raw_side_kernel, 48, sends, partial_sum(pay, groups[0]), one)
    pay = partial_sum(pay, groups[1])
    planes_r, solved_r, part, *sends, pay = kernel_call(
        solve_kernel, solve_shapes, g, *moved, pay, *solver
    )
    *moved, pay = exchange(solved_side_kernel, 48, sends, partial_sum(pay, groups[2]), one)
    pay = partial_sum(pay, groups[3])
    z0, raw0, g, *sends, row_r, pay = kernel_call(
        first_apply_kernel,
        [field, field, field] + raw_sends + [row_shape, one],
        part, *moved, *operator, pay, planes_r, solved_r,
    )
    *moved, pay = exchange(raw_side_kernel, 48, sends, partial_sum(pay, groups[0]), one)
    pay = partial_sum(pay, groups[1])
    planes_q, solved_q, part, *sends, pay = kernel_call(
        solve_kernel, solve_shapes, g, *moved, pay, *solver
    )
    *moved, pay = exchange(solved_side_kernel, 48, sends, partial_sum(pay, groups[2]), one)
    first_sums = partial_sum(pay, groups[3])
    y, z1, raw1, g, *sends = kernel_call(
        second_apply_kernel,
        [field, field, field, field] + raw_sends,
        part, *moved, *operator, first_sums, row_r, z0,
    )
    planes_r, solved_r, pay = kernel_call(
        first_dots_kernel,
        boxes + [one],
        first_sums, row_r, near, planes_r, planes_q, solved_r, solved_q, z1, raw1, raw0,
    )
    *moved, pay = exchange(raw_side_kernel, 48, sends, pay, one)
    planes_w, solved_w, part, *sends, pay = kernel_call(
        solve_kernel, solve_shapes, g, *moved, pay, *solver
    )
    (pay,) = kernel_call(
        second_dots_kernel, [sums], pay, planes_r, planes_q, planes_w, solved_r, solved_q, solved_w
    )
    *moved, pay = exchange(solved_side_kernel, 48, sends, gather_sums(pay), sums)
    pressure, residual, direction = kernel_call(
        last_kernel,
        [field, field, field],
        part, *moved, near, pay, first_sums, row_r,
        y, z0, z1, planes_r, planes_q, planes_w,
    )
    return pressure.reshape(shape), residual.reshape(shape), direction.reshape(shape)


def solution(mesh):
    split = P(None, None, None, "axial", "azim", None)
    in_specs = (P(None, None, None, None, "axial", "azim", None), split, P(ALL, None))
    return jax.shard_map(
        per_device, mesh=mesh, in_specs=in_specs, out_specs=(split, split, split), check_vma=False
    )
```

```python
import math

import jax
import jax.numpy as jnp
import numpy as np
from jax import lax
from jax.experimental import pallas as pl
from jax.experimental.pallas import tpu as pltpu
from jax.sharding import PartitionSpec as P

ALL = ("axial", "azim")
time_increment = 0.02
mass_shift = 0.05
VMEM_GRANT = 20 << 20
TAIL = 16
gll_points = [
    -1.0,
    -0.8717401485096066,
    -0.5917001814331423,
    -0.20929921790247888,
    0.20929921790247888,
    0.5917001814331423,
    0.8717401485096066,
    1.0,
]


def legendre_value(order, point):
    before = 1.0
    current = point
    for step_idx in range(1, order):
        after = ((2 * step_idx + 1) * point * current - step_idx * before) / (step_idx + 1)
        before = current
        current = after
    return current


def jacobi_eigen(matrix):
    size_n = len(matrix)
    work = [list(row) for row in matrix]
    vectors = [
        [1.0 if row_idx == col_idx else 0.0 for col_idx in range(size_n)]
        for row_idx in range(size_n)
    ]
    for sweep_idx in range(15):
        for row_idx in range(size_n):
            for col_idx in range(row_idx + 1, size_n):
                off_value = work[row_idx][col_idx]
                if off_value != 0.0:
                    theta = (work[col_idx][col_idx] - work[row_idx][row_idx]) / (2.0 * off_value)
                    root_val = math.sqrt(theta * theta + 1.0)
                    tangent = 1.0 / (theta + root_val) if theta >= 0.0 else 1.0 / (theta - root_val)
                    cosine = 1.0 / math.sqrt(tangent * tangent + 1.0)
                    sine = tangent * cosine
                    for other in range(size_n):
                        left_val = work[other][row_idx]
                        right_val = work[other][col_idx]
                        work[other][row_idx] = cosine * left_val - sine * right_val
                        work[other][col_idx] = sine * left_val + cosine * right_val
                    for other in range(size_n):
                        left_val = work[row_idx][other]
                        right_val = work[col_idx][other]
                        work[row_idx][other] = cosine * left_val - sine * right_val
                        work[col_idx][other] = sine * left_val + cosine * right_val
                    for other in range(size_n):
                        left_val = vectors[other][row_idx]
                        right_val = vectors[other][col_idx]
                        vectors[other][row_idx] = cosine * left_val - sine * right_val
                        vectors[other][col_idx] = sine * left_val + cosine * right_val
    return ([work[row_idx][row_idx] for row_idx in range(size_n)], vectors)


def gll_tables():
    degree = 7
    points = degree + 1
    legendre_at = [legendre_value(degree, node_val) for node_val in gll_points]
    weights = [2.0 / (degree * (degree + 1) * value * value) for value in legendre_at]
    derivative = [[0.0] * points for row_idx in range(points)]
    for row_idx in range(points):
        for col_idx in range(points):
            if row_idx != col_idx:
                derivative[row_idx][col_idx] = legendre_at[row_idx] / (
                    legendre_at[col_idx] * (gll_points[row_idx] - gll_points[col_idx])
                )
    derivative[0][0] = -degree * (degree + 1) / 4.0
    derivative[degree][degree] = degree * (degree + 1) / 4.0
    stiffness = [
        [
            sum(
                (
                    derivative[mid_idx][row_idx] * weights[mid_idx] * derivative[mid_idx][col_idx]
                    for mid_idx in range(points)
                )
            )
            for col_idx in range(points)
        ]
        for row_idx in range(points)
    ]
    line_len = 3 * degree + 1
    big_stiff = [[0.0] * line_len for row_idx in range(line_len)]
    big_mass = [0.0] * line_len
    for element in range(3):
        offset = element * degree
        for row_idx in range(points):
            big_mass[offset + row_idx] += weights[row_idx]
            for col_idx in range(points):
                big_stiff[offset + row_idx][offset + col_idx] += stiffness[row_idx][col_idx]
    start_node = degree - 1
    box_len = degree + 3
    scaling = [1.0 / math.sqrt(big_mass[start_node + row_idx]) for row_idx in range(box_len)]
    symmetric = [
        [
            scaling[row_idx]
            * big_stiff[start_node + row_idx][start_node + col_idx]
            * scaling[col_idx]
            for col_idx in range(box_len)
        ]
        for row_idx in range(box_len)
    ]
    eigval, eigvec = jacobi_eigen(symmetric)
    fdm_basis = [
        [scaling[row_idx] * eigvec[row_idx][col_idx] for col_idx in range(box_len)]
        for row_idx in range(box_len)
    ]
    return (weights, derivative, fdm_basis, eigval)

WEIGHTS, DERIV, BASIS, EIGVAL = (np.asarray(t, np.float64) for t in gll_tables())


def f32(table):
    return jnp.asarray(table, jnp.float32)


F32 = jnp.float32
BF16 = jnp.bfloat16
LANES = 128
INTERPRET = False


def split_terms(table, depth):
    padded = np.zeros((table.shape[0], depth))
    padded[:, : table.shape[1]] = table
    high = padded.astype(jnp.bfloat16)
    low = (padded - high.astype(np.float64)).astype(jnp.bfloat16)
    return jnp.asarray(np.concatenate([high, high, low], axis=1))


def box_tables():
    pairs = [(b + 1, c + 1) for b in range(8) for c in range(8)]
    pairs += [(b + 1, {6: 0, 1: 9}.get(c)) for b in range(8) for c in range(8)]
    pairs += [(0, c + 1) for c in range(8)] + [(9, c + 1) for c in range(8)]
    table = np.zeros((144, 112))
    for row, (b, c) in enumerate(pairs):
        if c is not None:
            table[row, :100] = np.outer(BASIS[b], BASIS[c]).reshape(100)
    sums = np.ones(112)
    sums[:100] = (EIGVAL[:, None] + EIGVAL[None, :]).reshape(100)
    return table, sums


EYE = np.eye(8)
GRAD = np.concatenate([np.kron(DERIV, EYE), np.kron(EYE, DERIV)])
BOX_ROWS, SPECTRUM = box_tables()
EVEN = [bool(abs(BASIS[0, i] - BASIS[9, i]) < abs(BASIS[0, i] + BASIS[9, i])) for i in range(10)]


def constant_tables(radial):
    plane = (WEIGHTS[:, None] * WEIGHTS[None, :]).reshape(64, 1)
    mult_r = np.ones((8, radial))
    mult_r[0, 1:] = 2.0
    mult_r[7, :-1] = 2.0
    ends = np.array([2.0, 1, 1, 1, 1, 1, 1, 2.0])
    mult = (ends[:, None, None] * mult_r[None]).reshape(64, radial)
    return dict(
        plane=f32(np.broadcast_to(plane, (64, radial))),
        over=f32(1.0 / mult),
        spectrum=f32(np.broadcast_to(SPECTRUM[:, None], (112, radial))),
        grad=split_terms(GRAD, 64),
        div=split_terms(GRAD.T, 128),
        into=split_terms(BOX_ROWS.T, 144),
        outof=split_terms(BOX_ROWS, 112),
    )


def product(table_ref, values):
    high = values.astype(BF16)
    low = (values - high.astype(F32)).astype(BF16)
    return jnp.dot(
        table_ref[...], jnp.concatenate([high, low, high], axis=0), preferred_element_type=F32
    )


def combine(coefs, terms):
    total = None
    for coef, term in zip(coefs, terms):
        scaled = float(coef) * term
        total = scaled if total is None else total + scaled
    return total


def skew_apply(matrix, parts):
    plus = [parts[b] + parts[7 - b] for b in range(4)]
    minus = [parts[b] - parts[7 - b] for b in range(4)]
    result = [None] * 8
    for a in range(4):
        even = combine([0.5 * (matrix[a, b] + matrix[a, 7 - b]) for b in range(4)], plus)
        odd = combine([0.5 * (matrix[a, b] - matrix[a, 7 - b]) for b in range(4)], minus)
        result[a] = even + odd
        result[7 - a] = odd - even
    return result


def to_spectral(parts):
    plus = [parts[a] + parts[9 - a] for a in range(5)]
    minus = [parts[a] - parts[9 - a] for a in range(5)]
    return [combine(BASIS[:5, i], plus if EVEN[i] else minus) for i in range(10)]


def from_spectral(parts):
    evens = [i for i in range(10) if EVEN[i]]
    odds = [i for i in range(10) if not EVEN[i]]
    result = [None] * 10
    for a in range(5):
        even = combine(BASIS[a, evens], [parts[i] for i in evens])
        odd = combine(BASIS[a, odds], [parts[i] for i in odds])
        result[a] = even + odd
        result[9 - a] = even - odd
    return result


def masks():
    layer = lax.broadcasted_iota(jnp.int32, (8, LANES), 0)
    elem = lax.broadcasted_iota(jnp.int32, (8, LANES), 1)
    return layer, elem > 0, elem < LANES - 1


def spread(values, first, last):
    layer, has_before, has_after = masks()
    cubes = values.reshape(values.shape[0] // 8, 8, LANES)
    before = pltpu.roll(cubes, 1, axis=2)
    after = pltpu.roll(cubes, LANES - 1, axis=2)
    before_mask = ((layer == first) & has_before)[None]
    after_mask = ((layer == last) & has_after)[None]
    result = jnp.where(before_mask, before, jnp.where(after_mask, after, 0.0))
    return result.reshape(values.shape)


def radial_sum(values):
    layer, has_before, has_after = masks()
    cubes = values.reshape(values.shape[0] // 8, 8, LANES)
    up = pltpu.roll(cubes, 1, axis=1)
    down = pltpu.roll(cubes, 7, axis=1)
    ends = jnp.where((layer == 0)[None], up, down)
    before = pltpu.roll(ends, 1, axis=2)
    after = pltpu.roll(ends, LANES - 1, axis=2)
    before_mask = ((layer == 0) & has_before)[None]
    after_mask = ((layer == 7) & has_after)[None]
    ends = jnp.where(before_mask, before, jnp.where(after_mask, after, 0.0))
    return (cubes + ends).reshape(values.shape)


def total(values):
    return jnp.sum(values, axis=(0, 1), keepdims=True)


def add_rows(block, extra):
    pieces = []
    for b in range(8):
        piece = block[8 * b : 8 * b + 8]
        pieces.append(piece + extra[b] if b in extra else piece)
    return jnp.concatenate(pieces, axis=0)


def is_even():
    return lax.axis_index("axial") % 2 == 0


def send_axial(inner_ref, outer_ref, low, high):
    even = is_even()
    row = 0
    for low_piece, high_piece in zip(low, high):
        size = low_piece.shape[0]
        inner_ref[row : row + size] = jnp.where(even, high_piece, low_piece)
        outer_ref[row : row + size] = jnp.where(even, low_piece, high_piece)
        row += size


def got_axial(inner_ref, outer_ref):
    even = is_even()

    def before(start, size):
        return jnp.where(even, outer_ref[start : start + size], inner_ref[start : start + size])

    def after(start, size):
        return jnp.where(even, inner_ref[start : start + size], outer_ref[start : start + size])

    return before, after


def conv_kernel(
    u_hbm, row_hbm, plane_hbm, grad_hbm,
    conv_ref, row_ref, out_ref, early_ref, in_ref, late_ref,
    u_ref, small_ref, plane_ref, grad_ref, sems,
):
    copies = [
        pltpu.make_async_copy(source, target, sems.at[k])
        for k, (source, target) in enumerate(
            ((u_hbm, u_ref), (plane_hbm, plane_ref), (grad_hbm, grad_ref), (row_hbm, small_ref))
        )
    ]
    for copy in copies:
        copy.start()
    row_ref[...] = jnp.zeros(row_ref.shape, F32)
    for copy in copies:
        copy.wait()
    size = small_ref.shape[1]
    for k in range(-(-size // LANES)):
        stop = min(LANES, size - LANES * k)
        row_ref[k : k + 1, :stop] = small_ref[:, LANES * k : LANES * k + stop]
    plane = plane_ref[...]
    fields = [[u_ref[d, a] for a in range(8)] for d in range(3)]
    low, high = [], []
    for comp in range(3):
        parts = fields[comp]
        flat = product(grad_ref, jnp.concatenate(parts, axis=1))
        along_a = skew_apply(DERIV, parts)
        for a in range(8):
            cols = slice(LANES * a, LANES * a + LANES)
            value = (
                fields[0][a] * along_a[a]
                + fields[1][a] * flat[:64, cols]
                + fields[2][a] * flat[64:, cols]
            )
            value = radial_sum(float(WEIGHTS[a]) * plane * value)
            conv_ref[comp, a] = value
            for side, rows in enumerate((value[:8], value[56:])):
                if a in (0, 7):
                    start = 16 * comp + (8 if a else 0)
                    late_ref[side, start : start + 8] = rows
                else:
                    start = 48 * comp + 8 * (a - 1)
                    early_ref[side, start : start + 8] = rows
            if a == 0:
                low.append(value)
            if a == 7:
                high.append(value)
    row = row_ref[...]
    send_axial(in_ref, out_ref, low + [row], high + [row])


def inverse_kernel(diff_ref, spectrum_ref, inverse_ref):
    mean = diff_ref[0]
    for a in range(1, 8):
        mean = mean + diff_ref[a]
    kbar = jnp.sum(mean, axis=0, keepdims=True) * (1.0 / 512.0)
    plane_spectrum = kbar * spectrum_ref[...] + mass_shift
    for i in range(10):
        inverse_ref[i] = 1.0 / (plane_spectrum + float(EIGVAL[i]) * kbar)


def conv_side_kernel(out_ref, in_ref, late_ref, row_ref, send_ref):
    before, after = got_axial(in_ref, out_ref)
    count = row_ref.shape[0]
    for side, b in ((0, 0), (1, 7)):
        for comp in range(3):
            first = slice(16 * comp, 16 * comp + 8)
            last = slice(16 * comp + 8, 16 * comp + 16)
            row = 64 * comp + 8 * b
            send_ref[side, first] = late_ref[side, first] + before(row, 8)
            send_ref[side, last] = late_ref[side, last] + after(row, 8)
        for place, rows in enumerate((before(192, count), row_ref[...], after(192, count))):
            start = 48 + place * count
            send_ref[side, start : start + count] = rows


def coarse_share(raw, near_ref):
    middle = raw[1]
    for a in range(2, 7):
        middle = middle + raw[a]
    per_axial = (0.5 * raw[0], middle + 0.5 * (raw[0] + raw[7]), 0.5 * raw[7])
    rows = []
    for part in per_axial:
        inner = part[8:16]
        for b in range(2, 7):
            inner = inner + part[8 * b : 8 * b + 8]
        ends = (part[:8], part[56:])
        for piece in (0.5 * ends[0], inner + 0.5 * (ends[0] + ends[1]), 0.5 * ends[1]):
            rows.append(jnp.sum(piece, axis=0, keepdims=True))
    rows = jnp.concatenate(rows + [jnp.zeros((7, LANES), F32)], axis=0)
    shares = jnp.sum(rows, axis=1, keepdims=True)
    return jnp.sum(shares * near_ref[...], axis=0, keepdims=True)


def send_sums(pay_ref, row, scalars):
    width = pay_ref.shape[1]
    place = lax.broadcasted_iota(jnp.int32, (1, width), 1)
    for k, value in enumerate(scalars):
        row = jnp.where(place == width - 1 - k, value, row)
    pay_ref[...] = jnp.broadcast_to(row, pay_ref.shape)


def got_sums(ref, scalars):
    row = jnp.sum(ref[...], axis=0, keepdims=True)
    width = row.shape[1]
    place = lax.broadcasted_iota(jnp.int32, (1, width), 1)
    values = [
        jnp.sum(jnp.where(place == width - 1 - k, row, 0.0), axis=1, keepdims=True)
        for k in range(scalars)
    ]
    return jnp.where(place >= width - TAIL, 0.0, row), values


def send_raw(raw, g_ref, in_ref, out_ref, early_ref, late_ref):
    parts = [radial_sum(raw[a]) for a in range(8)]
    for a in range(8):
        g_ref[a] = parts[a]
    send_axial(in_ref, out_ref, [parts[0], parts[1]], [parts[7], parts[6]])
    for side, (edge, inner) in enumerate(((0, 1), (7, 6))):
        edges = [part[8 * edge : 8 * edge + 8] for part in parts]
        inners = [part[8 * inner : 8 * inner + 8] for part in parts]
        for a in range(1, 7):
            early_ref[side, 8 * a - 8 : 8 * a] = edges[a]
            early_ref[side, 40 + 8 * a : 48 + 8 * a] = inners[a]
        late_ref[side, :8] = edges[0]
        late_ref[side, 8:16] = edges[7]
        late_ref[side, 16:24] = inners[0]
        late_ref[side, 24:32] = inners[7]


def raw_side_kernel(out_ref, in_ref, late_ref, row_ref, send_ref, pass_ref):
    pass_ref[...] = row_ref[...]
    before, after = got_axial(in_ref, out_ref)
    for side, (edge, inner) in enumerate(((0, 1), (7, 6))):
        send_ref[side, :8] = before(64 + 8 * edge, 8)
        send_ref[side, 8:16] = late_ref[side, :8] + before(8 * edge, 8)
        send_ref[side, 16:24] = late_ref[side, 8:16] + after(8 * edge, 8)
        send_ref[side, 24:32] = after(64 + 8 * edge, 8)
        send_ref[side, 32:40] = late_ref[side, 16:24] + before(8 * inner, 8)
        send_ref[side, 40:48] = late_ref[side, 24:32] + after(8 * inner, 8)


def divergence_kernel(
    conv_ref, u_ref, out_ref, in_ref, early_ref, late_ref, row_ref, plane_ref, over_ref, div_ref,
    g_ref, send_out_ref, send_early_ref, send_in_ref, send_late_ref, near_ref, pay_ref,
):
    before, after = got_axial(in_ref, out_ref)
    plane, over = plane_ref[...], over_ref[...]

    def side_rows(side, comp, a):
        if a in (0, 7):
            start = 16 * comp + (8 if a else 0)
            return late_ref[side, start : start + 8]
        start = 48 * comp + 8 * (a - 1)
        return early_ref[side, start : start + 8]

    moved = []
    for comp in range(3):
        parts = []
        for a in range(8):
            value = conv_ref[comp, a]
            if a == 0:
                value = value + before(64 * comp, 64)
            if a == 7:
                value = value + after(64 * comp, 64)
            value = add_rows(value, {0: side_rows(1, comp, a), 7: side_rows(0, comp, a)})
            scale = time_increment * (0.5 if a in (0, 7) else 1.0)
            parts.append(float(WEIGHTS[a]) * plane * u_ref[comp, a] - scale * over * value)
        moved.append(parts)
    flat = product(
        div_ref,
        jnp.concatenate([jnp.concatenate(moved[1], axis=1), jnp.concatenate(moved[2], axis=1)], axis=0),
    )
    along_a = skew_apply(DERIV.T, moved[0])
    raw = [along_a[a] + flat[:, LANES * a : LANES * a + LANES] for a in range(8)]
    send_raw(raw, g_ref, send_in_ref, send_out_ref, send_early_ref, send_late_ref)
    count = row_ref.shape[0]
    width = near_ref.shape[1] // LANES
    near_ref[...] = jnp.zeros(near_ref.shape, F32)
    for i in range(3):
        start = 48 + i * count
        middle = (before(192, count), row_ref[...], after(192, count))[i]
        sides = (late_ref[1, start : start + count], middle, late_ref[0, start : start + count])
        for j, rows in enumerate(sides):
            for k in range(width):
                near_ref[3 * i + j : 3 * i + j + 1, LANES * k : LANES * k + LANES] = rows[k : k + 1]
    send_sums(pay_ref, coarse_share(raw, near_ref), [])


def got_planes(g_ref, in_ref, out_ref, early_ref, late_ref):
    before, after = got_axial(in_ref, out_ref)

    def edge_rows(side, e):
        if e in (0, 1, 8, 9):
            start = 8 * (0, 1, 8, 9).index(e)
            return late_ref[side, start : start + 8]
        return early_ref[side, 8 * e - 16 : 8 * e - 8]

    def inner_rows(side, a):
        if a in (0, 7):
            start = 40 if a else 32
            return late_ref[side, start : start + 8]
        return early_ref[side, 40 + 8 * a : 48 + 8 * a]

    zero = jnp.zeros((80, LANES), F32)
    planes = []
    for e in range(10):
        if e == 0:
            value = before(64, 64)
        elif e == 9:
            value = after(64, 64)
        else:
            value = g_ref[e - 1]
        if e == 1:
            value = value + before(0, 64)
        if e == 8:
            value = value + after(0, 64)
        value = add_rows(value, {0: edge_rows(1, e), 7: edge_rows(0, e)})
        if e in (0, 9):
            rows = [value, zero]
        else:
            rows = [value, spread(value, 6, 1), inner_rows(1, e - 1), inner_rows(0, e - 1)]
        planes.append(jnp.concatenate(rows, axis=0))
    return planes


def solve_kernel(
    g_ref, out_ref, in_ref, early_ref, late_ref, row_ref,
    inverse_ref, into_ref, outof_ref,
    planes_ref, solved_ref, part_ref, send_out_ref, send_early_ref, send_in_ref, send_late_ref,
    pass_ref,
):
    pass_ref[...] = row_ref[...]
    planes = got_planes(g_ref, in_ref, out_ref, early_ref, late_ref)
    for e in range(10):
        planes_ref[e] = planes[e]
    flat = product(into_ref, jnp.concatenate(planes, axis=1))
    parts = to_spectral([flat[:, LANES * e : LANES * e + LANES] for e in range(10)])
    parts = [parts[i] * inverse_ref[i] for i in range(10)]
    parts = from_spectral(parts)
    flat = product(outof_ref, jnp.concatenate(parts, axis=1))
    solved = [flat[:, LANES * e : LANES * e + LANES] for e in range(10)]
    for e in range(10):
        solved_ref[e] = solved[e]
    outer_a = [radial_sum(solved[0][:64]), radial_sum(solved[9][:64])]
    edges = []
    for a in range(8):
        rows = solved[a + 1]
        value = radial_sum(rows[:64] + spread(rows[64:128], 1, 6))
        outer_b = radial_sum(rows[128:144])
        part_ref[a] = value
        for side in range(2):
            edge = value[56 * side : 56 * side + 8]
            face = outer_b[8 * side : 8 * side + 8]
            if a in (0, 1, 6, 7):
                start = 8 * (0, 1, 6, 7).index(a)
                send_late_ref[side, start : start + 8] = edge
            else:
                send_early_ref[side, 8 * a - 16 : 8 * a - 8] = edge
            if a in (0, 7):
                start = 40 if a else 32
                send_late_ref[side, start : start + 8] = face
            else:
                send_early_ref[side, 24 + 8 * a : 32 + 8 * a] = face
        if a in (0, 7):
            edges.append((value, outer_b))
    send_axial(
        send_in_ref,
        send_out_ref,
        [edges[0][0], outer_a[0], edges[0][1]],
        [edges[1][0], outer_a[1], edges[1][1]],
    )


def solved_side_kernel(out_ref, in_ref, late_ref, row_ref, send_ref, pass_ref):
    pass_ref[...] = row_ref[...]
    before, after = got_axial(in_ref, out_ref)
    for side, b in ((0, 0), (1, 7)):
        row = 8 * b
        send_ref[side, :8] = late_ref[side, :8] + before(row, 8)
        send_ref[side, 8:16] = late_ref[side, 8:16] + before(64 + row, 8)
        send_ref[side, 16:24] = late_ref[side, 16:24] + after(64 + row, 8)
        send_ref[side, 24:32] = late_ref[side, 24:32] + after(row, 8)
        send_ref[side, 32:40] = late_ref[side, 32:40] + before(128 + 8 * side, 8)
        send_ref[side, 40:48] = late_ref[side, 40:48] + after(128 + 8 * side, 8)


def got_solved(part_ref, in_ref, out_ref, early_ref, late_ref):
    before, after = got_axial(in_ref, out_ref)
    extra = {0: (before, 0), 1: (before, 64), 6: (after, 64), 7: (after, 0)}

    def edge_rows(side, a):
        if a in extra:
            start = 8 * (0, 1, 6, 7).index(a)
            return late_ref[side, start : start + 8]
        return early_ref[side, 8 * a - 16 : 8 * a - 8]

    def face_rows(side, a):
        if a in (0, 7):
            start = 40 if a else 32
            return late_ref[side, start : start + 8]
        return early_ref[side, 24 + 8 * a : 32 + 8 * a]

    result = []
    for a in range(8):
        value = part_ref[a]
        if a in extra:
            side, start = extra[a]
            value = value + side(start, 64)
        result.append(
            add_rows(
                value,
                {0: edge_rows(1, a), 1: face_rows(1, a), 6: face_rows(0, a), 7: edge_rows(0, a)},
            )
        )
    return result


def add_coarse(parts, row, near_ref):
    values = jnp.sum(near_ref[...] * row, axis=1, keepdims=True)
    own = [[values[3 * i + j : 3 * i + j + 1] for j in range(3)] for i in range(3)]
    fields = []
    for i in range(3):
        ends = [0.5 * (own[i][1] + own[i][j]) for j in (0, 2)]
        rows = [jnp.broadcast_to(value, (8, LANES)) for value in (ends[0], own[i][1], ends[1])]
        fields.append(jnp.concatenate([rows[0]] + [rows[1]] * 6 + [rows[2]], axis=0))
    first, last = 0.5 * (fields[0] + fields[1]), 0.5 * (fields[1] + fields[2])
    return [
        parts[a] + (first if a == 0 else last if a == 7 else fields[1]) for a in range(8)
    ]


def apply_operator(values, diff_ref, plane_ref, grad_ref, div_ref):
    plane = plane_ref[...]
    coef = [float(WEIGHTS[a]) * plane * diff_ref[a] for a in range(8)]
    flat = product(grad_ref, jnp.concatenate(values, axis=1))
    along_a = skew_apply(DERIV, values)
    flux = jnp.concatenate(
        [
            jnp.concatenate([coef[a], coef[a]], axis=0) * flat[:, LANES * a : LANES * a + LANES]
            for a in range(8)
        ],
        axis=1,
    )
    flat = product(div_ref, flux)
    along_a = skew_apply(DERIV.T, [coef[a] * along_a[a] for a in range(8)])
    return [
        along_a[a]
        + flat[:, LANES * a : LANES * a + LANES]
        + (mass_shift * float(WEIGHTS[a])) * plane * values[a]
        for a in range(8)
    ]


def dot_parts(first, second):
    result = first[0] * second[0]
    for a in range(1, 8):
        result = result + first[a] * second[a]
    return total(result)


def norm(row):
    return jnp.sum(row * row, axis=1, keepdims=True)


def dot_planes(first, second):
    result = None
    for e in range(10):
        stop = 64 if e in (0, 9) else 144
        term = first[e][:stop] * second[e][:stop]
        term = jnp.sum(term.reshape(stop // 8, 8, LANES), axis=0)
        result = term if result is None else result + term
    return total(result)


def first_apply_kernel(
    part_ref, out_ref, in_ref, early_ref, late_ref, near_ref, diff_ref, plane_ref, grad_ref, div_ref,
    sums_ref, planes_ref, solved_ref,
    z_ref, raw_ref, g_ref, send_out_ref, send_early_ref, send_in_ref, send_late_ref, row_ref, pay_ref,
):
    row, _ = got_sums(sums_ref, 0)
    values = got_solved(part_ref, in_ref, out_ref, early_ref, late_ref)
    values = add_coarse(values, row, near_ref)
    raw = apply_operator(values, diff_ref, plane_ref, grad_ref, div_ref)
    send_raw(raw, g_ref, send_in_ref, send_out_ref, send_early_ref, send_late_ref)
    for a in range(8):
        z_ref[a] = values[a]
        raw_ref[a] = raw[a]
    row_ref[0:1] = row
    scalars = [dot_planes(planes_ref, solved_ref), dot_parts(values, raw)]
    send_sums(pay_ref, coarse_share(raw, near_ref), scalars)


def first_step(sums_ref, row_ref):
    row_q, (local_rz, curv) = got_sums(sums_ref, 2)
    row_r = row_ref[0:1]
    rz = local_rz + norm(row_r)
    return row_r, row_q, rz, curv, rz / curv


def second_apply_kernel(
    part_ref, out_ref, in_ref, early_ref, late_ref, near_ref, diff_ref, plane_ref, grad_ref, div_ref,
    sums_ref, row_ref, z0_ref,
    y_ref, z_ref, raw_ref, g_ref, send_out_ref, send_early_ref, send_in_ref, send_late_ref,
):
    _, row_q, _, _, alpha = first_step(sums_ref, row_ref)
    change = got_solved(part_ref, in_ref, out_ref, early_ref, late_ref)
    change = add_coarse(change, row_q, near_ref)
    values = [z0_ref[a] - alpha * change[a] for a in range(8)]
    raw = apply_operator(values, diff_ref, plane_ref, grad_ref, div_ref)
    send_raw(raw, g_ref, send_in_ref, send_out_ref, send_early_ref, send_late_ref)
    for a in range(8):
        y_ref[a] = change[a]
        z_ref[a] = values[a]
        raw_ref[a] = raw[a]


def first_dots_kernel(
    sums_ref, row_ref, near_ref, planes_r_ref, planes_q_ref, solved_r_ref, solved_q_ref,
    z_ref, raw_ref, old_raw_ref,
    planes_ref, solved_ref, pay_ref,
):
    alpha = first_step(sums_ref, row_ref)[4]
    planes, solved = [], []
    for e in range(10):
        planes.append(planes_r_ref[e] - alpha * planes_q_ref[e])
        solved.append(solved_r_ref[e] - alpha * solved_q_ref[e])
        planes_ref[e] = planes[e]
        solved_ref[e] = solved[e]
    values = [z_ref[a] for a in range(8)]
    raw = [raw_ref[a] for a in range(8)]
    scalars = [
        dot_planes(planes, solved),
        dot_planes(planes, solved_q_ref),
        dot_planes(planes_q_ref, solved),
        dot_planes(planes_q_ref, solved_q_ref),
        dot_parts(values, raw),
        dot_parts(values, [old_raw_ref[a] for a in range(8)]),
    ]
    send_sums(pay_ref, coarse_share(raw, near_ref), scalars)


def second_dots_kernel(
    row_ref, planes_r_ref, planes_q_ref, planes_w_ref, solved_r_ref, solved_q_ref, solved_w_ref,
    pay_ref,
):
    scalars = [
        dot_planes(planes_r_ref, solved_w_ref),
        dot_planes(planes_q_ref, solved_w_ref),
        dot_planes(planes_w_ref, solved_r_ref),
        dot_planes(planes_w_ref, solved_q_ref),
        dot_planes(planes_w_ref, solved_w_ref),
    ]
    row = row_ref[...]
    width = row.shape[1]
    place = lax.broadcasted_iota(jnp.int32, (1, width), 1)
    for k, value in enumerate(scalars):
        row = jnp.where(place == width - 7 - k, value, row)
    pay_ref[...] = jnp.broadcast_to(row, pay_ref.shape)


def last_kernel(
    part_ref, out_ref, in_ref, early_ref, late_ref, near_ref, sums_ref, old_sums_ref, row_ref,
    y_ref, z0_ref, z1_ref, planes_r_ref, planes_q_ref, planes_w_ref,
    pressure_ref, residual_ref, direction_ref,
):
    row_r, row_q, rz0, curv0, alpha0 = first_step(old_sums_ref, row_ref)
    row_w, scalars = got_sums(sums_ref, 11)
    rr, rq, qr, qq, first_curv, cross, rw, qw, wr, wq, ww = scalars
    row_r = row_r - alpha0 * row_q
    rz1 = rr + norm(row_r)
    beta0 = rz1 / rz0
    curv1 = first_curv + beta0 * (2.0 * cross + beta0 * curv0)
    alpha1 = rz1 / curv1
    row = row_w + beta0 * row_q
    row_r = row_r - alpha1 * row
    step = -alpha1 * beta0
    rz2 = (
        rr
        - alpha1 * (rw + wr)
        + step * (rq + qr)
        + alpha1 * alpha1 * ww
        - alpha1 * step * (wq + qw)
        + step * step * qq
        + norm(row_r)
    )
    beta1 = rz2 / rz1
    change = got_solved(part_ref, in_ref, out_ref, early_ref, late_ref)
    change = add_coarse(change, row_w, near_ref)
    for a in range(8):
        first = z0_ref[a]
        second = z1_ref[a] + beta0 * first
        image = planes_w_ref[a + 1, :64] + beta0 * planes_q_ref[a + 1, :64]
        residual_ref[a] = planes_r_ref[a + 1, :64] - alpha1 * image
        pressure_ref[a] = alpha0 * first + alpha1 * second
        direction_ref[a] = (
            z1_ref[a] - alpha1 * (change[a] + beta0 * y_ref[a]) + beta1 * second
        )


def kernel_call(kernel, out_shapes, *args, **options):
    outs = [jax.ShapeDtypeStruct(shape, F32) for shape in out_shapes]
    return pl.pallas_call(
        kernel,
        out_shape=outs,
        compiler_params=pltpu.CompilerParams(vmem_limit_bytes=VMEM_GRANT),
        interpret=INTERPRET,
        **options,
    )(*args)


def axial_swap(inner_rows, outer_rows):
    count = lax.axis_size("axial")
    inner = [(i, i ^ 1) for i in range(count)]
    outer = [((2 * i + 1) % count, (2 * i + 2) % count) for i in range(count // 2)]
    outer = outer + [(b, a) for a, b in outer]
    from_outer = lax.ppermute(outer_rows, "axial", outer)
    from_inner = lax.ppermute(inner_rows, "axial", inner)
    return from_inner, from_outer


def azim_swap(sides):
    count = lax.axis_size("azim")
    if count == 2:
        return lax.ppermute(sides, "azim", [(0, 1), (1, 0)])
    after = lax.ppermute(sides[0], "azim", [((i + 1) % count, i) for i in range(count)])
    before = lax.ppermute(sides[1], "azim", [(i, (i + 1) % count) for i in range(count)])
    return jnp.stack([after, before])


def sum_steps():
    azim = lax.axis_size("azim")
    count = lax.axis_size("axial") * azim
    steps, step = [], 2 * azim
    while step < count:
        steps.append(step)
        step *= 2
    step = 1
    while step < azim:
        steps.append(step)
        step *= 2
    groups = [steps[k::4] for k in range(4)]
    groups[0] = groups[0] + [azim]
    return groups


def partial_sum(row, steps):
    count = lax.axis_size("axial") * lax.axis_size("azim")
    for step in steps:
        row = row + lax.ppermute(row, ALL, [(i, i ^ step) for i in range(count)])
    return row


def gather_sums(rows):
    return lax.all_to_all(rows, ALL, 0, 0, tiled=True)


def per_device(velocity, diffusivity, coarse_factor):
    shape = diffusivity.shape
    devices = lax.axis_size("axial") * lax.axis_size("azim")
    u = velocity.reshape(3, 8, 64, LANES)
    diff = diffusivity.reshape(8, 64, LANES)
    tables = constant_tables(LANES)
    plane, over, spectrum = tables["plane"], tables["over"], tables["spectrum"]
    grad, div, into, outof = tables["grad"], tables["div"], tables["into"], tables["outof"]
    coarse_size = coarse_factor.shape[1]
    width = -(-(coarse_size + TAIL) // LANES)
    count = 8 * -(-width // 8)

    field, sums, row_shape = (8, 64, LANES), (devices, width * LANES), (8, width * LANES)
    boxes = [(10, 144, LANES), (10, 144, LANES)]
    raw_sends = [(128, LANES), (2, 96, LANES), (128, LANES), (2, 32, LANES)]
    solved_sends = [(144, LANES), (2, 80, LANES), (144, LANES), (2, 48, LANES)]

    far = pl.BlockSpec(memory_space=pltpu.HBM)
    conv, row, *sends = kernel_call(
        conv_kernel,
        [(3,) + field, (count, LANES), (192 + count, LANES), (2, 144, LANES)]
        + [(192 + count, LANES), (2, 48, LANES)],
        *(pltpu.with_memory_space_constraint(x, pltpu.HBM) for x in (u, coarse_factor, plane, grad)),
        in_specs=[far] * 4,
        scratch_shapes=[
            pltpu.VMEM((3,) + field, F32),
            pltpu.VMEM((1, coarse_size), F32),
            pltpu.VMEM(plane.shape, F32),
            pltpu.VMEM(grad.shape, BF16),
            pltpu.SemaphoreType.DMA((4,)),
        ],
    )
    (inverse,) = kernel_call(inverse_kernel, [(10, 112, LANES)], diff, spectrum)

    def exchange(side_kernel, late_rows, sends, extra, extra_shape=None):
        send_out, send_early, send_in, send_late = sends
        inner, outer = axial_swap(send_in, send_out)
        early = azim_swap(send_early)
        shapes = [(2, late_rows, LANES)]
        shapes = shapes if extra_shape is None else shapes + [extra_shape]
        late, *passed = kernel_call(side_kernel, shapes, outer, inner, send_late, extra)
        return [outer, inner, early, azim_swap(late)] + passed

    one = (1, width * LANES)
    groups = sum_steps()
    moved = exchange(conv_side_kernel, 48 + 3 * count, sends, row)
    g, *sends, near, pay = kernel_call(
        divergence_kernel,
        [field] + raw_sends + [(16, width * LANES), one],
        conv, u, *moved, row, plane, over, div,
    )
    solver = (inverse, into, outof)
    operator = (near, diff, plane, grad, div)
    solve_shapes = boxes + [field] + solved_sends + [one]

    *moved, pay = exchange(raw_side_kernel, 48, sends, partial_sum(pay, groups[0]), one)
    pay = partial_sum(pay, groups[1])
    planes_r, solved_r, part, *sends, pay = kernel_call(
        solve_kernel, solve_shapes, g, *moved, pay, *solver
    )
    *moved, pay = exchange(solved_side_kernel, 48, sends, partial_sum(pay, groups[2]), one)
    pay = partial_sum(pay, groups[3])
    z0, raw0, g, *sends, row_r, pay = kernel_call(
        first_apply_kernel,
        [field, field, field] + raw_sends + [row_shape, one],
        part, *moved, *operator, pay, planes_r, solved_r,
    )
    *moved, pay = exchange(raw_side_kernel, 48, sends, partial_sum(pay, groups[0]), one)
    pay = partial_sum(pay, groups[1])
    planes_q, solved_q, part, *sends, pay = kernel_call(
        solve_kernel, solve_shapes, g, *moved, pay, *solver
    )
    *moved, pay = exchange(solved_side_kernel, 48, sends, partial_sum(pay, groups[2]), one)
    first_sums = partial_sum(pay, groups[3])
    y, z1, raw1, g, *sends = kernel_call(
        second_apply_kernel,
        [field, field, field, field] + raw_sends,
        part, *moved, *operator, first_sums, row_r, z0,
    )
    planes_r, solved_r, pay = kernel_call(
        first_dots_kernel,
        boxes + [one],
        first_sums, row_r, near, planes_r, planes_q, solved_r, solved_q, z1, raw1, raw0,
    )
    *moved, pay = exchange(raw_side_kernel, 48, sends, pay, one)
    planes_w, solved_w, part, *sends, pay = kernel_call(
        solve_kernel, solve_shapes, g, *moved, pay, *solver
    )
    (pay,) = kernel_call(
        second_dots_kernel, [one], pay, planes_r, planes_q, planes_w, solved_r, solved_q, solved_w
    )
    gathered = gather_sums(jnp.broadcast_to(pay, sums))
    *moved, _ = exchange(solved_side_kernel, 48, sends, pay, one)
    pressure, residual, direction = kernel_call(
        last_kernel,
        [field, field, field],
        part, *moved, near, gathered, first_sums, row_r,
        y, z0, z1, planes_r, planes_q, planes_w,
    )
    return pressure.reshape(shape), residual.reshape(shape), direction.reshape(shape)


def solution(mesh):
    split = P(None, None, None, "axial", "azim", None)
    in_specs = (P(None, None, None, None, "axial", "azim", None), split, P(ALL, None))
    return jax.shard_map(
        per_device, mesh=mesh, in_specs=in_specs, out_specs=(split, split, split), check_vma=False
    )
```

```python
import math

import jax
import jax.numpy as jnp
import numpy as np
from jax import lax
from jax.experimental import pallas as pl
from jax.experimental.pallas import tpu as pltpu
from jax.sharding import PartitionSpec as P

ALL = ("axial", "azim")
time_increment = 0.02
mass_shift = 0.05
VMEM_GRANT = 20 << 20
TAIL = 16
SUM_ROWS = 32
gll_points = [
    -1.0,
    -0.8717401485096066,
    -0.5917001814331423,
    -0.20929921790247888,
    0.20929921790247888,
    0.5917001814331423,
    0.8717401485096066,
    1.0,
]


def legendre_value(order, point):
    before = 1.0
    current = point
    for step_idx in range(1, order):
        after = ((2 * step_idx + 1) * point * current - step_idx * before) / (step_idx + 1)
        before = current
        current = after
    return current


def jacobi_eigen(matrix):
    size_n = len(matrix)
    work = [list(row) for row in matrix]
    vectors = [
        [1.0 if row_idx == col_idx else 0.0 for col_idx in range(size_n)]
        for row_idx in range(size_n)
    ]
    for sweep_idx in range(15):
        for row_idx in range(size_n):
            for col_idx in range(row_idx + 1, size_n):
                off_value = work[row_idx][col_idx]
                if off_value != 0.0:
                    theta = (work[col_idx][col_idx] - work[row_idx][row_idx]) / (2.0 * off_value)
                    root_val = math.sqrt(theta * theta + 1.0)
                    tangent = 1.0 / (theta + root_val) if theta >= 0.0 else 1.0 / (theta - root_val)
                    cosine = 1.0 / math.sqrt(tangent * tangent + 1.0)
                    sine = tangent * cosine
                    for other in range(size_n):
                        left_val = work[other][row_idx]
                        right_val = work[other][col_idx]
                        work[other][row_idx] = cosine * left_val - sine * right_val
                        work[other][col_idx] = sine * left_val + cosine * right_val
                    for other in range(size_n):
                        left_val = work[row_idx][other]
                        right_val = work[col_idx][other]
                        work[row_idx][other] = cosine * left_val - sine * right_val
                        work[col_idx][other] = sine * left_val + cosine * right_val
                    for other in range(size_n):
                        left_val = vectors[other][row_idx]
                        right_val = vectors[other][col_idx]
                        vectors[other][row_idx] = cosine * left_val - sine * right_val
                        vectors[other][col_idx] = sine * left_val + cosine * right_val
    return ([work[row_idx][row_idx] for row_idx in range(size_n)], vectors)


def gll_tables():
    degree = 7
    points = degree + 1
    legendre_at = [legendre_value(degree, node_val) for node_val in gll_points]
    weights = [2.0 / (degree * (degree + 1) * value * value) for value in legendre_at]
    derivative = [[0.0] * points for row_idx in range(points)]
    for row_idx in range(points):
        for col_idx in range(points):
            if row_idx != col_idx:
                derivative[row_idx][col_idx] = legendre_at[row_idx] / (
                    legendre_at[col_idx] * (gll_points[row_idx] - gll_points[col_idx])
                )
    derivative[0][0] = -degree * (degree + 1) / 4.0
    derivative[degree][degree] = degree * (degree + 1) / 4.0
    stiffness = [
        [
            sum(
                (
                    derivative[mid_idx][row_idx] * weights[mid_idx] * derivative[mid_idx][col_idx]
                    for mid_idx in range(points)
                )
            )
            for col_idx in range(points)
        ]
        for row_idx in range(points)
    ]
    line_len = 3 * degree + 1
    big_stiff = [[0.0] * line_len for row_idx in range(line_len)]
    big_mass = [0.0] * line_len
    for element in range(3):
        offset = element * degree
        for row_idx in range(points):
            big_mass[offset + row_idx] += weights[row_idx]
            for col_idx in range(points):
                big_stiff[offset + row_idx][offset + col_idx] += stiffness[row_idx][col_idx]
    start_node = degree - 1
    box_len = degree + 3
    scaling = [1.0 / math.sqrt(big_mass[start_node + row_idx]) for row_idx in range(box_len)]
    symmetric = [
        [
            scaling[row_idx]
            * big_stiff[start_node + row_idx][start_node + col_idx]
            * scaling[col_idx]
            for col_idx in range(box_len)
        ]
        for row_idx in range(box_len)
    ]
    eigval, eigvec = jacobi_eigen(symmetric)
    fdm_basis = [
        [scaling[row_idx] * eigvec[row_idx][col_idx] for col_idx in range(box_len)]
        for row_idx in range(box_len)
    ]
    return (weights, derivative, fdm_basis, eigval)

WEIGHTS, DERIV, BASIS, EIGVAL = (np.asarray(t, np.float64) for t in gll_tables())


def f32(table):
    return jnp.asarray(table, jnp.float32)


F32 = jnp.float32
BF16 = jnp.bfloat16
LANES = 128
INTERPRET = False


def split_terms(table, depth):
    padded = np.zeros((table.shape[0], depth))
    padded[:, : table.shape[1]] = table
    high = padded.astype(jnp.bfloat16)
    low = (padded - high.astype(np.float64)).astype(jnp.bfloat16)
    return jnp.asarray(np.concatenate([high, high, low], axis=1))


def box_tables():
    pairs = [(b + 1, c + 1) for b in range(8) for c in range(8)]
    pairs += [(b + 1, {6: 0, 1: 9}.get(c)) for b in range(8) for c in range(8)]
    pairs += [(0, c + 1) for c in range(8)] + [(9, c + 1) for c in range(8)]
    table = np.zeros((144, 112))
    for row, (b, c) in enumerate(pairs):
        if c is not None:
            table[row, :100] = np.outer(BASIS[b], BASIS[c]).reshape(100)
    sums = np.ones(112)
    sums[:100] = (EIGVAL[:, None] + EIGVAL[None, :]).reshape(100)
    return table, sums


EYE = np.eye(8)
GRAD = np.concatenate([np.kron(DERIV, EYE), np.kron(EYE, DERIV)])
BOX_ROWS, SPECTRUM = box_tables()
EVEN = [bool(abs(BASIS[0, i] - BASIS[9, i]) < abs(BASIS[0, i] + BASIS[9, i])) for i in range(10)]


def constant_tables(radial):
    plane = (WEIGHTS[:, None] * WEIGHTS[None, :]).reshape(64, 1)
    mult_r = np.ones((8, radial))
    mult_r[0, 1:] = 2.0
    mult_r[7, :-1] = 2.0
    ends = np.array([2.0, 1, 1, 1, 1, 1, 1, 2.0])
    mult = (ends[:, None, None] * mult_r[None]).reshape(64, radial)
    return dict(
        plane=f32(np.broadcast_to(plane, (64, radial))),
        over=f32(1.0 / mult),
        spectrum=f32(np.broadcast_to(SPECTRUM[:, None], (112, radial))),
        grad=split_terms(GRAD, 64),
        div=split_terms(GRAD.T, 128),
        into=split_terms(BOX_ROWS.T, 144),
        outof=split_terms(BOX_ROWS, 112),
    )


def product(table_ref, values):
    high = values.astype(BF16)
    low = (values - high.astype(F32)).astype(BF16)
    return jnp.dot(
        table_ref[...], jnp.concatenate([high, low, high], axis=0), preferred_element_type=F32
    )


def combine(coefs, terms):
    total = None
    for coef, term in zip(coefs, terms):
        scaled = float(coef) * term
        total = scaled if total is None else total + scaled
    return total


def skew_apply(matrix, parts):
    plus = [parts[b] + parts[7 - b] for b in range(4)]
    minus = [parts[b] - parts[7 - b] for b in range(4)]
    result = [None] * 8
    for a in range(4):
        even = combine([0.5 * (matrix[a, b] + matrix[a, 7 - b]) for b in range(4)], plus)
        odd = combine([0.5 * (matrix[a, b] - matrix[a, 7 - b]) for b in range(4)], minus)
        result[a] = even + odd
        result[7 - a] = odd - even
    return result


def to_spectral(parts):
    plus = [parts[a] + parts[9 - a] for a in range(5)]
    minus = [parts[a] - parts[9 - a] for a in range(5)]
    return [combine(BASIS[:5, i], plus if EVEN[i] else minus) for i in range(10)]


def from_spectral(parts):
    evens = [i for i in range(10) if EVEN[i]]
    odds = [i for i in range(10) if not EVEN[i]]
    result = [None] * 10
    for a in range(5):
        even = combine(BASIS[a, evens], [parts[i] for i in evens])
        odd = combine(BASIS[a, odds], [parts[i] for i in odds])
        result[a] = even + odd
        result[9 - a] = even - odd
    return result


def masks():
    layer = lax.broadcasted_iota(jnp.int32, (8, LANES), 0)
    elem = lax.broadcasted_iota(jnp.int32, (8, LANES), 1)
    return layer, elem > 0, elem < LANES - 1


def spread(values, first, last):
    layer, has_before, has_after = masks()
    cubes = values.reshape(values.shape[0] // 8, 8, LANES)
    before = pltpu.roll(cubes, 1, axis=2)
    after = pltpu.roll(cubes, LANES - 1, axis=2)
    before_mask = ((layer == first) & has_before)[None]
    after_mask = ((layer == last) & has_after)[None]
    result = jnp.where(before_mask, before, jnp.where(after_mask, after, 0.0))
    return result.reshape(values.shape)


def radial_sum(values):
    layer, has_before, has_after = masks()
    cubes = values.reshape(values.shape[0] // 8, 8, LANES)
    up = pltpu.roll(cubes, 1, axis=1)
    down = pltpu.roll(cubes, 7, axis=1)
    ends = jnp.where((layer == 0)[None], up, down)
    before = pltpu.roll(ends, 1, axis=2)
    after = pltpu.roll(ends, LANES - 1, axis=2)
    before_mask = ((layer == 0) & has_before)[None]
    after_mask = ((layer == 7) & has_after)[None]
    ends = jnp.where(before_mask, before, jnp.where(after_mask, after, 0.0))
    return (cubes + ends).reshape(values.shape)


def total(values):
    return jnp.sum(values, axis=(0, 1), keepdims=True)


def add_rows(block, extra):
    pieces = []
    for b in range(8):
        piece = block[8 * b : 8 * b + 8]
        pieces.append(piece + extra[b] if b in extra else piece)
    return jnp.concatenate(pieces, axis=0)


def is_even():
    return lax.axis_index("axial") % 2 == 0


def send_axial(inner_ref, outer_ref, low, high):
    even = is_even()
    row = 0
    for low_piece, high_piece in zip(low, high):
        size = low_piece.shape[0]
        inner_ref[row : row + size] = jnp.where(even, high_piece, low_piece)
        outer_ref[row : row + size] = jnp.where(even, low_piece, high_piece)
        row += size


def got_axial(inner_ref, outer_ref):
    even = is_even()

    def before(start, size):
        return jnp.where(even, outer_ref[start : start + size], inner_ref[start : start + size])

    def after(start, size):
        return jnp.where(even, inner_ref[start : start + size], outer_ref[start : start + size])

    return before, after


def conv_kernel(
    u_hbm, row_hbm, plane_hbm, grad_hbm,
    conv_ref, row_ref, out_ref, early_ref, in_ref, late_ref,
    u_ref, small_ref, plane_ref, grad_ref, sems,
):
    copies = [
        pltpu.make_async_copy(source, target, sems.at[k])
        for k, (source, target) in enumerate(
            ((u_hbm, u_ref), (plane_hbm, plane_ref), (grad_hbm, grad_ref), (row_hbm, small_ref))
        )
    ]
    for copy in copies:
        copy.start()
    row_ref[...] = jnp.zeros(row_ref.shape, F32)
    for copy in copies:
        copy.wait()
    size = small_ref.shape[1]
    for k in range(-(-size // LANES)):
        stop = min(LANES, size - LANES * k)
        row_ref[k : k + 1, :stop] = small_ref[:, LANES * k : LANES * k + stop]
    plane = plane_ref[...]
    fields = [[u_ref[d, a] for a in range(8)] for d in range(3)]
    low, high = [], []
    for comp in range(3):
        parts = fields[comp]
        flat = product(grad_ref, jnp.concatenate(parts, axis=1))
        along_a = skew_apply(DERIV, parts)
        for a in range(8):
            cols = slice(LANES * a, LANES * a + LANES)
            value = (
                fields[0][a] * along_a[a]
                + fields[1][a] * flat[:64, cols]
                + fields[2][a] * flat[64:, cols]
            )
            value = radial_sum(float(WEIGHTS[a]) * plane * value)
            conv_ref[comp, a] = value
            for side, rows in enumerate((value[:8], value[56:])):
                if a in (0, 7):
                    start = 16 * comp + (8 if a else 0)
                    late_ref[side, start : start + 8] = rows
                else:
                    start = 48 * comp + 8 * (a - 1)
                    early_ref[side, start : start + 8] = rows
            if a == 0:
                low.append(value)
            if a == 7:
                high.append(value)
    row = row_ref[...]
    send_axial(in_ref, out_ref, low + [row], high + [row])


def inverse_kernel(diff_ref, spectrum_ref, inverse_ref):
    mean = diff_ref[0]
    for a in range(1, 8):
        mean = mean + diff_ref[a]
    kbar = jnp.sum(mean, axis=0, keepdims=True) * (1.0 / 512.0)
    plane_spectrum = kbar * spectrum_ref[...] + mass_shift
    for i in range(10):
        inverse_ref[i] = 1.0 / (plane_spectrum + float(EIGVAL[i]) * kbar)


def conv_side_kernel(out_ref, in_ref, late_ref, row_ref, send_ref):
    before, after = got_axial(in_ref, out_ref)
    count = row_ref.shape[0]
    for side, b in ((0, 0), (1, 7)):
        for comp in range(3):
            first = slice(16 * comp, 16 * comp + 8)
            last = slice(16 * comp + 8, 16 * comp + 16)
            row = 64 * comp + 8 * b
            send_ref[side, first] = late_ref[side, first] + before(row, 8)
            send_ref[side, last] = late_ref[side, last] + after(row, 8)
        for place, rows in enumerate((before(192, count), row_ref[...], after(192, count))):
            start = 48 + place * count
            send_ref[side, start : start + count] = rows


def coarse_share(raw, near_ref):
    middle = raw[1]
    for a in range(2, 7):
        middle = middle + raw[a]
    per_axial = (0.5 * raw[0], middle + 0.5 * (raw[0] + raw[7]), 0.5 * raw[7])
    rows = []
    for part in per_axial:
        inner = part[8:16]
        for b in range(2, 7):
            inner = inner + part[8 * b : 8 * b + 8]
        ends = (part[:8], part[56:])
        for piece in (0.5 * ends[0], inner + 0.5 * (ends[0] + ends[1]), 0.5 * ends[1]):
            rows.append(jnp.sum(piece, axis=0, keepdims=True))
    rows = jnp.concatenate(rows + [jnp.zeros((7, LANES), F32)], axis=0)
    shares = jnp.sum(rows, axis=1, keepdims=True)
    return jnp.sum(shares * near_ref[...], axis=0, keepdims=True)


def send_sums(pay_ref, row, scalars):
    width = pay_ref.shape[1]
    place = lax.broadcasted_iota(jnp.int32, (1, width), 1)
    for k, value in enumerate(scalars):
        row = jnp.where(place == width - 1 - k, value, row)
    pay_ref[...] = jnp.broadcast_to(row, pay_ref.shape)


def got_sums(ref, scalars):
    row = jnp.sum(ref[...], axis=0, keepdims=True)
    width = row.shape[1]
    place = lax.broadcasted_iota(jnp.int32, (1, width), 1)
    values = [
        jnp.sum(jnp.where(place == width - 1 - k, row, 0.0), axis=1, keepdims=True)
        for k in range(scalars)
    ]
    return jnp.where(place >= width - TAIL, 0.0, row), values


def send_raw(raw, g_ref, in_ref, out_ref, early_ref, late_ref):
    parts = [radial_sum(raw[a]) for a in range(8)]
    for a in range(8):
        g_ref[a] = parts[a]
    send_axial(in_ref, out_ref, [parts[0], parts[1]], [parts[7], parts[6]])
    for side, (edge, inner) in enumerate(((0, 1), (7, 6))):
        edges = [part[8 * edge : 8 * edge + 8] for part in parts]
        inners = [part[8 * inner : 8 * inner + 8] for part in parts]
        for a in range(1, 7):
            early_ref[side, 8 * a - 8 : 8 * a] = edges[a]
            early_ref[side, 40 + 8 * a : 48 + 8 * a] = inners[a]
        late_ref[side, :8] = edges[0]
        late_ref[side, 8:16] = edges[7]
        late_ref[side, 16:24] = inners[0]
        late_ref[side, 24:32] = inners[7]


def raw_side_kernel(out_ref, in_ref, late_ref, row_ref, send_ref, pass_ref):
    pass_ref[...] = row_ref[...]
    before, after = got_axial(in_ref, out_ref)
    for side, (edge, inner) in enumerate(((0, 1), (7, 6))):
        send_ref[side, :8] = before(64 + 8 * edge, 8)
        send_ref[side, 8:16] = late_ref[side, :8] + before(8 * edge, 8)
        send_ref[side, 16:24] = late_ref[side, 8:16] + after(8 * edge, 8)
        send_ref[side, 24:32] = after(64 + 8 * edge, 8)
        send_ref[side, 32:40] = late_ref[side, 16:24] + before(8 * inner, 8)
        send_ref[side, 40:48] = late_ref[side, 24:32] + after(8 * inner, 8)


def divergence_kernel(
    conv_ref, u_ref, out_ref, in_ref, early_ref, late_ref, row_ref, plane_ref, over_ref, div_ref,
    g_ref, send_out_ref, send_early_ref, send_in_ref, send_late_ref, near_ref, pay_ref,
):
    before, after = got_axial(in_ref, out_ref)
    plane, over = plane_ref[...], over_ref[...]

    def side_rows(side, comp, a):
        if a in (0, 7):
            start = 16 * comp + (8 if a else 0)
            return late_ref[side, start : start + 8]
        start = 48 * comp + 8 * (a - 1)
        return early_ref[side, start : start + 8]

    moved = []
    for comp in range(3):
        parts = []
        for a in range(8):
            value = conv_ref[comp, a]
            if a == 0:
                value = value + before(64 * comp, 64)
            if a == 7:
                value = value + after(64 * comp, 64)
            value = add_rows(value, {0: side_rows(1, comp, a), 7: side_rows(0, comp, a)})
            scale = time_increment * (0.5 if a in (0, 7) else 1.0)
            parts.append(float(WEIGHTS[a]) * plane * u_ref[comp, a] - scale * over * value)
        moved.append(parts)
    flat = product(
        div_ref,
        jnp.concatenate([jnp.concatenate(moved[1], axis=1), jnp.concatenate(moved[2], axis=1)], axis=0),
    )
    along_a = skew_apply(DERIV.T, moved[0])
    raw = [along_a[a] + flat[:, LANES * a : LANES * a + LANES] for a in range(8)]
    send_raw(raw, g_ref, send_in_ref, send_out_ref, send_early_ref, send_late_ref)
    count = row_ref.shape[0]
    width = near_ref.shape[1] // LANES
    near_ref[...] = jnp.zeros(near_ref.shape, F32)
    for i in range(3):
        start = 48 + i * count
        middle = (before(192, count), row_ref[...], after(192, count))[i]
        sides = (late_ref[1, start : start + count], middle, late_ref[0, start : start + count])
        for j, rows in enumerate(sides):
            for k in range(width):
                near_ref[3 * i + j : 3 * i + j + 1, LANES * k : LANES * k + LANES] = rows[k : k + 1]
    send_sums(pay_ref, coarse_share(raw, near_ref), [])


def got_planes(g_ref, in_ref, out_ref, early_ref, late_ref):
    before, after = got_axial(in_ref, out_ref)

    def edge_rows(side, e):
        if e in (0, 1, 8, 9):
            start = 8 * (0, 1, 8, 9).index(e)
            return late_ref[side, start : start + 8]
        return early_ref[side, 8 * e - 16 : 8 * e - 8]

    def inner_rows(side, a):
        if a in (0, 7):
            start = 40 if a else 32
            return late_ref[side, start : start + 8]
        return early_ref[side, 40 + 8 * a : 48 + 8 * a]

    zero = jnp.zeros((80, LANES), F32)
    planes = []
    for e in range(10):
        if e == 0:
            value = before(64, 64)
        elif e == 9:
            value = after(64, 64)
        else:
            value = g_ref[e - 1]
        if e == 1:
            value = value + before(0, 64)
        if e == 8:
            value = value + after(0, 64)
        value = add_rows(value, {0: edge_rows(1, e), 7: edge_rows(0, e)})
        if e in (0, 9):
            rows = [value, zero]
        else:
            rows = [value, spread(value, 6, 1), inner_rows(1, e - 1), inner_rows(0, e - 1)]
        planes.append(jnp.concatenate(rows, axis=0))
    return planes


def solve_kernel(
    g_ref, out_ref, in_ref, early_ref, late_ref, row_ref,
    inverse_ref, into_ref, outof_ref,
    planes_ref, solved_ref, part_ref, send_out_ref, send_early_ref, send_in_ref, send_late_ref,
    pass_ref,
):
    pass_ref[...] = jnp.broadcast_to(row_ref[...], pass_ref.shape)
    planes = got_planes(g_ref, in_ref, out_ref, early_ref, late_ref)
    for e in range(10):
        planes_ref[e] = planes[e]
    flat = product(into_ref, jnp.concatenate(planes, axis=1))
    parts = to_spectral([flat[:, LANES * e : LANES * e + LANES] for e in range(10)])
    parts = [parts[i] * inverse_ref[i] for i in range(10)]
    parts = from_spectral(parts)
    flat = product(outof_ref, jnp.concatenate(parts, axis=1))
    solved = [flat[:, LANES * e : LANES * e + LANES] for e in range(10)]
    for e in range(10):
        solved_ref[e] = solved[e]
    outer_a = [radial_sum(solved[0][:64]), radial_sum(solved[9][:64])]
    edges = []
    for a in range(8):
        rows = solved[a + 1]
        value = radial_sum(rows[:64] + spread(rows[64:128], 1, 6))
        outer_b = radial_sum(rows[128:144])
        part_ref[a] = value
        for side in range(2):
            edge = value[56 * side : 56 * side + 8]
            face = outer_b[8 * side : 8 * side + 8]
            if a in (0, 1, 6, 7):
                start = 8 * (0, 1, 6, 7).index(a)
                send_late_ref[side, start : start + 8] = edge
            else:
                send_early_ref[side, 8 * a - 16 : 8 * a - 8] = edge
            if a in (0, 7):
                start = 40 if a else 32
                send_late_ref[side, start : start + 8] = face
            else:
                send_early_ref[side, 24 + 8 * a : 32 + 8 * a] = face
        if a in (0, 7):
            edges.append((value, outer_b))
    send_axial(
        send_in_ref,
        send_out_ref,
        [edges[0][0], outer_a[0], edges[0][1]],
        [edges[1][0], outer_a[1], edges[1][1]],
    )


def solved_side_kernel(out_ref, in_ref, late_ref, row_ref, send_ref, pass_ref):
    pass_ref[...] = row_ref[...]
    before, after = got_axial(in_ref, out_ref)
    for side, b in ((0, 0), (1, 7)):
        row = 8 * b
        send_ref[side, :8] = late_ref[side, :8] + before(row, 8)
        send_ref[side, 8:16] = late_ref[side, 8:16] + before(64 + row, 8)
        send_ref[side, 16:24] = late_ref[side, 16:24] + after(64 + row, 8)
        send_ref[side, 24:32] = late_ref[side, 24:32] + after(row, 8)
        send_ref[side, 32:40] = late_ref[side, 32:40] + before(128 + 8 * side, 8)
        send_ref[side, 40:48] = late_ref[side, 40:48] + after(128 + 8 * side, 8)


def got_solved(part_ref, in_ref, out_ref, early_ref, late_ref):
    before, after = got_axial(in_ref, out_ref)
    extra = {0: (before, 0), 1: (before, 64), 6: (after, 64), 7: (after, 0)}

    def edge_rows(side, a):
        if a in extra:
            start = 8 * (0, 1, 6, 7).index(a)
            return late_ref[side, start : start + 8]
        return early_ref[side, 8 * a - 16 : 8 * a - 8]

    def face_rows(side, a):
        if a in (0, 7):
            start = 40 if a else 32
            return late_ref[side, start : start + 8]
        return early_ref[side, 24 + 8 * a : 32 + 8 * a]

    result = []
    for a in range(8):
        value = part_ref[a]
        if a in extra:
            side, start = extra[a]
            value = value + side(start, 64)
        result.append(
            add_rows(
                value,
                {0: edge_rows(1, a), 1: face_rows(1, a), 6: face_rows(0, a), 7: edge_rows(0, a)},
            )
        )
    return result


def add_coarse(parts, row, near_ref):
    values = jnp.sum(near_ref[...] * row, axis=1, keepdims=True)
    own = [[values[3 * i + j : 3 * i + j + 1] for j in range(3)] for i in range(3)]
    fields = []
    for i in range(3):
        ends = [0.5 * (own[i][1] + own[i][j]) for j in (0, 2)]
        rows = [jnp.broadcast_to(value, (8, LANES)) for value in (ends[0], own[i][1], ends[1])]
        fields.append(jnp.concatenate([rows[0]] + [rows[1]] * 6 + [rows[2]], axis=0))
    first, last = 0.5 * (fields[0] + fields[1]), 0.5 * (fields[1] + fields[2])
    return [
        parts[a] + (first if a == 0 else last if a == 7 else fields[1]) for a in range(8)
    ]


def apply_operator(values, diff_ref, plane_ref, grad_ref, div_ref):
    plane = plane_ref[...]
    coef = [float(WEIGHTS[a]) * plane * diff_ref[a] for a in range(8)]
    flat = product(grad_ref, jnp.concatenate(values, axis=1))
    along_a = skew_apply(DERIV, values)
    flux = jnp.concatenate(
        [
            jnp.concatenate([coef[a], coef[a]], axis=0) * flat[:, LANES * a : LANES * a + LANES]
            for a in range(8)
        ],
        axis=1,
    )
    flat = product(div_ref, flux)
    along_a = skew_apply(DERIV.T, [coef[a] * along_a[a] for a in range(8)])
    return [
        along_a[a]
        + flat[:, LANES * a : LANES * a + LANES]
        + (mass_shift * float(WEIGHTS[a])) * plane * values[a]
        for a in range(8)
    ]


def dot_parts(first, second):
    result = first[0] * second[0]
    for a in range(1, 8):
        result = result + first[a] * second[a]
    return total(result)


def norm(row):
    return jnp.sum(row * row, axis=1, keepdims=True)


def dot_planes(first, second):
    result = None
    for e in range(10):
        stop = 64 if e in (0, 9) else 144
        term = first[e][:stop] * second[e][:stop]
        term = jnp.sum(term.reshape(stop // 8, 8, LANES), axis=0)
        result = term if result is None else result + term
    return total(result)


def first_apply_kernel(
    part_ref, out_ref, in_ref, early_ref, late_ref, near_ref, diff_ref, plane_ref, grad_ref, div_ref,
    sums_ref, planes_ref, solved_ref,
    z_ref, raw_ref, g_ref, send_out_ref, send_early_ref, send_in_ref, send_late_ref, row_ref, pay_ref,
):
    row, _ = got_sums(sums_ref, 0)
    values = got_solved(part_ref, in_ref, out_ref, early_ref, late_ref)
    values = add_coarse(values, row, near_ref)
    raw = apply_operator(values, diff_ref, plane_ref, grad_ref, div_ref)
    send_raw(raw, g_ref, send_in_ref, send_out_ref, send_early_ref, send_late_ref)
    for a in range(8):
        z_ref[a] = values[a]
        raw_ref[a] = raw[a]
    row_ref[0:1] = row
    scalars = [dot_planes(planes_ref, solved_ref), dot_parts(values, raw)]
    send_sums(pay_ref, coarse_share(raw, near_ref), scalars)


def first_step(sums_ref, row_ref):
    row_q, (local_rz, curv) = got_sums(sums_ref, 2)
    row_r = row_ref[0:1]
    rz = local_rz + norm(row_r)
    return row_r, row_q, rz, curv, rz / curv


def second_apply_kernel(
    part_ref, out_ref, in_ref, early_ref, late_ref, near_ref, diff_ref, plane_ref, grad_ref, div_ref,
    sums_ref, row_ref, z0_ref,
    y_ref, z_ref, raw_ref, g_ref, send_out_ref, send_early_ref, send_in_ref, send_late_ref,
):
    _, row_q, _, _, alpha = first_step(sums_ref, row_ref)
    change = got_solved(part_ref, in_ref, out_ref, early_ref, late_ref)
    change = add_coarse(change, row_q, near_ref)
    values = [z0_ref[a] - alpha * change[a] for a in range(8)]
    raw = apply_operator(values, diff_ref, plane_ref, grad_ref, div_ref)
    send_raw(raw, g_ref, send_in_ref, send_out_ref, send_early_ref, send_late_ref)
    for a in range(8):
        y_ref[a] = change[a]
        z_ref[a] = values[a]
        raw_ref[a] = raw[a]


def first_dots_kernel(
    sums_ref, row_ref, near_ref, planes_r_ref, planes_q_ref, solved_r_ref, solved_q_ref,
    z_ref, raw_ref, old_raw_ref,
    planes_ref, solved_ref, pay_ref,
):
    alpha = first_step(sums_ref, row_ref)[4]
    planes, solved = [], []
    for e in range(10):
        planes.append(planes_r_ref[e] - alpha * planes_q_ref[e])
        solved.append(solved_r_ref[e] - alpha * solved_q_ref[e])
        planes_ref[e] = planes[e]
        solved_ref[e] = solved[e]
    values = [z_ref[a] for a in range(8)]
    raw = [raw_ref[a] for a in range(8)]
    scalars = [
        dot_planes(planes, solved),
        dot_planes(planes, solved_q_ref),
        dot_planes(planes_q_ref, solved),
        dot_planes(planes_q_ref, solved_q_ref),
        dot_parts(values, raw),
        dot_parts(values, [old_raw_ref[a] for a in range(8)]),
    ]
    send_sums(pay_ref, coarse_share(raw, near_ref), scalars)


def second_dots_kernel(
    row_ref, planes_r_ref, planes_q_ref, planes_w_ref, solved_r_ref, solved_q_ref, solved_w_ref,
    pay_ref,
):
    scalars = [
        dot_planes(planes_r_ref, solved_w_ref),
        dot_planes(planes_q_ref, solved_w_ref),
        dot_planes(planes_w_ref, solved_r_ref),
        dot_planes(planes_w_ref, solved_q_ref),
        dot_planes(planes_w_ref, solved_w_ref),
    ]
    row = row_ref[...]
    width = row.shape[1]
    place = lax.broadcasted_iota(jnp.int32, (1, width), 1)
    for k, value in enumerate(scalars):
        row = jnp.where(place == width - 7 - k, value, row)
    pay_ref[...] = jnp.broadcast_to(row, pay_ref.shape)


def last_kernel(
    part_ref, out_ref, in_ref, early_ref, late_ref, near_ref, sums_ref, old_sums_ref, row_ref,
    y_ref, z0_ref, z1_ref, planes_r_ref, planes_q_ref, planes_w_ref,
    pressure_ref, residual_ref, direction_ref,
):
    row_r, row_q, rz0, curv0, alpha0 = first_step(old_sums_ref, row_ref)
    row_w, scalars = got_sums(sums_ref, 11)
    rr, rq, qr, qq, first_curv, cross, rw, qw, wr, wq, ww = scalars
    row_r = row_r - alpha0 * row_q
    rz1 = rr + norm(row_r)
    beta0 = rz1 / rz0
    curv1 = first_curv + beta0 * (2.0 * cross + beta0 * curv0)
    alpha1 = rz1 / curv1
    row = row_w + beta0 * row_q
    row_r = row_r - alpha1 * row
    step = -alpha1 * beta0
    rz2 = (
        rr
        - alpha1 * (rw + wr)
        + step * (rq + qr)
        + alpha1 * alpha1 * ww
        - alpha1 * step * (wq + qw)
        + step * step * qq
        + norm(row_r)
    )
    beta1 = rz2 / rz1
    change = got_solved(part_ref, in_ref, out_ref, early_ref, late_ref)
    change = add_coarse(change, row_w, near_ref)
    for a in range(8):
        first = z0_ref[a]
        second = z1_ref[a] + beta0 * first
        image = planes_w_ref[a + 1, :64] + beta0 * planes_q_ref[a + 1, :64]
        residual_ref[a] = planes_r_ref[a + 1, :64] - alpha1 * image
        pressure_ref[a] = alpha0 * first + alpha1 * second
        direction_ref[a] = (
            z1_ref[a] - alpha1 * (change[a] + beta0 * y_ref[a]) + beta1 * second
        )


def kernel_call(kernel, out_shapes, *args, **options):
    outs = [jax.ShapeDtypeStruct(shape, F32) for shape in out_shapes]
    return pl.pallas_call(
        kernel,
        out_shape=outs,
        compiler_params=pltpu.CompilerParams(vmem_limit_bytes=VMEM_GRANT),
        interpret=INTERPRET,
        **options,
    )(*args)


def axial_swap(inner_rows, outer_rows):
    count = lax.axis_size("axial")
    inner = [(i, i ^ 1) for i in range(count)]
    outer = [((2 * i + 1) % count, (2 * i + 2) % count) for i in range(count // 2)]
    outer = outer + [(b, a) for a, b in outer]
    from_outer = lax.ppermute(outer_rows, "axial", outer)
    from_inner = lax.ppermute(inner_rows, "axial", inner)
    return from_inner, from_outer


def azim_swap(sides):
    count = lax.axis_size("azim")
    if count == 2:
        return lax.ppermute(sides, "azim", [(0, 1), (1, 0)])
    after = lax.ppermute(sides[0], "azim", [((i + 1) % count, i) for i in range(count)])
    before = lax.ppermute(sides[1], "azim", [(i, (i + 1) % count) for i in range(count)])
    return jnp.stack([after, before])


def sum_steps():
    azim = lax.axis_size("azim")
    count = lax.axis_size("axial") * azim
    steps, step = [], 2 * azim
    while step < count:
        steps.append(step)
        step *= 2
    step = 1
    while step < azim:
        steps.append(step)
        step *= 2
    groups = [steps[k::4] for k in range(4)]
    groups[0] = groups[0] + [azim]
    return groups


def partial_sum(row, steps):
    count = lax.axis_size("axial") * lax.axis_size("azim")
    for step in steps:
        row = row[:1] + lax.ppermute(row, ALL, [(i, i ^ step) for i in range(count)])[:1]
    return row


def gather_sums(rows):
    return lax.all_to_all(rows, ALL, 0, 0, tiled=True)


def per_device(velocity, diffusivity, coarse_factor):
    shape = diffusivity.shape
    devices = lax.axis_size("axial") * lax.axis_size("azim")
    u = velocity.reshape(3, 8, 64, LANES)
    diff = diffusivity.reshape(8, 64, LANES)
    tables = constant_tables(LANES)
    plane, over, spectrum = tables["plane"], tables["over"], tables["spectrum"]
    grad, div, into, outof = tables["grad"], tables["div"], tables["into"], tables["outof"]
    coarse_size = coarse_factor.shape[1]
    width = -(-(coarse_size + TAIL) // LANES)
    count = 8 * -(-width // 8)

    field, sums, row_shape = (8, 64, LANES), (devices, width * LANES), (8, width * LANES)
    boxes = [(10, 144, LANES), (10, 144, LANES)]
    raw_sends = [(128, LANES), (2, 96, LANES), (128, LANES), (2, 32, LANES)]
    solved_sends = [(144, LANES), (2, 80, LANES), (144, LANES), (2, 48, LANES)]

    far = pl.BlockSpec(memory_space=pltpu.HBM)
    conv, row, *sends = kernel_call(
        conv_kernel,
        [(3,) + field, (count, LANES), (192 + count, LANES), (2, 144, LANES)]
        + [(192 + count, LANES), (2, 48, LANES)],
        *(pltpu.with_memory_space_constraint(x, pltpu.HBM) for x in (u, coarse_factor, plane, grad)),
        in_specs=[far] * 4,
        scratch_shapes=[
            pltpu.VMEM((3,) + field, F32),
            pltpu.VMEM((1, coarse_size), F32),
            pltpu.VMEM(plane.shape, F32),
            pltpu.VMEM(grad.shape, BF16),
            pltpu.SemaphoreType.DMA((4,)),
        ],
    )
    (inverse,) = kernel_call(inverse_kernel, [(10, 112, LANES)], diff, spectrum)

    def exchange(side_kernel, late_rows, sends, extra, extra_shape=None):
        send_out, send_early, send_in, send_late = sends
        inner, outer = axial_swap(send_in, send_out)
        early = azim_swap(send_early)
        shapes = [(2, late_rows, LANES)]
        shapes = shapes if extra_shape is None else shapes + [extra_shape]
        late, *passed = kernel_call(side_kernel, shapes, outer, inner, send_late, extra)
        return [outer, inner, early, azim_swap(late)] + passed

    one, copies = (1, width * LANES), (SUM_ROWS, width * LANES)
    groups = sum_steps()
    moved = exchange(conv_side_kernel, 48 + 3 * count, sends, row)
    g, *sends, near, pay = kernel_call(
        divergence_kernel,
        [field] + raw_sends + [(16, width * LANES), copies],
        conv, u, *moved, row, plane, over, div,
    )
    solver = (inverse, into, outof)
    operator = (near, diff, plane, grad, div)
    solve_shapes = boxes + [field] + solved_sends + [copies]

    *moved, pay = exchange(raw_side_kernel, 48, sends, partial_sum(pay, groups[0]), one)
    pay = partial_sum(pay, groups[1])
    planes_r, solved_r, part, *sends, pay = kernel_call(
        solve_kernel, solve_shapes, g, *moved, pay, *solver
    )
    *moved, pay = exchange(solved_side_kernel, 48, sends, partial_sum(pay, groups[2]), one)
    pay = partial_sum(pay, groups[3])
    z0, raw0, g, *sends, row_r, pay = kernel_call(
        first_apply_kernel,
        [field, field, field] + raw_sends + [row_shape, copies],
        part, *moved, *operator, pay, planes_r, solved_r,
    )
    *moved, pay = exchange(raw_side_kernel, 48, sends, partial_sum(pay, groups[0]), one)
    pay = partial_sum(pay, groups[1])
    planes_q, solved_q, part, *sends, pay = kernel_call(
        solve_kernel, solve_shapes, g, *moved, pay, *solver
    )
    *moved, pay = exchange(solved_side_kernel, 48, sends, partial_sum(pay, groups[2]), one)
    first_sums = partial_sum(pay, groups[3])
    y, z1, raw1, g, *sends = kernel_call(
        second_apply_kernel,
        [field, field, field, field] + raw_sends,
        part, *moved, *operator, first_sums, row_r, z0,
    )
    planes_r, solved_r, pay = kernel_call(
        first_dots_kernel,
        boxes + [one],
        first_sums, row_r, near, planes_r, planes_q, solved_r, solved_q, z1, raw1, raw0,
    )
    *moved, pay = exchange(raw_side_kernel, 48, sends, pay, one)
    planes_w, solved_w, part, *sends, pay = kernel_call(
        solve_kernel, solve_shapes, g, *moved, pay, *solver
    )
    (pay,) = kernel_call(
        second_dots_kernel, [one], pay[:1], planes_r, planes_q, planes_w, solved_r, solved_q, solved_w
    )
    gathered = gather_sums(jnp.broadcast_to(pay, sums))
    *moved, _ = exchange(solved_side_kernel, 48, sends, pay, one)
    pressure, residual, direction = kernel_call(
        last_kernel,
        [field, field, field],
        part, *moved, near, gathered, first_sums, row_r,
        y, z0, z1, planes_r, planes_q, planes_w,
    )
    return pressure.reshape(shape), residual.reshape(shape), direction.reshape(shape)


def solution(mesh):
    split = P(None, None, None, "axial", "azim", None)
    in_specs = (P(None, None, None, None, "axial", "azim", None), split, P(ALL, None))
    return jax.shard_map(
        per_device, mesh=mesh, in_specs=in_specs, out_specs=(split, split, split), check_vma=False
    )
```

```python
import math

import jax
import jax.numpy as jnp
import numpy as np
from jax import lax
from jax.experimental import pallas as pl
from jax.experimental.pallas import tpu as pltpu
from jax.sharding import PartitionSpec as P

ALL = ("axial", "azim")
time_increment = 0.02
mass_shift = 0.05
VMEM_GRANT = 20 << 20
TAIL = 16
SUM_ROWS = 32
gll_points = [
    -1.0,
    -0.8717401485096066,
    -0.5917001814331423,
    -0.20929921790247888,
    0.20929921790247888,
    0.5917001814331423,
    0.8717401485096066,
    1.0,
]


def legendre_value(order, point):
    before = 1.0
    current = point
    for step_idx in range(1, order):
        after = ((2 * step_idx + 1) * point * current - step_idx * before) / (step_idx + 1)
        before = current
        current = after
    return current


def jacobi_eigen(matrix):
    size_n = len(matrix)
    work = [list(row) for row in matrix]
    vectors = [
        [1.0 if row_idx == col_idx else 0.0 for col_idx in range(size_n)]
        for row_idx in range(size_n)
    ]
    for sweep_idx in range(15):
        for row_idx in range(size_n):
            for col_idx in range(row_idx + 1, size_n):
                off_value = work[row_idx][col_idx]
                if off_value != 0.0:
                    theta = (work[col_idx][col_idx] - work[row_idx][row_idx]) / (2.0 * off_value)
                    root_val = math.sqrt(theta * theta + 1.0)
                    tangent = 1.0 / (theta + root_val) if theta >= 0.0 else 1.0 / (theta - root_val)
                    cosine = 1.0 / math.sqrt(tangent * tangent + 1.0)
                    sine = tangent * cosine
                    for other in range(size_n):
                        left_val = work[other][row_idx]
                        right_val = work[other][col_idx]
                        work[other][row_idx] = cosine * left_val - sine * right_val
                        work[other][col_idx] = sine * left_val + cosine * right_val
                    for other in range(size_n):
                        left_val = work[row_idx][other]
                        right_val = work[col_idx][other]
                        work[row_idx][other] = cosine * left_val - sine * right_val
                        work[col_idx][other] = sine * left_val + cosine * right_val
                    for other in range(size_n):
                        left_val = vectors[other][row_idx]
                        right_val = vectors[other][col_idx]
                        vectors[other][row_idx] = cosine * left_val - sine * right_val
                        vectors[other][col_idx] = sine * left_val + cosine * right_val
    return ([work[row_idx][row_idx] for row_idx in range(size_n)], vectors)


def gll_tables():
    degree = 7
    points = degree + 1
    legendre_at = [legendre_value(degree, node_val) for node_val in gll_points]
    weights = [2.0 / (degree * (degree + 1) * value * value) for value in legendre_at]
    derivative = [[0.0] * points for row_idx in range(points)]
    for row_idx in range(points):
        for col_idx in range(points):
            if row_idx != col_idx:
                derivative[row_idx][col_idx] = legendre_at[row_idx] / (
                    legendre_at[col_idx] * (gll_points[row_idx] - gll_points[col_idx])
                )
    derivative[0][0] = -degree * (degree + 1) / 4.0
    derivative[degree][degree] = degree * (degree + 1) / 4.0
    stiffness = [
        [
            sum(
                (
                    derivative[mid_idx][row_idx] * weights[mid_idx] * derivative[mid_idx][col_idx]
                    for mid_idx in range(points)
                )
            )
            for col_idx in range(points)
        ]
        for row_idx in range(points)
    ]
    line_len = 3 * degree + 1
    big_stiff = [[0.0] * line_len for row_idx in range(line_len)]
    big_mass = [0.0] * line_len
    for element in range(3):
        offset = element * degree
        for row_idx in range(points):
            big_mass[offset + row_idx] += weights[row_idx]
            for col_idx in range(points):
                big_stiff[offset + row_idx][offset + col_idx] += stiffness[row_idx][col_idx]
    start_node = degree - 1
    box_len = degree + 3
    scaling = [1.0 / math.sqrt(big_mass[start_node + row_idx]) for row_idx in range(box_len)]
    symmetric = [
        [
            scaling[row_idx]
            * big_stiff[start_node + row_idx][start_node + col_idx]
            * scaling[col_idx]
            for col_idx in range(box_len)
        ]
        for row_idx in range(box_len)
    ]
    eigval, eigvec = jacobi_eigen(symmetric)
    fdm_basis = [
        [scaling[row_idx] * eigvec[row_idx][col_idx] for col_idx in range(box_len)]
        for row_idx in range(box_len)
    ]
    return (weights, derivative, fdm_basis, eigval)

WEIGHTS, DERIV, BASIS, EIGVAL = (np.asarray(t, np.float64) for t in gll_tables())


def f32(table):
    return jnp.asarray(table, jnp.float32)


F32 = jnp.float32
BF16 = jnp.bfloat16
LANES = 128
INTERPRET = False


def split_terms(table, depth):
    padded = np.zeros((table.shape[0], depth))
    padded[:, : table.shape[1]] = table
    high = padded.astype(jnp.bfloat16)
    low = (padded - high.astype(np.float64)).astype(jnp.bfloat16)
    return jnp.asarray(np.concatenate([high, high, low], axis=1))


def box_tables():
    pairs = [(b + 1, c + 1) for b in range(8) for c in range(8)]
    pairs += [(b + 1, {6: 0, 1: 9}.get(c)) for b in range(8) for c in range(8)]
    pairs += [(0, c + 1) for c in range(8)] + [(9, c + 1) for c in range(8)]
    table = np.zeros((144, 112))
    for row, (b, c) in enumerate(pairs):
        if c is not None:
            table[row, :100] = np.outer(BASIS[b], BASIS[c]).reshape(100)
    sums = np.ones(112)
    sums[:100] = (EIGVAL[:, None] + EIGVAL[None, :]).reshape(100)
    return table, sums


EYE = np.eye(8)
GRAD = np.concatenate([np.kron(DERIV, EYE), np.kron(EYE, DERIV)])
BOX_ROWS, SPECTRUM = box_tables()
EVEN = [bool(abs(BASIS[0, i] - BASIS[9, i]) < abs(BASIS[0, i] + BASIS[9, i])) for i in range(10)]


def constant_tables(radial):
    plane = (WEIGHTS[:, None] * WEIGHTS[None, :]).reshape(64, 1)
    mult_r = np.ones((8, radial))
    mult_r[0, 1:] = 2.0
    mult_r[7, :-1] = 2.0
    ends = np.array([2.0, 1, 1, 1, 1, 1, 1, 2.0])
    mult = (ends[:, None, None] * mult_r[None]).reshape(64, radial)
    return dict(
        plane=f32(np.broadcast_to(plane, (64, radial))),
        over=f32(1.0 / mult),
        spectrum=f32(np.broadcast_to(SPECTRUM[:, None], (112, radial))),
        grad=split_terms(GRAD, 64),
        div=split_terms(GRAD.T, 128),
        into=split_terms(BOX_ROWS.T, 144),
        outof=split_terms(BOX_ROWS, 112),
    )


def product(table_ref, values):
    high = values.astype(BF16)
    low = (values - high.astype(F32)).astype(BF16)
    return jnp.dot(
        table_ref[...], jnp.concatenate([high, low, high], axis=0), preferred_element_type=F32
    )


def combine(coefs, terms):
    total = None
    for coef, term in zip(coefs, terms):
        scaled = float(coef) * term
        total = scaled if total is None else total + scaled
    return total


def skew_apply(matrix, parts):
    plus = [parts[b] + parts[7 - b] for b in range(4)]
    minus = [parts[b] - parts[7 - b] for b in range(4)]
    result = [None] * 8
    for a in range(4):
        even = combine([0.5 * (matrix[a, b] + matrix[a, 7 - b]) for b in range(4)], plus)
        odd = combine([0.5 * (matrix[a, b] - matrix[a, 7 - b]) for b in range(4)], minus)
        result[a] = even + odd
        result[7 - a] = odd - even
    return result


def to_spectral(parts):
    plus = [parts[a] + parts[9 - a] for a in range(5)]
    minus = [parts[a] - parts[9 - a] for a in range(5)]
    return [combine(BASIS[:5, i], plus if EVEN[i] else minus) for i in range(10)]


def from_spectral(parts):
    evens = [i for i in range(10) if EVEN[i]]
    odds = [i for i in range(10) if not EVEN[i]]
    result = [None] * 10
    for a in range(5):
        even = combine(BASIS[a, evens], [parts[i] for i in evens])
        odd = combine(BASIS[a, odds], [parts[i] for i in odds])
        result[a] = even + odd
        result[9 - a] = even - odd
    return result


def masks():
    layer = lax.broadcasted_iota(jnp.int32, (8, LANES), 0)
    elem = lax.broadcasted_iota(jnp.int32, (8, LANES), 1)
    return layer, elem > 0, elem < LANES - 1


def spread(values, first, last):
    layer, has_before, has_after = masks()
    cubes = values.reshape(values.shape[0] // 8, 8, LANES)
    before = pltpu.roll(cubes, 1, axis=2)
    after = pltpu.roll(cubes, LANES - 1, axis=2)
    before_mask = ((layer == first) & has_before)[None]
    after_mask = ((layer == last) & has_after)[None]
    result = jnp.where(before_mask, before, jnp.where(after_mask, after, 0.0))
    return result.reshape(values.shape)


def radial_sum(values):
    layer, has_before, has_after = masks()
    cubes = values.reshape(values.shape[0] // 8, 8, LANES)
    up = pltpu.roll(cubes, 1, axis=1)
    down = pltpu.roll(cubes, 7, axis=1)
    ends = jnp.where((layer == 0)[None], up, down)
    before = pltpu.roll(ends, 1, axis=2)
    after = pltpu.roll(ends, LANES - 1, axis=2)
    before_mask = ((layer == 0) & has_before)[None]
    after_mask = ((layer == 7) & has_after)[None]
    ends = jnp.where(before_mask, before, jnp.where(after_mask, after, 0.0))
    return (cubes + ends).reshape(values.shape)


def total(values):
    return jnp.sum(values, axis=(0, 1), keepdims=True)


def add_rows(block, extra):
    pieces = []
    for b in range(8):
        piece = block[8 * b : 8 * b + 8]
        pieces.append(piece + extra[b] if b in extra else piece)
    return jnp.concatenate(pieces, axis=0)


def is_even():
    return lax.axis_index("axial") % 2 == 0


def send_axial(inner_ref, outer_ref, low, high):
    even = is_even()
    row = 0
    for low_piece, high_piece in zip(low, high):
        size = low_piece.shape[0]
        inner_ref[row : row + size] = jnp.where(even, high_piece, low_piece)
        outer_ref[row : row + size] = jnp.where(even, low_piece, high_piece)
        row += size


def got_axial(inner_ref, outer_ref):
    even = is_even()

    def before(start, size):
        return jnp.where(even, outer_ref[start : start + size], inner_ref[start : start + size])

    def after(start, size):
        return jnp.where(even, inner_ref[start : start + size], outer_ref[start : start + size])

    return before, after


def conv_kernel(
    u_hbm, row_hbm, plane_hbm, grad_hbm,
    conv_ref, row_ref, out_ref, early_ref, in_ref, late_ref,
    u_ref, small_ref, plane_ref, grad_ref, sems,
):
    copies = [
        pltpu.make_async_copy(source, target, sems.at[k])
        for k, (source, target) in enumerate(
            ((u_hbm, u_ref), (plane_hbm, plane_ref), (grad_hbm, grad_ref), (row_hbm, small_ref))
        )
    ]
    for copy in copies:
        copy.start()
    row_ref[...] = jnp.zeros(row_ref.shape, F32)
    for copy in copies:
        copy.wait()
    size = small_ref.shape[1]
    for k in range(-(-size // LANES)):
        stop = min(LANES, size - LANES * k)
        row_ref[k : k + 1, :stop] = small_ref[:, LANES * k : LANES * k + stop]
    plane = plane_ref[...]
    fields = [[u_ref[d, a] for a in range(8)] for d in range(3)]
    low, high = [], []
    for comp in range(3):
        parts = fields[comp]
        flat = product(grad_ref, jnp.concatenate(parts, axis=1))
        along_a = skew_apply(DERIV, parts)
        for a in range(8):
            cols = slice(LANES * a, LANES * a + LANES)
            value = (
                fields[0][a] * along_a[a]
                + fields[1][a] * flat[:64, cols]
                + fields[2][a] * flat[64:, cols]
            )
            value = radial_sum(float(WEIGHTS[a]) * plane * value)
            conv_ref[comp, a] = value
            for side, rows in enumerate((value[:8], value[56:])):
                if a in (0, 7):
                    start = 16 * comp + (8 if a else 0)
                    late_ref[side, start : start + 8] = rows
                else:
                    start = 48 * comp + 8 * (a - 1)
                    early_ref[side, start : start + 8] = rows
            if a == 0:
                low.append(value)
            if a == 7:
                high.append(value)
    row = row_ref[...]
    send_axial(in_ref, out_ref, low + [row], high + [row])


def inverse_kernel(diff_ref, spectrum_ref, inverse_ref):
    mean = diff_ref[0]
    for a in range(1, 8):
        mean = mean + diff_ref[a]
    kbar = jnp.sum(mean, axis=0, keepdims=True) * (1.0 / 512.0)
    plane_spectrum = kbar * spectrum_ref[...] + mass_shift
    for i in range(10):
        inverse_ref[i] = 1.0 / (plane_spectrum + float(EIGVAL[i]) * kbar)


def conv_side_kernel(out_ref, in_ref, late_ref, row_ref, send_ref):
    before, after = got_axial(in_ref, out_ref)
    count = row_ref.shape[0]
    for side, b in ((0, 0), (1, 7)):
        for comp in range(3):
            first = slice(16 * comp, 16 * comp + 8)
            last = slice(16 * comp + 8, 16 * comp + 16)
            row = 64 * comp + 8 * b
            send_ref[side, first] = late_ref[side, first] + before(row, 8)
            send_ref[side, last] = late_ref[side, last] + after(row, 8)
        for place, rows in enumerate((before(192, count), row_ref[...], after(192, count))):
            start = 48 + place * count
            send_ref[side, start : start + count] = rows


def coarse_share(raw, near_ref):
    middle = raw[1]
    for a in range(2, 7):
        middle = middle + raw[a]
    per_axial = (0.5 * raw[0], middle + 0.5 * (raw[0] + raw[7]), 0.5 * raw[7])
    rows = []
    for part in per_axial:
        inner = part[8:16]
        for b in range(2, 7):
            inner = inner + part[8 * b : 8 * b + 8]
        ends = (part[:8], part[56:])
        for piece in (0.5 * ends[0], inner + 0.5 * (ends[0] + ends[1]), 0.5 * ends[1]):
            rows.append(jnp.sum(piece, axis=0, keepdims=True))
    rows = jnp.concatenate(rows + [jnp.zeros((7, LANES), F32)], axis=0)
    shares = jnp.sum(rows, axis=1, keepdims=True)
    return jnp.sum(shares * near_ref[...], axis=0, keepdims=True)


def send_sums(pay_ref, row, scalars):
    width = pay_ref.shape[1]
    place = lax.broadcasted_iota(jnp.int32, (1, width), 1)
    for k, value in enumerate(scalars):
        row = jnp.where(place == width - 1 - k, value, row)
    pay_ref[...] = jnp.broadcast_to(row, pay_ref.shape)


def got_sums(ref, scalars):
    row = jnp.sum(ref[...], axis=0, keepdims=True)
    width = row.shape[1]
    place = lax.broadcasted_iota(jnp.int32, (1, width), 1)
    values = [
        jnp.sum(jnp.where(place == width - 1 - k, row, 0.0), axis=1, keepdims=True)
        for k in range(scalars)
    ]
    return jnp.where(place >= width - TAIL, 0.0, row), values


def send_raw(raw, g_ref, in_ref, out_ref, early_ref, late_ref):
    parts = [radial_sum(raw[a]) for a in range(8)]
    for a in range(8):
        g_ref[a] = parts[a]
    send_axial(in_ref, out_ref, [parts[0], parts[1]], [parts[7], parts[6]])
    for side, (edge, inner) in enumerate(((0, 1), (7, 6))):
        edges = [part[8 * edge : 8 * edge + 8] for part in parts]
        inners = [part[8 * inner : 8 * inner + 8] for part in parts]
        for a in range(1, 7):
            early_ref[side, 8 * a - 8 : 8 * a] = edges[a]
            early_ref[side, 40 + 8 * a : 48 + 8 * a] = inners[a]
        late_ref[side, :8] = edges[0]
        late_ref[side, 8:16] = edges[7]
        late_ref[side, 16:24] = inners[0]
        late_ref[side, 24:32] = inners[7]


def raw_side_kernel(out_ref, in_ref, late_ref, row_ref, send_ref, pass_ref):
    pass_ref[...] = row_ref[...]
    before, after = got_axial(in_ref, out_ref)
    for side, (edge, inner) in enumerate(((0, 1), (7, 6))):
        send_ref[side, :8] = before(64 + 8 * edge, 8)
        send_ref[side, 8:16] = late_ref[side, :8] + before(8 * edge, 8)
        send_ref[side, 16:24] = late_ref[side, 8:16] + after(8 * edge, 8)
        send_ref[side, 24:32] = after(64 + 8 * edge, 8)
        send_ref[side, 32:40] = late_ref[side, 16:24] + before(8 * inner, 8)
        send_ref[side, 40:48] = late_ref[side, 24:32] + after(8 * inner, 8)


def divergence_kernel(
    conv_ref, u_ref, out_ref, in_ref, early_ref, late_ref, row_ref, plane_ref, over_ref, div_ref,
    g_ref, send_out_ref, send_early_ref, send_in_ref, send_late_ref, near_ref, pay_ref,
):
    before, after = got_axial(in_ref, out_ref)
    plane, over = plane_ref[...], over_ref[...]

    def side_rows(side, comp, a):
        if a in (0, 7):
            start = 16 * comp + (8 if a else 0)
            return late_ref[side, start : start + 8]
        start = 48 * comp + 8 * (a - 1)
        return early_ref[side, start : start + 8]

    moved = []
    for comp in range(3):
        parts = []
        for a in range(8):
            value = conv_ref[comp, a]
            if a == 0:
                value = value + before(64 * comp, 64)
            if a == 7:
                value = value + after(64 * comp, 64)
            value = add_rows(value, {0: side_rows(1, comp, a), 7: side_rows(0, comp, a)})
            scale = time_increment * (0.5 if a in (0, 7) else 1.0)
            parts.append(float(WEIGHTS[a]) * plane * u_ref[comp, a] - scale * over * value)
        moved.append(parts)
    flat = product(
        div_ref,
        jnp.concatenate([jnp.concatenate(moved[1], axis=1), jnp.concatenate(moved[2], axis=1)], axis=0),
    )
    along_a = skew_apply(DERIV.T, moved[0])
    raw = [along_a[a] + flat[:, LANES * a : LANES * a + LANES] for a in range(8)]
    send_raw(raw, g_ref, send_in_ref, send_out_ref, send_early_ref, send_late_ref)
    count = row_ref.shape[0]
    width = near_ref.shape[1] // LANES
    near_ref[...] = jnp.zeros(near_ref.shape, F32)
    for i in range(3):
        start = 48 + i * count
        middle = (before(192, count), row_ref[...], after(192, count))[i]
        sides = (late_ref[1, start : start + count], middle, late_ref[0, start : start + count])
        for j, rows in enumerate(sides):
            for k in range(width):
                near_ref[3 * i + j : 3 * i + j + 1, LANES * k : LANES * k + LANES] = rows[k : k + 1]
    send_sums(pay_ref, coarse_share(raw, near_ref), [])


def got_planes(g_ref, in_ref, out_ref, early_ref, late_ref):
    before, after = got_axial(in_ref, out_ref)

    def edge_rows(side, e):
        if e in (0, 1, 8, 9):
            start = 8 * (0, 1, 8, 9).index(e)
            return late_ref[side, start : start + 8]
        return early_ref[side, 8 * e - 16 : 8 * e - 8]

    def inner_rows(side, a):
        if a in (0, 7):
            start = 40 if a else 32
            return late_ref[side, start : start + 8]
        return early_ref[side, 40 + 8 * a : 48 + 8 * a]

    zero = jnp.zeros((80, LANES), F32)
    planes = []
    for e in range(10):
        if e == 0:
            value = before(64, 64)
        elif e == 9:
            value = after(64, 64)
        else:
            value = g_ref[e - 1]
        if e == 1:
            value = value + before(0, 64)
        if e == 8:
            value = value + after(0, 64)
        value = add_rows(value, {0: edge_rows(1, e), 7: edge_rows(0, e)})
        if e in (0, 9):
            rows = [value, zero]
        else:
            rows = [value, spread(value, 6, 1), inner_rows(1, e - 1), inner_rows(0, e - 1)]
        planes.append(jnp.concatenate(rows, axis=0))
    return planes


def to_part(rows):
    return radial_sum(rows[:64] + spread(rows[64:128], 1, 6)), radial_sum(rows[128:144])


def solve_ends_kernel(
    g_ref, out_ref, in_ref, early_ref, late_ref, row_ref, inverse_ref, into_ref, outof_ref,
    planes_ref, middle_ref, ends_ref, send_out_ref, send_in_ref, pass_ref,
):
    pass_ref[...] = jnp.broadcast_to(row_ref[...], pass_ref.shape)
    planes = got_planes(g_ref, in_ref, out_ref, early_ref, late_ref)
    for e in range(10):
        planes_ref[e] = planes[e]
    flat = product(into_ref, jnp.concatenate(planes, axis=1))
    parts = to_spectral([flat[:, LANES * e : LANES * e + LANES] for e in range(10)])
    parts = [parts[i] * inverse_ref[i] for i in range(10)]
    parts = from_spectral(parts)
    flat = product(outof_ref, jnp.concatenate([parts[e] for e in (0, 1, 8, 9)], axis=1))
    ends = [flat[:, LANES * k : LANES * k + LANES] for k in range(4)]
    low, low_faces = to_part(ends[1])
    high, high_faces = to_part(ends[2])
    send_axial(
        send_in_ref,
        send_out_ref,
        [low, radial_sum(ends[0][:64]), low_faces],
        [high, radial_sum(ends[3][:64]), high_faces],
    )
    for k in range(4):
        ends_ref[k] = ends[k]
    for e in range(2, 8):
        middle_ref[e - 2] = parts[e]


def solve_rest_kernel(
    middle_ref, ends_ref, outof_ref, solved_ref, part_ref, send_early_ref, send_late_ref,
):
    flat = product(outof_ref, jnp.concatenate([middle_ref[k] for k in range(6)], axis=1))
    solved = [flat[:, LANES * k : LANES * k + LANES] for k in range(6)]
    solved = [ends_ref[0], ends_ref[1]] + solved + [ends_ref[2], ends_ref[3]]
    for e in range(10):
        solved_ref[e] = solved[e]
    for a in range(8):
        value, outer_b = to_part(solved[a + 1])
        part_ref[a] = value
        for side in range(2):
            edge = value[56 * side : 56 * side + 8]
            face = outer_b[8 * side : 8 * side + 8]
            if a in (0, 1, 6, 7):
                start = 8 * (0, 1, 6, 7).index(a)
                send_late_ref[side, start : start + 8] = edge
            else:
                send_early_ref[side, 8 * a - 16 : 8 * a - 8] = edge
            if a in (0, 7):
                start = 40 if a else 32
                send_late_ref[side, start : start + 8] = face
            else:
                send_early_ref[side, 24 + 8 * a : 32 + 8 * a] = face


def solved_side_kernel(out_ref, in_ref, late_ref, row_ref, send_ref, pass_ref):
    pass_ref[...] = row_ref[...]
    before, after = got_axial(in_ref, out_ref)
    for side, b in ((0, 0), (1, 7)):
        row = 8 * b
        send_ref[side, :8] = late_ref[side, :8] + before(row, 8)
        send_ref[side, 8:16] = late_ref[side, 8:16] + before(64 + row, 8)
        send_ref[side, 16:24] = late_ref[side, 16:24] + after(64 + row, 8)
        send_ref[side, 24:32] = late_ref[side, 24:32] + after(row, 8)
        send_ref[side, 32:40] = late_ref[side, 32:40] + before(128 + 8 * side, 8)
        send_ref[side, 40:48] = late_ref[side, 40:48] + after(128 + 8 * side, 8)


def got_solved(part_ref, in_ref, out_ref, early_ref, late_ref):
    before, after = got_axial(in_ref, out_ref)
    extra = {0: (before, 0), 1: (before, 64), 6: (after, 64), 7: (after, 0)}

    def edge_rows(side, a):
        if a in extra:
            start = 8 * (0, 1, 6, 7).index(a)
            return late_ref[side, start : start + 8]
        return early_ref[side, 8 * a - 16 : 8 * a - 8]

    def face_rows(side, a):
        if a in (0, 7):
            start = 40 if a else 32
            return late_ref[side, start : start + 8]
        return early_ref[side, 24 + 8 * a : 32 + 8 * a]

    result = []
    for a in range(8):
        value = part_ref[a]
        if a in extra:
            side, start = extra[a]
            value = value + side(start, 64)
        result.append(
            add_rows(
                value,
                {0: edge_rows(1, a), 1: face_rows(1, a), 6: face_rows(0, a), 7: edge_rows(0, a)},
            )
        )
    return result


def add_coarse(parts, row, near_ref):
    values = jnp.sum(near_ref[...] * row, axis=1, keepdims=True)
    own = [[values[3 * i + j : 3 * i + j + 1] for j in range(3)] for i in range(3)]
    fields = []
    for i in range(3):
        ends = [0.5 * (own[i][1] + own[i][j]) for j in (0, 2)]
        rows = [jnp.broadcast_to(value, (8, LANES)) for value in (ends[0], own[i][1], ends[1])]
        fields.append(jnp.concatenate([rows[0]] + [rows[1]] * 6 + [rows[2]], axis=0))
    first, last = 0.5 * (fields[0] + fields[1]), 0.5 * (fields[1] + fields[2])
    return [
        parts[a] + (first if a == 0 else last if a == 7 else fields[1]) for a in range(8)
    ]


def apply_operator(values, diff_ref, plane_ref, grad_ref, div_ref):
    plane = plane_ref[...]
    coef = [float(WEIGHTS[a]) * plane * diff_ref[a] for a in range(8)]
    flat = product(grad_ref, jnp.concatenate(values, axis=1))
    along_a = skew_apply(DERIV, values)
    flux = jnp.concatenate(
        [
            jnp.concatenate([coef[a], coef[a]], axis=0) * flat[:, LANES * a : LANES * a + LANES]
            for a in range(8)
        ],
        axis=1,
    )
    flat = product(div_ref, flux)
    along_a = skew_apply(DERIV.T, [coef[a] * along_a[a] for a in range(8)])
    return [
        along_a[a]
        + flat[:, LANES * a : LANES * a + LANES]
        + (mass_shift * float(WEIGHTS[a])) * plane * values[a]
        for a in range(8)
    ]


def dot_parts(first, second):
    result = first[0] * second[0]
    for a in range(1, 8):
        result = result + first[a] * second[a]
    return total(result)


def norm(row):
    return jnp.sum(row * row, axis=1, keepdims=True)


def dot_planes(first, second):
    result = None
    for e in range(10):
        stop = 64 if e in (0, 9) else 144
        term = first[e][:stop] * second[e][:stop]
        term = jnp.sum(term.reshape(stop // 8, 8, LANES), axis=0)
        result = term if result is None else result + term
    return total(result)


def first_apply_kernel(
    part_ref, out_ref, in_ref, early_ref, late_ref, near_ref, diff_ref, plane_ref, grad_ref, div_ref,
    sums_ref, planes_ref, solved_ref,
    z_ref, raw_ref, g_ref, send_out_ref, send_early_ref, send_in_ref, send_late_ref, row_ref, pay_ref,
):
    row, _ = got_sums(sums_ref, 0)
    values = got_solved(part_ref, in_ref, out_ref, early_ref, late_ref)
    values = add_coarse(values, row, near_ref)
    raw = apply_operator(values, diff_ref, plane_ref, grad_ref, div_ref)
    send_raw(raw, g_ref, send_in_ref, send_out_ref, send_early_ref, send_late_ref)
    for a in range(8):
        z_ref[a] = values[a]
        raw_ref[a] = raw[a]
    row_ref[0:1] = row
    scalars = [dot_planes(planes_ref, solved_ref), dot_parts(values, raw)]
    send_sums(pay_ref, coarse_share(raw, near_ref), scalars)


def first_step(sums_ref, row_ref):
    row_q, (local_rz, curv) = got_sums(sums_ref, 2)
    row_r = row_ref[0:1]
    rz = local_rz + norm(row_r)
    return row_r, row_q, rz, curv, rz / curv


def second_apply_kernel(
    part_ref, out_ref, in_ref, early_ref, late_ref, near_ref, diff_ref, plane_ref, grad_ref, div_ref,
    sums_ref, row_ref, z0_ref,
    y_ref, z_ref, raw_ref, g_ref, send_out_ref, send_early_ref, send_in_ref, send_late_ref,
):
    _, row_q, _, _, alpha = first_step(sums_ref, row_ref)
    change = got_solved(part_ref, in_ref, out_ref, early_ref, late_ref)
    change = add_coarse(change, row_q, near_ref)
    values = [z0_ref[a] - alpha * change[a] for a in range(8)]
    raw = apply_operator(values, diff_ref, plane_ref, grad_ref, div_ref)
    send_raw(raw, g_ref, send_in_ref, send_out_ref, send_early_ref, send_late_ref)
    for a in range(8):
        y_ref[a] = change[a]
        z_ref[a] = values[a]
        raw_ref[a] = raw[a]


def first_dots_kernel(
    sums_ref, row_ref, near_ref, planes_r_ref, planes_q_ref, solved_r_ref, solved_q_ref,
    z_ref, raw_ref, old_raw_ref,
    planes_ref, solved_ref, pay_ref,
):
    alpha = first_step(sums_ref, row_ref)[4]
    planes, solved = [], []
    for e in range(10):
        planes.append(planes_r_ref[e] - alpha * planes_q_ref[e])
        solved.append(solved_r_ref[e] - alpha * solved_q_ref[e])
        planes_ref[e] = planes[e]
        solved_ref[e] = solved[e]
    values = [z_ref[a] for a in range(8)]
    raw = [raw_ref[a] for a in range(8)]
    scalars = [
        dot_planes(planes, solved),
        dot_planes(planes, solved_q_ref),
        dot_planes(planes_q_ref, solved),
        dot_planes(planes_q_ref, solved_q_ref),
        dot_parts(values, raw),
        dot_parts(values, [old_raw_ref[a] for a in range(8)]),
    ]
    send_sums(pay_ref, coarse_share(raw, near_ref), scalars)


def second_dots_kernel(
    row_ref, planes_r_ref, planes_q_ref, planes_w_ref, solved_r_ref, solved_q_ref, solved_w_ref,
    pay_ref,
):
    scalars = [
        dot_planes(planes_r_ref, solved_w_ref),
        dot_planes(planes_q_ref, solved_w_ref),
        dot_planes(planes_w_ref, solved_r_ref),
        dot_planes(planes_w_ref, solved_q_ref),
        dot_planes(planes_w_ref, solved_w_ref),
    ]
    row = row_ref[...]
    width = row.shape[1]
    place = lax.broadcasted_iota(jnp.int32, (1, width), 1)
    for k, value in enumerate(scalars):
        row = jnp.where(place == width - 7 - k, value, row)
    pay_ref[...] = jnp.broadcast_to(row, pay_ref.shape)


def last_kernel(
    part_ref, out_ref, in_ref, early_ref, late_ref, near_ref, sums_ref, old_sums_ref, row_ref, _,
    y_ref, z0_ref, z1_ref, planes_r_ref, planes_q_ref, planes_w_ref,
    pressure_ref, residual_ref, direction_ref,
):
    row_r, row_q, rz0, curv0, alpha0 = first_step(old_sums_ref, row_ref)
    row_w, scalars = got_sums(sums_ref, 11)
    rr, rq, qr, qq, first_curv, cross, rw, qw, wr, wq, ww = scalars
    row_r = row_r - alpha0 * row_q
    rz1 = rr + norm(row_r)
    beta0 = rz1 / rz0
    curv1 = first_curv + beta0 * (2.0 * cross + beta0 * curv0)
    alpha1 = rz1 / curv1
    row = row_w + beta0 * row_q
    row_r = row_r - alpha1 * row
    step = -alpha1 * beta0
    rz2 = (
        rr
        - alpha1 * (rw + wr)
        + step * (rq + qr)
        + alpha1 * alpha1 * ww
        - alpha1 * step * (wq + qw)
        + step * step * qq
        + norm(row_r)
    )
    beta1 = rz2 / rz1
    change = got_solved(part_ref, in_ref, out_ref, early_ref, late_ref)
    change = add_coarse(change, row_w, near_ref)
    for a in range(8):
        first = z0_ref[a]
        second = z1_ref[a] + beta0 * first
        image = planes_w_ref[a + 1, :64] + beta0 * planes_q_ref[a + 1, :64]
        residual_ref[a] = planes_r_ref[a + 1, :64] - alpha1 * image
        pressure_ref[a] = alpha0 * first + alpha1 * second
        direction_ref[a] = (
            z1_ref[a] - alpha1 * (change[a] + beta0 * y_ref[a]) + beta1 * second
        )


def kernel_call(kernel, out_shapes, *args, **options):
    outs = [jax.ShapeDtypeStruct(shape, F32) for shape in out_shapes]
    return pl.pallas_call(
        kernel,
        out_shape=outs,
        compiler_params=pltpu.CompilerParams(vmem_limit_bytes=VMEM_GRANT),
        interpret=INTERPRET,
        **options,
    )(*args)


def axial_swap(inner_rows, outer_rows):
    count = lax.axis_size("axial")
    inner = [(i, i ^ 1) for i in range(count)]
    outer = [((2 * i + 1) % count, (2 * i + 2) % count) for i in range(count // 2)]
    outer = outer + [(b, a) for a, b in outer]
    from_outer = lax.ppermute(outer_rows, "axial", outer)
    from_inner = lax.ppermute(inner_rows, "axial", inner)
    return from_inner, from_outer


def azim_swap(sides):
    count = lax.axis_size("azim")
    if count == 2:
        return lax.ppermute(sides, "azim", [(0, 1), (1, 0)])
    after = lax.ppermute(sides[0], "azim", [((i + 1) % count, i) for i in range(count)])
    before = lax.ppermute(sides[1], "azim", [(i, (i + 1) % count) for i in range(count)])
    return jnp.stack([after, before])


def sum_steps():
    azim = lax.axis_size("azim")
    count = lax.axis_size("axial") * azim
    steps, step = [], 2 * azim
    while step < count:
        steps.append(step)
        step *= 2
    step = 1
    while step < azim:
        steps.append(step)
        step *= 2
    groups = [steps[k::4] for k in range(4)]
    groups[0] = groups[0] + [azim]
    return groups


def partial_sum(row, steps):
    count = lax.axis_size("axial") * lax.axis_size("azim")
    for step in steps:
        row = row[:1] + lax.ppermute(row, ALL, [(i, i ^ step) for i in range(count)])[:1]
    return row


def gather_sums(rows):
    return lax.all_to_all(rows, ALL, 0, 0, tiled=True)


def per_device(velocity, diffusivity, coarse_factor):
    shape = diffusivity.shape
    devices = lax.axis_size("axial") * lax.axis_size("azim")
    u = velocity.reshape(3, 8, 64, LANES)
    diff = diffusivity.reshape(8, 64, LANES)
    tables = constant_tables(LANES)
    plane, over, spectrum = tables["plane"], tables["over"], tables["spectrum"]
    grad, div, into, outof = tables["grad"], tables["div"], tables["into"], tables["outof"]
    coarse_size = coarse_factor.shape[1]
    width = -(-(coarse_size + TAIL) // LANES)
    count = 8 * -(-width // 8)

    field, sums, row_shape = (8, 64, LANES), (devices, width * LANES), (8, width * LANES)
    boxes = [(10, 144, LANES), (10, 144, LANES)]
    raw_sends = [(128, LANES), (2, 96, LANES), (128, LANES), (2, 32, LANES)]

    far = pl.BlockSpec(memory_space=pltpu.HBM)
    conv, row, *sends = kernel_call(
        conv_kernel,
        [(3,) + field, (count, LANES), (192 + count, LANES), (2, 144, LANES)]
        + [(192 + count, LANES), (2, 48, LANES)],
        *(pltpu.with_memory_space_constraint(x, pltpu.HBM) for x in (u, coarse_factor, plane, grad)),
        in_specs=[far] * 4,
        scratch_shapes=[
            pltpu.VMEM((3,) + field, F32),
            pltpu.VMEM((1, coarse_size), F32),
            pltpu.VMEM(plane.shape, F32),
            pltpu.VMEM(grad.shape, BF16),
            pltpu.SemaphoreType.DMA((4,)),
        ],
    )
    (inverse,) = kernel_call(inverse_kernel, [(10, 112, LANES)], diff, spectrum)

    def exchange(side_kernel, late_rows, sends, extra, extra_shape=None):
        send_out, send_early, send_in, send_late = sends
        inner, outer = axial_swap(send_in, send_out)
        early = azim_swap(send_early)
        shapes = [(2, late_rows, LANES)]
        shapes = shapes if extra_shape is None else shapes + [extra_shape]
        late, *passed = kernel_call(side_kernel, shapes, outer, inner, send_late, extra)
        return [outer, inner, early, azim_swap(late)] + passed

    one, copies = (1, width * LANES), (SUM_ROWS, width * LANES)
    groups = sum_steps()
    moved = exchange(conv_side_kernel, 48 + 3 * count, sends, row)
    g, *sends, near, pay = kernel_call(
        divergence_kernel,
        [field] + raw_sends + [(16, width * LANES), copies],
        conv, u, *moved, row, plane, over, div,
    )
    solver = (inverse, into, outof)
    operator = (near, diff, plane, grad, div)

    def solve(g, moved, pay):
        ends = [(6, 112, LANES), (4, 144, LANES), (144, LANES), (144, LANES), copies]
        planes, middle, ends, send_out, send_in, pay = kernel_call(
            solve_ends_kernel, boxes[:1] + ends, g, *moved, pay, *solver
        )
        solved, part, send_early, send_late = kernel_call(
            solve_rest_kernel,
            boxes[:1] + [field, (2, 80, LANES), (2, 48, LANES)],
            middle, ends, outof,
        )
        return planes, solved, part, send_out, send_early, send_in, send_late, pay


    *moved, pay = exchange(raw_side_kernel, 48, sends, partial_sum(pay, groups[0]), one)
    pay = partial_sum(pay, groups[1])
    planes_r, solved_r, part, *sends, pay = solve(g, moved, pay)
    *moved, pay = exchange(solved_side_kernel, 48, sends, partial_sum(pay, groups[2]), one)
    pay = partial_sum(pay, groups[3])
    z0, raw0, g, *sends, row_r, pay = kernel_call(
        first_apply_kernel,
        [field, field, field] + raw_sends + [row_shape, copies],
        part, *moved, *operator, pay, planes_r, solved_r,
    )
    *moved, pay = exchange(raw_side_kernel, 48, sends, partial_sum(pay, groups[0]), one)
    pay = partial_sum(pay, groups[1])
    planes_q, solved_q, part, *sends, pay = solve(g, moved, pay)
    *moved, pay = exchange(solved_side_kernel, 48, sends, partial_sum(pay, groups[2]), one)
    first_sums = partial_sum(pay, groups[3])
    y, z1, raw1, g, *sends = kernel_call(
        second_apply_kernel,
        [field, field, field, field] + raw_sends,
        part, *moved, *operator, first_sums, row_r, z0,
    )
    planes_r, solved_r, pay = kernel_call(
        first_dots_kernel,
        boxes + [one],
        first_sums, row_r, near, planes_r, planes_q, solved_r, solved_q, z1, raw1, raw0,
    )
    *moved, pay = exchange(raw_side_kernel, 48, sends, pay, one)
    planes_w, solved_w, part, *sends, pay = solve(g, moved, pay)
    (pay,) = kernel_call(
        second_dots_kernel, [one], pay[:1], planes_r, planes_q, planes_w, solved_r, solved_q, solved_w
    )
    gathered = gather_sums(jnp.broadcast_to(pay, sums))
    *moved, passed = exchange(solved_side_kernel, 48, sends, pay, one)
    pressure, residual, direction = kernel_call(
        last_kernel,
        [field, field, field],
        part, *moved, near, gathered, first_sums, row_r, passed,
        y, z0, z1, planes_r, planes_q, planes_w,
    )
    return pressure.reshape(shape), residual.reshape(shape), direction.reshape(shape)


def solution(mesh):
    split = P(None, None, None, "axial", "azim", None)
    in_specs = (P(None, None, None, None, "axial", "azim", None), split, P(ALL, None))
    return jax.shard_map(
        per_device, mesh=mesh, in_specs=in_specs, out_specs=(split, split, split), check_vma=False
    )
```

```python
import math

import jax
import jax.numpy as jnp
import numpy as np
from jax import lax
from jax.experimental import pallas as pl
from jax.experimental.pallas import tpu as pltpu
from jax.sharding import PartitionSpec as P

ALL = ("axial", "azim")
time_increment = 0.02
mass_shift = 0.05
VMEM_GRANT = 20 << 20
TAIL = 16
SUM_ROWS = 32
gll_points = [
    -1.0,
    -0.8717401485096066,
    -0.5917001814331423,
    -0.20929921790247888,
    0.20929921790247888,
    0.5917001814331423,
    0.8717401485096066,
    1.0,
]


def legendre_value(order, point):
    before = 1.0
    current = point
    for step_idx in range(1, order):
        after = ((2 * step_idx + 1) * point * current - step_idx * before) / (step_idx + 1)
        before = current
        current = after
    return current


def jacobi_eigen(matrix):
    size_n = len(matrix)
    work = [list(row) for row in matrix]
    vectors = [
        [1.0 if row_idx == col_idx else 0.0 for col_idx in range(size_n)]
        for row_idx in range(size_n)
    ]
    for sweep_idx in range(15):
        for row_idx in range(size_n):
            for col_idx in range(row_idx + 1, size_n):
                off_value = work[row_idx][col_idx]
                if off_value != 0.0:
                    theta = (work[col_idx][col_idx] - work[row_idx][row_idx]) / (2.0 * off_value)
                    root_val = math.sqrt(theta * theta + 1.0)
                    tangent = 1.0 / (theta + root_val) if theta >= 0.0 else 1.0 / (theta - root_val)
                    cosine = 1.0 / math.sqrt(tangent * tangent + 1.0)
                    sine = tangent * cosine
                    for other in range(size_n):
                        left_val = work[other][row_idx]
                        right_val = work[other][col_idx]
                        work[other][row_idx] = cosine * left_val - sine * right_val
                        work[other][col_idx] = sine * left_val + cosine * right_val
                    for other in range(size_n):
                        left_val = work[row_idx][other]
                        right_val = work[col_idx][other]
                        work[row_idx][other] = cosine * left_val - sine * right_val
                        work[col_idx][other] = sine * left_val + cosine * right_val
                    for other in range(size_n):
                        left_val = vectors[other][row_idx]
                        right_val = vectors[other][col_idx]
                        vectors[other][row_idx] = cosine * left_val - sine * right_val
                        vectors[other][col_idx] = sine * left_val + cosine * right_val
    return ([work[row_idx][row_idx] for row_idx in range(size_n)], vectors)


def gll_tables():
    degree = 7
    points = degree + 1
    legendre_at = [legendre_value(degree, node_val) for node_val in gll_points]
    weights = [2.0 / (degree * (degree + 1) * value * value) for value in legendre_at]
    derivative = [[0.0] * points for row_idx in range(points)]
    for row_idx in range(points):
        for col_idx in range(points):
            if row_idx != col_idx:
                derivative[row_idx][col_idx] = legendre_at[row_idx] / (
                    legendre_at[col_idx] * (gll_points[row_idx] - gll_points[col_idx])
                )
    derivative[0][0] = -degree * (degree + 1) / 4.0
    derivative[degree][degree] = degree * (degree + 1) / 4.0
    stiffness = [
        [
            sum(
                (
                    derivative[mid_idx][row_idx] * weights[mid_idx] * derivative[mid_idx][col_idx]
                    for mid_idx in range(points)
                )
            )
            for col_idx in range(points)
        ]
        for row_idx in range(points)
    ]
    line_len = 3 * degree + 1
    big_stiff = [[0.0] * line_len for row_idx in range(line_len)]
    big_mass = [0.0] * line_len
    for element in range(3):
        offset = element * degree
        for row_idx in range(points):
            big_mass[offset + row_idx] += weights[row_idx]
            for col_idx in range(points):
                big_stiff[offset + row_idx][offset + col_idx] += stiffness[row_idx][col_idx]
    start_node = degree - 1
    box_len = degree + 3
    scaling = [1.0 / math.sqrt(big_mass[start_node + row_idx]) for row_idx in range(box_len)]
    symmetric = [
        [
            scaling[row_idx]
            * big_stiff[start_node + row_idx][start_node + col_idx]
            * scaling[col_idx]
            for col_idx in range(box_len)
        ]
        for row_idx in range(box_len)
    ]
    eigval, eigvec = jacobi_eigen(symmetric)
    fdm_basis = [
        [scaling[row_idx] * eigvec[row_idx][col_idx] for col_idx in range(box_len)]
        for row_idx in range(box_len)
    ]
    return (weights, derivative, fdm_basis, eigval)

WEIGHTS, DERIV, BASIS, EIGVAL = (np.asarray(t, np.float64) for t in gll_tables())


def f32(table):
    return jnp.asarray(table, jnp.float32)


F32 = jnp.float32
BF16 = jnp.bfloat16
LANES = 128
INTERPRET = False


def split_terms(table, depth):
    padded = np.zeros((table.shape[0], depth))
    padded[:, : table.shape[1]] = table
    high = padded.astype(jnp.bfloat16)
    low = (padded - high.astype(np.float64)).astype(jnp.bfloat16)
    return jnp.asarray(np.concatenate([high, high, low], axis=1))


def box_tables():
    pairs = [(b + 1, c + 1) for b in range(8) for c in range(8)]
    pairs += [(b + 1, {6: 0, 1: 9}.get(c)) for b in range(8) for c in range(8)]
    pairs += [(0, c + 1) for c in range(8)] + [(9, c + 1) for c in range(8)]
    table = np.zeros((144, 112))
    for row, (b, c) in enumerate(pairs):
        if c is not None:
            table[row, :100] = np.outer(BASIS[b], BASIS[c]).reshape(100)
    sums = np.ones(112)
    sums[:100] = (EIGVAL[:, None] + EIGVAL[None, :]).reshape(100)
    return table, sums


EYE = np.eye(8)
GRAD = np.concatenate([np.kron(DERIV, EYE), np.kron(EYE, DERIV)])
BOX_ROWS, SPECTRUM = box_tables()
EVEN = [bool(abs(BASIS[0, i] - BASIS[9, i]) < abs(BASIS[0, i] + BASIS[9, i])) for i in range(10)]


def constant_tables(radial):
    plane = (WEIGHTS[:, None] * WEIGHTS[None, :]).reshape(64, 1)
    mult_r = np.ones((8, radial))
    mult_r[0, 1:] = 2.0
    mult_r[7, :-1] = 2.0
    ends = np.array([2.0, 1, 1, 1, 1, 1, 1, 2.0])
    mult = (ends[:, None, None] * mult_r[None]).reshape(64, radial)
    return dict(
        plane=f32(np.broadcast_to(plane, (64, radial))),
        over=f32(1.0 / mult),
        spectrum=f32(np.broadcast_to(SPECTRUM[:, None], (112, radial))),
        grad=split_terms(GRAD, 64),
        div=split_terms(GRAD.T, 128),
        into=split_terms(BOX_ROWS.T, 144),
        outof=split_terms(BOX_ROWS, 112),
    )


def product(table_ref, values):
    high = values.astype(BF16)
    low = (values - high.astype(F32)).astype(BF16)
    return jnp.dot(
        table_ref[...], jnp.concatenate([high, low, high], axis=0), preferred_element_type=F32
    )


def combine(coefs, terms):
    total = None
    for coef, term in zip(coefs, terms):
        scaled = float(coef) * term
        total = scaled if total is None else total + scaled
    return total


def skew_apply(matrix, parts, rows=range(4)):
    plus = [parts[b] + parts[7 - b] for b in range(4)]
    minus = [parts[b] - parts[7 - b] for b in range(4)]
    result = [None] * 8
    for a in rows:
        even = combine([0.5 * (matrix[a, b] + matrix[a, 7 - b]) for b in range(4)], plus)
        odd = combine([0.5 * (matrix[a, b] - matrix[a, 7 - b]) for b in range(4)], minus)
        result[a] = even + odd
        result[7 - a] = odd - even
    return result


def to_spectral(parts):
    plus = [parts[a] + parts[9 - a] for a in range(5)]
    minus = [parts[a] - parts[9 - a] for a in range(5)]
    return [combine(BASIS[:5, i], plus if EVEN[i] else minus) for i in range(10)]


def from_spectral(parts):
    evens = [i for i in range(10) if EVEN[i]]
    odds = [i for i in range(10) if not EVEN[i]]
    result = [None] * 10
    for a in range(5):
        even = combine(BASIS[a, evens], [parts[i] for i in evens])
        odd = combine(BASIS[a, odds], [parts[i] for i in odds])
        result[a] = even + odd
        result[9 - a] = even - odd
    return result


def masks():
    layer = lax.broadcasted_iota(jnp.int32, (8, LANES), 0)
    elem = lax.broadcasted_iota(jnp.int32, (8, LANES), 1)
    return layer, elem > 0, elem < LANES - 1


def spread(values, first, last):
    layer, has_before, has_after = masks()
    cubes = values.reshape(values.shape[0] // 8, 8, LANES)
    before = pltpu.roll(cubes, 1, axis=2)
    after = pltpu.roll(cubes, LANES - 1, axis=2)
    before_mask = ((layer == first) & has_before)[None]
    after_mask = ((layer == last) & has_after)[None]
    result = jnp.where(before_mask, before, jnp.where(after_mask, after, 0.0))
    return result.reshape(values.shape)


def radial_sum(values):
    layer, has_before, has_after = masks()
    cubes = values.reshape(values.shape[0] // 8, 8, LANES)
    up = pltpu.roll(cubes, 1, axis=1)
    down = pltpu.roll(cubes, 7, axis=1)
    ends = jnp.where((layer == 0)[None], up, down)
    before = pltpu.roll(ends, 1, axis=2)
    after = pltpu.roll(ends, LANES - 1, axis=2)
    before_mask = ((layer == 0) & has_before)[None]
    after_mask = ((layer == 7) & has_after)[None]
    ends = jnp.where(before_mask, before, jnp.where(after_mask, after, 0.0))
    return (cubes + ends).reshape(values.shape)


def total(values):
    return jnp.sum(values, axis=(0, 1), keepdims=True)


def add_rows(block, extra):
    pieces = []
    for b in range(8):
        piece = block[8 * b : 8 * b + 8]
        pieces.append(piece + extra[b] if b in extra else piece)
    return jnp.concatenate(pieces, axis=0)


def is_even():
    return lax.axis_index("axial") % 2 == 0


def send_axial(inner_ref, outer_ref, low, high):
    even = is_even()
    row = 0
    for low_piece, high_piece in zip(low, high):
        size = low_piece.shape[0]
        inner_ref[row : row + size] = jnp.where(even, high_piece, low_piece)
        outer_ref[row : row + size] = jnp.where(even, low_piece, high_piece)
        row += size


def got_axial(inner_ref, outer_ref):
    even = is_even()

    def before(start, size):
        return jnp.where(even, outer_ref[start : start + size], inner_ref[start : start + size])

    def after(start, size):
        return jnp.where(even, inner_ref[start : start + size], outer_ref[start : start + size])

    return before, after


def conv_kernel(
    u_hbm, row_hbm, plane_hbm, grad_hbm,
    conv_ref, row_ref, out_ref, early_ref, in_ref, late_ref,
    u_ref, small_ref, plane_ref, grad_ref, sems,
):
    copies = [
        pltpu.make_async_copy(source, target, sems.at[k])
        for k, (source, target) in enumerate(
            ((u_hbm, u_ref), (plane_hbm, plane_ref), (grad_hbm, grad_ref), (row_hbm, small_ref))
        )
    ]
    for copy in copies:
        copy.start()
    row_ref[...] = jnp.zeros(row_ref.shape, F32)
    for copy in copies:
        copy.wait()
    size = small_ref.shape[1]
    for k in range(-(-size // LANES)):
        stop = min(LANES, size - LANES * k)
        row_ref[k : k + 1, :stop] = small_ref[:, LANES * k : LANES * k + stop]
    plane = plane_ref[...]
    fields = [[u_ref[d, a] for a in range(8)] for d in range(3)]
    low, high = [], []
    for comp in range(3):
        parts = fields[comp]
        flat = product(grad_ref, jnp.concatenate(parts, axis=1))
        along_a = skew_apply(DERIV, parts)
        for a in range(8):
            cols = slice(LANES * a, LANES * a + LANES)
            value = (
                fields[0][a] * along_a[a]
                + fields[1][a] * flat[:64, cols]
                + fields[2][a] * flat[64:, cols]
            )
            value = radial_sum(float(WEIGHTS[a]) * plane * value)
            conv_ref[comp, a] = value
            for side, rows in enumerate((value[:8], value[56:])):
                if a in (0, 7):
                    start = 16 * comp + (8 if a else 0)
                    late_ref[side, start : start + 8] = rows
                else:
                    start = 48 * comp + 8 * (a - 1)
                    early_ref[side, start : start + 8] = rows
            if a == 0:
                low.append(value)
            if a == 7:
                high.append(value)
    row = row_ref[...]
    send_axial(in_ref, out_ref, low + [row], high + [row])


def inverse_kernel(diff_ref, spectrum_ref, inverse_ref):
    mean = diff_ref[0]
    for a in range(1, 8):
        mean = mean + diff_ref[a]
    kbar = jnp.sum(mean, axis=0, keepdims=True) * (1.0 / 512.0)
    plane_spectrum = kbar * spectrum_ref[...] + mass_shift
    for i in range(10):
        inverse_ref[i] = 1.0 / (plane_spectrum + float(EIGVAL[i]) * kbar)


def conv_side_kernel(out_ref, in_ref, late_ref, row_ref, send_ref):
    before, after = got_axial(in_ref, out_ref)
    count = row_ref.shape[0]
    for side, b in ((0, 0), (1, 7)):
        for comp in range(3):
            first = slice(16 * comp, 16 * comp + 8)
            last = slice(16 * comp + 8, 16 * comp + 16)
            row = 64 * comp + 8 * b
            send_ref[side, first] = late_ref[side, first] + before(row, 8)
            send_ref[side, last] = late_ref[side, last] + after(row, 8)
        send_ref[side, 48:] = jnp.zeros((send_ref.shape[1] - 48, LANES), F32)
        for place, rows in enumerate((before(192, count), row_ref[...], after(192, count))):
            width = min(count, (send_ref.shape[1] - 48) // 3)
            start = 48 + place * width
            send_ref[side, start : start + width] = rows[:width]


def coarse_share(raw, near_ref):
    middle = raw[1]
    for a in range(2, 7):
        middle = middle + raw[a]
    per_axial = (0.5 * raw[0], middle + 0.5 * (raw[0] + raw[7]), 0.5 * raw[7])
    rows = []
    for part in per_axial:
        inner = part[8:16]
        for b in range(2, 7):
            inner = inner + part[8 * b : 8 * b + 8]
        ends = (part[:8], part[56:])
        for piece in (0.5 * ends[0], inner + 0.5 * (ends[0] + ends[1]), 0.5 * ends[1]):
            rows.append(jnp.sum(piece, axis=0, keepdims=True))
    rows = jnp.concatenate(rows + [jnp.zeros((7, LANES), F32)], axis=0)
    shares = jnp.sum(rows, axis=1, keepdims=True)
    return jnp.sum(shares * near_ref[...], axis=0, keepdims=True)


def send_sums(pay_ref, row, scalars):
    width = pay_ref.shape[1]
    place = lax.broadcasted_iota(jnp.int32, (1, width), 1)
    for k, value in enumerate(scalars):
        row = jnp.where(place == width - 1 - k, value, row)
    pay_ref[...] = jnp.broadcast_to(row, pay_ref.shape)


def got_sums(ref, scalars):
    row = jnp.sum(ref[...], axis=0, keepdims=True)
    width = row.shape[1]
    place = lax.broadcasted_iota(jnp.int32, (1, width), 1)
    values = [
        jnp.sum(jnp.where(place == width - 1 - k, row, 0.0), axis=1, keepdims=True)
        for k in range(scalars)
    ]
    return jnp.where(place >= width - TAIL, 0.0, row), values


def send_raw_ends(parts, in_ref, out_ref):
    send_axial(in_ref, out_ref, [parts[0], parts[1]], [parts[7], parts[6]])


def send_raw_rest(parts, g_ref, early_ref, late_ref):
    for a in range(8):
        g_ref[a] = parts[a]
    for side, (edge, inner) in enumerate(((0, 1), (7, 6))):
        edges = [part[8 * edge : 8 * edge + 8] for part in parts]
        inners = [part[8 * inner : 8 * inner + 8] for part in parts]
        for a in range(1, 7):
            early_ref[side, 8 * a - 8 : 8 * a] = edges[a]
            early_ref[side, 40 + 8 * a : 48 + 8 * a] = inners[a]
        late_ref[side, :8] = edges[0]
        late_ref[side, 8:16] = edges[7]
        late_ref[side, 16:24] = inners[0]
        late_ref[side, 24:32] = inners[7]


def send_raw(raw, g_ref, in_ref, out_ref, early_ref, late_ref):
    parts = [radial_sum(raw[a]) for a in range(8)]
    send_raw_ends(parts, in_ref, out_ref)
    send_raw_rest(parts, g_ref, early_ref, late_ref)


def raw_side_kernel(out_ref, in_ref, late_ref, row_ref, send_ref, pass_ref):
    pass_ref[...] = row_ref[...]
    before, after = got_axial(in_ref, out_ref)
    for side, (edge, inner) in enumerate(((0, 1), (7, 6))):
        send_ref[side, :8] = before(64 + 8 * edge, 8)
        send_ref[side, 8:16] = late_ref[side, :8] + before(8 * edge, 8)
        send_ref[side, 16:24] = late_ref[side, 8:16] + after(8 * edge, 8)
        send_ref[side, 24:32] = after(64 + 8 * edge, 8)
        send_ref[side, 32:40] = late_ref[side, 16:24] + before(8 * inner, 8)
        send_ref[side, 40:48] = late_ref[side, 24:32] + after(8 * inner, 8)


def divergence_kernel(
    early_ref, conv_ref, u_ref, out_ref, in_ref, late_ref, row_ref, plane_ref, over_ref, div_ref,
    g_ref, send_out_ref, send_early_ref, send_in_ref, send_late_ref, near_ref, pay_ref,
):
    before, after = got_axial(in_ref, out_ref)
    plane, over = plane_ref[...], over_ref[...]

    def side_rows(side, comp, a):
        if a in (0, 7):
            start = 16 * comp + (8 if a else 0)
            return late_ref[side, start : start + 8]
        start = 48 * comp + 8 * (a - 1)
        return early_ref[side, start : start + 8]

    moved = []
    for comp in range(3):
        parts = []
        for a in range(8):
            value = conv_ref[comp, a]
            if a == 0:
                value = value + before(64 * comp, 64)
            if a == 7:
                value = value + after(64 * comp, 64)
            value = add_rows(value, {0: side_rows(1, comp, a), 7: side_rows(0, comp, a)})
            scale = time_increment * (0.5 if a in (0, 7) else 1.0)
            parts.append(float(WEIGHTS[a]) * plane * u_ref[comp, a] - scale * over * value)
        moved.append(parts)
    flat = product(
        div_ref,
        jnp.concatenate([jnp.concatenate(moved[1], axis=1), jnp.concatenate(moved[2], axis=1)], axis=0),
    )
    along_a = skew_apply(DERIV.T, moved[0])
    raw = [along_a[a] + flat[:, LANES * a : LANES * a + LANES] for a in range(8)]
    send_raw(raw, g_ref, send_in_ref, send_out_ref, send_early_ref, send_late_ref)
    count = row_ref.shape[0]
    width = near_ref.shape[1] // LANES
    near_ref[...] = jnp.zeros(near_ref.shape, F32)
    packed = min(count, (late_ref.shape[1] - 48) // 3)
    for i in range(3):
        start = 48 + i * packed
        middle = (before(192, count), row_ref[...], after(192, count))[i]
        sides = (late_ref[1, start : start + packed], middle, late_ref[0, start : start + packed])
        for j, rows in enumerate(sides):
            for k in range(width):
                near_ref[3 * i + j : 3 * i + j + 1, LANES * k : LANES * k + LANES] = rows[k : k + 1]
    send_sums(pay_ref, coarse_share(raw, near_ref), [])


def got_planes(g_ref, in_ref, out_ref, early_ref, late_ref):
    before, after = got_axial(in_ref, out_ref)

    def edge_rows(side, e):
        if e in (0, 1, 8, 9):
            start = 8 * (0, 1, 8, 9).index(e)
            return late_ref[side, start : start + 8]
        return early_ref[side, 8 * e - 16 : 8 * e - 8]

    def inner_rows(side, a):
        if a in (0, 7):
            start = 40 if a else 32
            return late_ref[side, start : start + 8]
        return early_ref[side, 40 + 8 * a : 48 + 8 * a]

    zero = jnp.zeros((80, LANES), F32)
    planes = []
    for e in range(10):
        if e == 0:
            value = before(64, 64)
        elif e == 9:
            value = after(64, 64)
        else:
            value = g_ref[e - 1]
        if e == 1:
            value = value + before(0, 64)
        if e == 8:
            value = value + after(0, 64)
        value = add_rows(value, {0: edge_rows(1, e), 7: edge_rows(0, e)})
        if e in (0, 9):
            rows = [value, zero]
        else:
            rows = [value, spread(value, 6, 1), inner_rows(1, e - 1), inner_rows(0, e - 1)]
        planes.append(jnp.concatenate(rows, axis=0))
    return planes


def to_part(rows):
    return radial_sum(rows[:64] + spread(rows[64:128], 1, 6)), radial_sum(rows[128:144])


def solve_ends_kernel(
    g_ref, out_ref, in_ref, early_ref, late_ref, row_ref, inverse_ref, into_ref, outof_ref,
    planes_ref, middle_ref, ends_ref, send_out_ref, send_in_ref, pass_ref,
):
    pass_ref[...] = jnp.broadcast_to(row_ref[...], pass_ref.shape)
    planes = got_planes(g_ref, in_ref, out_ref, early_ref, late_ref)
    for e in range(10):
        planes_ref[e] = planes[e]
    flat = product(into_ref, jnp.concatenate(planes, axis=1))
    parts = to_spectral([flat[:, LANES * e : LANES * e + LANES] for e in range(10)])
    parts = [parts[i] * inverse_ref[i] for i in range(10)]
    parts = from_spectral(parts)
    flat = product(outof_ref, jnp.concatenate([parts[e] for e in (0, 1, 8, 9)], axis=1))
    ends = [flat[:, LANES * k : LANES * k + LANES] for k in range(4)]
    low, low_faces = to_part(ends[1])
    high, high_faces = to_part(ends[2])
    send_axial(
        send_in_ref,
        send_out_ref,
        [low, radial_sum(ends[0][:64]), low_faces],
        [high, radial_sum(ends[3][:64]), high_faces],
    )
    for k in range(4):
        ends_ref[k] = ends[k]
    for e in range(2, 8):
        middle_ref[e - 2] = parts[e]


def solve_rest_kernel(
    middle_ref, ends_ref, outof_ref, solved_ref, part_ref, send_early_ref, send_late_ref,
):
    flat = product(outof_ref, jnp.concatenate([middle_ref[k] for k in range(6)], axis=1))
    solved = [flat[:, LANES * k : LANES * k + LANES] for k in range(6)]
    solved = [ends_ref[0], ends_ref[1]] + solved + [ends_ref[2], ends_ref[3]]
    for e in range(10):
        solved_ref[e] = solved[e]
    for a in range(8):
        value, outer_b = to_part(solved[a + 1])
        part_ref[a] = value
        for side in range(2):
            edge = value[56 * side : 56 * side + 8]
            face = outer_b[8 * side : 8 * side + 8]
            if a in (0, 1, 6, 7):
                start = 8 * (0, 1, 6, 7).index(a)
                send_late_ref[side, start : start + 8] = edge
            else:
                send_early_ref[side, 8 * a - 16 : 8 * a - 8] = edge
            if a in (0, 7):
                start = 40 if a else 32
                send_late_ref[side, start : start + 8] = face
            else:
                send_early_ref[side, 24 + 8 * a : 32 + 8 * a] = face


def solved_side_kernel(out_ref, in_ref, late_ref, row_ref, send_ref, pass_ref):
    pass_ref[...] = row_ref[...]
    before, after = got_axial(in_ref, out_ref)
    for side, b in ((0, 0), (1, 7)):
        row = 8 * b
        send_ref[side, :8] = late_ref[side, :8] + before(row, 8)
        send_ref[side, 8:16] = late_ref[side, 8:16] + before(64 + row, 8)
        send_ref[side, 16:24] = late_ref[side, 16:24] + after(64 + row, 8)
        send_ref[side, 24:32] = late_ref[side, 24:32] + after(row, 8)
        send_ref[side, 32:40] = late_ref[side, 32:40] + before(128 + 8 * side, 8)
        send_ref[side, 40:48] = late_ref[side, 40:48] + after(128 + 8 * side, 8)


def got_solved(part_ref, in_ref, out_ref, early_ref, late_ref):
    before, after = got_axial(in_ref, out_ref)
    extra = {0: (before, 0), 1: (before, 64), 6: (after, 64), 7: (after, 0)}

    def edge_rows(side, a):
        if a in extra:
            start = 8 * (0, 1, 6, 7).index(a)
            return late_ref[side, start : start + 8]
        return early_ref[side, 8 * a - 16 : 8 * a - 8]

    def face_rows(side, a):
        if a in (0, 7):
            start = 40 if a else 32
            return late_ref[side, start : start + 8]
        return early_ref[side, 24 + 8 * a : 32 + 8 * a]

    result = []
    for a in range(8):
        value = part_ref[a]
        if a in extra:
            side, start = extra[a]
            value = value + side(start, 64)
        result.append(
            add_rows(
                value,
                {0: edge_rows(1, a), 1: face_rows(1, a), 6: face_rows(0, a), 7: edge_rows(0, a)},
            )
        )
    return result


def add_coarse(parts, row, near_ref):
    values = jnp.sum(near_ref[...] * row, axis=1, keepdims=True)
    own = [[values[3 * i + j : 3 * i + j + 1] for j in range(3)] for i in range(3)]
    fields = []
    for i in range(3):
        ends = [0.5 * (own[i][1] + own[i][j]) for j in (0, 2)]
        rows = [jnp.broadcast_to(value, (8, LANES)) for value in (ends[0], own[i][1], ends[1])]
        fields.append(jnp.concatenate([rows[0]] + [rows[1]] * 6 + [rows[2]], axis=0))
    first, last = 0.5 * (fields[0] + fields[1]), 0.5 * (fields[1] + fields[2])
    return [
        parts[a] + (first if a == 0 else last if a == 7 else fields[1]) for a in range(8)
    ]


def flux_along(values, diff_ref, plane_ref):
    plane = plane_ref[...]
    slopes = skew_apply(DERIV, values)
    return [float(WEIGHTS[a]) * plane * diff_ref[a] * slopes[a] for a in range(8)]


def apply_layers(layers, values, flux, diff_ref, plane_ref, grad_ref, div_ref):
    plane = plane_ref[...]
    flat = product(grad_ref, jnp.concatenate([values[a] for a in layers], axis=1))
    across = []
    for k, a in enumerate(layers):
        coef = float(WEIGHTS[a]) * plane * diff_ref[a]
        coef = jnp.concatenate([coef, coef], axis=0)
        across.append(coef * flat[:, LANES * k : LANES * k + LANES])
    flat = product(div_ref, jnp.concatenate(across, axis=1))
    along_a = skew_apply(DERIV.T, flux, [a for a in layers if a < 4])
    return [
        along_a[a]
        + flat[:, LANES * k : LANES * k + LANES]
        + (mass_shift * float(WEIGHTS[a])) * plane * values[a]
        for k, a in enumerate(layers)
    ]


def apply_operator(values, diff_ref, plane_ref, grad_ref, div_ref):
    flux = flux_along(values, diff_ref, plane_ref)
    return apply_layers(range(8), values, flux, diff_ref, plane_ref, grad_ref, div_ref)


def dot_parts(first, second):
    result = first[0] * second[0]
    for a in range(1, 8):
        result = result + first[a] * second[a]
    return total(result)


def norm(row):
    return jnp.sum(row * row, axis=1, keepdims=True)


def dot_planes(first, second):
    result = None
    for e in range(10):
        stop = 64 if e in (0, 9) else 144
        term = first[e][:stop] * second[e][:stop]
        term = jnp.sum(term.reshape(stop // 8, 8, LANES), axis=0)
        result = term if result is None else result + term
    return total(result)


def first_apply_kernel(
    part_ref, out_ref, in_ref, early_ref, late_ref, near_ref, diff_ref, plane_ref, grad_ref, div_ref,
    sums_ref, planes_ref, solved_ref,
    z_ref, raw_ref, g_ref, send_out_ref, send_early_ref, send_in_ref, send_late_ref, row_ref, pay_ref,
):
    row, _ = got_sums(sums_ref, 0)
    values = got_solved(part_ref, in_ref, out_ref, early_ref, late_ref)
    values = add_coarse(values, row, near_ref)
    raw = apply_operator(values, diff_ref, plane_ref, grad_ref, div_ref)
    send_raw(raw, g_ref, send_in_ref, send_out_ref, send_early_ref, send_late_ref)
    for a in range(8):
        z_ref[a] = values[a]
        raw_ref[a] = raw[a]
    row_ref[0:1] = row
    scalars = [dot_planes(planes_ref, solved_ref), dot_parts(values, raw)]
    send_sums(pay_ref, coarse_share(raw, near_ref), scalars)


def first_step(sums_ref, row_ref):
    row_q, (local_rz, curv) = got_sums(sums_ref, 2)
    row_r = row_ref[0:1]
    rz = local_rz + norm(row_r)
    return row_r, row_q, rz, curv, rz / curv


END_LAYERS = (0, 1, 6, 7)


def apply_ends_kernel(
    part_ref, out_ref, in_ref, early_ref, late_ref, near_ref, diff_ref, plane_ref, grad_ref, div_ref,
    sums_ref, row_ref, z0_ref,
    y_ref, z_ref, flux_ref, ends_ref, send_out_ref, send_in_ref,
):
    _, row_q, _, _, alpha = first_step(sums_ref, row_ref)
    change = got_solved(part_ref, in_ref, out_ref, early_ref, late_ref)
    change = add_coarse(change, row_q, near_ref)
    values = [z0_ref[a] - alpha * change[a] for a in range(8)]
    flux = flux_along(values, diff_ref, plane_ref)
    ends = apply_layers(END_LAYERS, values, flux, diff_ref, plane_ref, grad_ref, div_ref)
    sent = {a: radial_sum(raw) for a, raw in zip(END_LAYERS, ends)}
    send_raw_ends(sent, send_in_ref, send_out_ref)
    for a in range(8):
        y_ref[a] = change[a]
        z_ref[a] = values[a]
        flux_ref[a] = flux[a]
    for k in range(4):
        ends_ref[k] = ends[k]


def apply_rest_kernel(
    z_ref, flux_ref, ends_ref, diff_ref, plane_ref, grad_ref, div_ref,
    raw_ref, g_ref, send_early_ref, send_late_ref,
):
    values = [z_ref[a] for a in range(8)]
    flux = [flux_ref[a] for a in range(8)]
    raw = apply_layers((2, 3, 4, 5), values, flux, diff_ref, plane_ref, grad_ref, div_ref)
    raw = [ends_ref[0], ends_ref[1]] + raw + [ends_ref[2], ends_ref[3]]
    send_raw_rest([radial_sum(part) for part in raw], g_ref, send_early_ref, send_late_ref)
    for a in range(8):
        raw_ref[a] = raw[a]


def first_dots_kernel(
    sums_ref, row_ref, near_ref, planes_r_ref, planes_q_ref, solved_r_ref, solved_q_ref,
    z_ref, raw_ref, old_raw_ref,
    planes_ref, solved_ref, pay_ref,
):
    alpha = first_step(sums_ref, row_ref)[4]
    planes, solved = [], []
    for e in range(10):
        planes.append(planes_r_ref[e] - alpha * planes_q_ref[e])
        solved.append(solved_r_ref[e] - alpha * solved_q_ref[e])
        planes_ref[e] = planes[e]
        solved_ref[e] = solved[e]
    values = [z_ref[a] for a in range(8)]
    raw = [raw_ref[a] for a in range(8)]
    scalars = [
        dot_planes(planes, solved),
        dot_planes(planes, solved_q_ref),
        dot_planes(planes_q_ref, solved),
        dot_planes(planes_q_ref, solved_q_ref),
        dot_parts(values, raw),
        dot_parts(values, [old_raw_ref[a] for a in range(8)]),
    ]
    send_sums(pay_ref, coarse_share(raw, near_ref), scalars)


def second_dots_kernel(
    row_ref, planes_r_ref, planes_q_ref, planes_w_ref, solved_r_ref, solved_q_ref, solved_w_ref,
    pay_ref,
):
    scalars = [
        dot_planes(planes_r_ref, solved_w_ref),
        dot_planes(planes_q_ref, solved_w_ref),
        dot_planes(planes_w_ref, solved_r_ref),
        dot_planes(planes_w_ref, solved_q_ref),
        dot_planes(planes_w_ref, solved_w_ref),
    ]
    row = row_ref[...]
    width = row.shape[1]
    place = lax.broadcasted_iota(jnp.int32, (1, width), 1)
    for k, value in enumerate(scalars):
        row = jnp.where(place == width - 7 - k, value, row)
    pay_ref[...] = jnp.broadcast_to(row, pay_ref.shape)


def last_kernel(
    part_ref, out_ref, in_ref, early_ref, late_ref, near_ref, sums_ref, old_sums_ref, row_ref, _,
    y_ref, z0_ref, z1_ref, planes_r_ref, planes_q_ref, planes_w_ref,
    pressure_ref, residual_ref, direction_ref,
):
    row_r, row_q, rz0, curv0, alpha0 = first_step(old_sums_ref, row_ref)
    row_w, scalars = got_sums(sums_ref, 11)
    rr, rq, qr, qq, first_curv, cross, rw, qw, wr, wq, ww = scalars
    row_r = row_r - alpha0 * row_q
    rz1 = rr + norm(row_r)
    beta0 = rz1 / rz0
    curv1 = first_curv + beta0 * (2.0 * cross + beta0 * curv0)
    alpha1 = rz1 / curv1
    row = row_w + beta0 * row_q
    row_r = row_r - alpha1 * row
    step = -alpha1 * beta0
    rz2 = (
        rr
        - alpha1 * (rw + wr)
        + step * (rq + qr)
        + alpha1 * alpha1 * ww
        - alpha1 * step * (wq + qw)
        + step * step * qq
        + norm(row_r)
    )
    beta1 = rz2 / rz1
    change = got_solved(part_ref, in_ref, out_ref, early_ref, late_ref)
    change = add_coarse(change, row_w, near_ref)
    for a in range(8):
        first = z0_ref[a]
        second = z1_ref[a] + beta0 * first
        image = planes_w_ref[a + 1, :64] + beta0 * planes_q_ref[a + 1, :64]
        residual_ref[a] = planes_r_ref[a + 1, :64] - alpha1 * image
        pressure_ref[a] = alpha0 * first + alpha1 * second
        direction_ref[a] = (
            z1_ref[a] - alpha1 * (change[a] + beta0 * y_ref[a]) + beta1 * second
        )


def kernel_call(kernel, out_shapes, *args, **options):
    outs = [jax.ShapeDtypeStruct(shape, F32) for shape in out_shapes]
    return pl.pallas_call(
        kernel,
        out_shape=outs,
        compiler_params=pltpu.CompilerParams(vmem_limit_bytes=VMEM_GRANT),
        interpret=INTERPRET,
        **options,
    )(*args)


def axial_swap(inner_rows, outer_rows):
    count = lax.axis_size("axial")
    inner = [(i, i ^ 1) for i in range(count)]
    outer = [((2 * i + 1) % count, (2 * i + 2) % count) for i in range(count // 2)]
    outer = outer + [(b, a) for a, b in outer]
    from_outer = lax.ppermute(outer_rows, "axial", outer)
    from_inner = lax.ppermute(inner_rows, "axial", inner)
    return from_inner, from_outer


def azim_swap(sides):
    count = lax.axis_size("azim")
    if count == 2:
        return lax.ppermute(sides, "azim", [(0, 1), (1, 0)])
    after = lax.ppermute(sides[0], "azim", [((i + 1) % count, i) for i in range(count)])
    before = lax.ppermute(sides[1], "azim", [(i, (i + 1) % count) for i in range(count)])
    return jnp.stack([after, before])


def sum_steps():
    azim = lax.axis_size("azim")
    count = lax.axis_size("axial") * azim
    steps, step = [], 2 * azim
    while step < count:
        steps.append(step)
        step *= 2
    step = 1
    while step < azim:
        steps.append(step)
        step *= 2
    groups = [steps[k::4] for k in range(4)]
    groups[0] = groups[0] + [azim]
    return groups


def partial_sum(row, steps):
    count = lax.axis_size("axial") * lax.axis_size("azim")
    for step in steps:
        row = row[:1] + lax.ppermute(row, ALL, [(i, i ^ step) for i in range(count)])[:1]
    return row


def gather_sums(rows):
    return lax.all_to_all(rows, ALL, 0, 0, tiled=True)


def per_device(velocity, diffusivity, coarse_factor):
    shape = diffusivity.shape
    devices = lax.axis_size("axial") * lax.axis_size("azim")
    u = velocity.reshape(3, 8, 64, LANES)
    diff = diffusivity.reshape(8, 64, LANES)
    tables = constant_tables(LANES)
    plane, over, spectrum = tables["plane"], tables["over"], tables["spectrum"]
    grad, div, into, outof = tables["grad"], tables["div"], tables["into"], tables["outof"]
    coarse_size = coarse_factor.shape[1]
    width = -(-(coarse_size + TAIL) // LANES)
    count = 8 * -(-width // 8)

    field, sums, row_shape = (8, 64, LANES), (devices, width * LANES), (8, width * LANES)
    boxes = [(10, 144, LANES), (10, 144, LANES)]
    raw_sends = [(128, LANES), (2, 96, LANES), (128, LANES), (2, 32, LANES)]

    far = pl.BlockSpec(memory_space=pltpu.HBM)
    conv, row, *sends = kernel_call(
        conv_kernel,
        [(3,) + field, (count, LANES), (192 + count, LANES), (2, 144, LANES)]
        + [(192 + count, LANES), (2, 48, LANES)],
        *(pltpu.with_memory_space_constraint(x, pltpu.HBM) for x in (u, coarse_factor, plane, grad)),
        in_specs=[far] * 4,
        scratch_shapes=[
            pltpu.VMEM((3,) + field, F32),
            pltpu.VMEM((1, coarse_size), F32),
            pltpu.VMEM(plane.shape, F32),
            pltpu.VMEM(grad.shape, BF16),
            pltpu.SemaphoreType.DMA((4,)),
        ],
    )
    (inverse,) = kernel_call(inverse_kernel, [(10, 112, LANES)], diff, spectrum)

    def exchange(side_kernel, late_rows, sends, extra, extra_shape=None):
        send_out, send_early, send_in, send_late = sends
        inner, outer = axial_swap(send_in, send_out)
        early = azim_swap(send_early)
        shapes = [(2, late_rows, LANES)]
        shapes = shapes if extra_shape is None else shapes + [extra_shape]
        late, *passed = kernel_call(side_kernel, shapes, outer, inner, send_late, extra)
        return [outer, inner, early, azim_swap(late)] + passed

    one, copies = (1, width * LANES), (SUM_ROWS, width * LANES)
    groups = sum_steps()
    moved = exchange(conv_side_kernel, 48 + 8 * -(-3 * width // 8), sends, row)
    g, *sends, near, pay = kernel_call(
        divergence_kernel,
        [field] + raw_sends + [(16, width * LANES), copies],
        moved[2], conv, u, *moved[:2], moved[3], row, plane, over, div,
    )
    solver = (inverse, into, outof)
    operator = (near, diff, plane, grad, div)

    def solve(g, moved, pay):
        ends = [(6, 112, LANES), (4, 144, LANES), (144, LANES), (144, LANES), copies]
        planes, middle, ends, send_out, send_in, pay = kernel_call(
            solve_ends_kernel, boxes[:1] + ends, g, *moved, pay, *solver
        )
        solved, part, send_early, send_late = kernel_call(
            solve_rest_kernel,
            boxes[:1] + [field, (2, 80, LANES), (2, 48, LANES)],
            middle, ends, outof,
        )
        return planes, solved, part, send_out, send_early, send_in, send_late, pay


    *moved, pay = exchange(raw_side_kernel, 48, sends, partial_sum(pay, groups[0]), one)
    pay = partial_sum(pay, groups[1])
    planes_r, solved_r, part, *sends, pay = solve(g, moved, pay)
    *moved, pay = exchange(solved_side_kernel, 48, sends, partial_sum(pay, groups[2]), one)
    pay = partial_sum(pay, groups[3])
    z0, raw0, g, *sends, row_r, pay = kernel_call(
        first_apply_kernel,
        [field, field, field] + raw_sends + [row_shape, copies],
        part, *moved, *operator, pay, planes_r, solved_r,
    )
    *moved, pay = exchange(raw_side_kernel, 48, sends, partial_sum(pay, groups[0]), one)
    pay = partial_sum(pay, groups[1])
    planes_q, solved_q, part, *sends, pay = solve(g, moved, pay)
    *moved, pay = exchange(solved_side_kernel, 48, sends, partial_sum(pay, groups[2]), one)
    first_sums = partial_sum(pay, groups[3])
    y, z1, flux, ends, send_out, send_in = kernel_call(
        apply_ends_kernel,
        [field, field, field, (4, 64, LANES), (128, LANES), (128, LANES)],
        part, *moved, *operator, first_sums, row_r, z0,
    )
    raw1, g, send_early, send_late = kernel_call(
        apply_rest_kernel,
        [field, field, (2, 96, LANES), (2, 32, LANES)],
        z1, flux, ends, diff, plane, grad, div,
    )
    sends = send_out, send_early, send_in, send_late
    planes_r, solved_r, pay = kernel_call(
        first_dots_kernel,
        boxes + [one],
        first_sums, row_r, near, planes_r, planes_q, solved_r, solved_q, z1, raw1, raw0,
    )
    *moved, pay = exchange(raw_side_kernel, 48, sends, pay, one)
    planes_w, solved_w, part, *sends, pay = solve(g, moved, pay)
    (pay,) = kernel_call(
        second_dots_kernel, [one], pay[:1], planes_r, planes_q, planes_w, solved_r, solved_q, solved_w
    )
    gathered = gather_sums(jnp.broadcast_to(pay, sums))
    *moved, passed = exchange(solved_side_kernel, 48, sends, pay, one)
    pressure, residual, direction = kernel_call(
        last_kernel,
        [field, field, field],
        part, *moved, near, gathered, first_sums, row_r, passed,
        y, z0, z1, planes_r, planes_q, planes_w,
    )
    return pressure.reshape(shape), residual.reshape(shape), direction.reshape(shape)


def solution(mesh):
    split = P(None, None, None, "axial", "azim", None)
    in_specs = (P(None, None, None, None, "axial", "azim", None), split, P(ALL, None))
    return jax.shard_map(
        per_device, mesh=mesh, in_specs=in_specs, out_specs=(split, split, split), check_vma=False
    )
```

```python
import math

import jax
import jax.numpy as jnp
import numpy as np
from jax import lax
from jax.experimental import pallas as pl
from jax.experimental.pallas import tpu as pltpu
from jax.sharding import PartitionSpec as P

ALL = ("axial", "azim")
time_increment = 0.02
mass_shift = 0.05
VMEM_GRANT = 20 << 20
TAIL = 16
SUM_ROWS = 32
gll_points = [
    -1.0,
    -0.8717401485096066,
    -0.5917001814331423,
    -0.20929921790247888,
    0.20929921790247888,
    0.5917001814331423,
    0.8717401485096066,
    1.0,
]


def legendre_value(order, point):
    before = 1.0
    current = point
    for step_idx in range(1, order):
        after = ((2 * step_idx + 1) * point * current - step_idx * before) / (step_idx + 1)
        before = current
        current = after
    return current


def jacobi_eigen(matrix):
    size_n = len(matrix)
    work = [list(row) for row in matrix]
    vectors = [
        [1.0 if row_idx == col_idx else 0.0 for col_idx in range(size_n)]
        for row_idx in range(size_n)
    ]
    for sweep_idx in range(15):
        for row_idx in range(size_n):
            for col_idx in range(row_idx + 1, size_n):
                off_value = work[row_idx][col_idx]
                if off_value != 0.0:
                    theta = (work[col_idx][col_idx] - work[row_idx][row_idx]) / (2.0 * off_value)
                    root_val = math.sqrt(theta * theta + 1.0)
                    tangent = 1.0 / (theta + root_val) if theta >= 0.0 else 1.0 / (theta - root_val)
                    cosine = 1.0 / math.sqrt(tangent * tangent + 1.0)
                    sine = tangent * cosine
                    for other in range(size_n):
                        left_val = work[other][row_idx]
                        right_val = work[other][col_idx]
                        work[other][row_idx] = cosine * left_val - sine * right_val
                        work[other][col_idx] = sine * left_val + cosine * right_val
                    for other in range(size_n):
                        left_val = work[row_idx][other]
                        right_val = work[col_idx][other]
                        work[row_idx][other] = cosine * left_val - sine * right_val
                        work[col_idx][other] = sine * left_val + cosine * right_val
                    for other in range(size_n):
                        left_val = vectors[other][row_idx]
                        right_val = vectors[other][col_idx]
                        vectors[other][row_idx] = cosine * left_val - sine * right_val
                        vectors[other][col_idx] = sine * left_val + cosine * right_val
    return ([work[row_idx][row_idx] for row_idx in range(size_n)], vectors)


def gll_tables():
    degree = 7
    points = degree + 1
    legendre_at = [legendre_value(degree, node_val) for node_val in gll_points]
    weights = [2.0 / (degree * (degree + 1) * value * value) for value in legendre_at]
    derivative = [[0.0] * points for row_idx in range(points)]
    for row_idx in range(points):
        for col_idx in range(points):
            if row_idx != col_idx:
                derivative[row_idx][col_idx] = legendre_at[row_idx] / (
                    legendre_at[col_idx] * (gll_points[row_idx] - gll_points[col_idx])
                )
    derivative[0][0] = -degree * (degree + 1) / 4.0
    derivative[degree][degree] = degree * (degree + 1) / 4.0
    stiffness = [
        [
            sum(
                (
                    derivative[mid_idx][row_idx] * weights[mid_idx] * derivative[mid_idx][col_idx]
                    for mid_idx in range(points)
                )
            )
            for col_idx in range(points)
        ]
        for row_idx in range(points)
    ]
    line_len = 3 * degree + 1
    big_stiff = [[0.0] * line_len for row_idx in range(line_len)]
    big_mass = [0.0] * line_len
    for element in range(3):
        offset = element * degree
        for row_idx in range(points):
            big_mass[offset + row_idx] += weights[row_idx]
            for col_idx in range(points):
                big_stiff[offset + row_idx][offset + col_idx] += stiffness[row_idx][col_idx]
    start_node = degree - 1
    box_len = degree + 3
    scaling = [1.0 / math.sqrt(big_mass[start_node + row_idx]) for row_idx in range(box_len)]
    symmetric = [
        [
            scaling[row_idx]
            * big_stiff[start_node + row_idx][start_node + col_idx]
            * scaling[col_idx]
            for col_idx in range(box_len)
        ]
        for row_idx in range(box_len)
    ]
    eigval, eigvec = jacobi_eigen(symmetric)
    fdm_basis = [
        [scaling[row_idx] * eigvec[row_idx][col_idx] for col_idx in range(box_len)]
        for row_idx in range(box_len)
    ]
    return (weights, derivative, fdm_basis, eigval)

WEIGHTS, DERIV, BASIS, EIGVAL = (np.asarray(t, np.float64) for t in gll_tables())


def f32(table):
    return jnp.asarray(table, jnp.float32)


F32 = jnp.float32
BF16 = jnp.bfloat16
LANES = 128
INTERPRET = False


def split_terms(table, depth):
    padded = np.zeros((table.shape[0], depth))
    padded[:, : table.shape[1]] = table
    high = padded.astype(jnp.bfloat16)
    low = (padded - high.astype(np.float64)).astype(jnp.bfloat16)
    return jnp.asarray(np.concatenate([high, high, low], axis=1))


def box_tables():
    pairs = [(b + 1, c + 1) for b in range(8) for c in range(8)]
    pairs += [(b + 1, {6: 0, 1: 9}.get(c)) for b in range(8) for c in range(8)]
    pairs += [(0, c + 1) for c in range(8)] + [(9, c + 1) for c in range(8)]
    table = np.zeros((144, 112))
    for row, (b, c) in enumerate(pairs):
        if c is not None:
            table[row, :100] = np.outer(BASIS[b], BASIS[c]).reshape(100)
    sums = np.ones(112)
    sums[:100] = (EIGVAL[:, None] + EIGVAL[None, :]).reshape(100)
    return table, sums


EYE = np.eye(8)
GRAD = np.concatenate([np.kron(DERIV, EYE), np.kron(EYE, DERIV)])
BOX_ROWS, SPECTRUM = box_tables()
EVEN = [bool(abs(BASIS[0, i] - BASIS[9, i]) < abs(BASIS[0, i] + BASIS[9, i])) for i in range(10)]


def constant_tables(radial):
    plane = (WEIGHTS[:, None] * WEIGHTS[None, :]).reshape(64, 1)
    mult_r = np.ones((8, radial))
    mult_r[0, 1:] = 2.0
    mult_r[7, :-1] = 2.0
    ends = np.array([2.0, 1, 1, 1, 1, 1, 1, 2.0])
    mult = (ends[:, None, None] * mult_r[None]).reshape(64, radial)
    return dict(
        plane=f32(np.broadcast_to(plane, (64, radial))),
        over=f32(1.0 / mult),
        spectrum=f32(np.broadcast_to(SPECTRUM[:, None], (112, radial))),
        grad=split_terms(GRAD, 64),
        div=split_terms(GRAD.T, 128),
        into=split_terms(BOX_ROWS.T, 144),
        outof=split_terms(BOX_ROWS, 112),
    )


def product(table_ref, values):
    high = values.astype(BF16)
    low = (values - high.astype(F32)).astype(BF16)
    return jnp.dot(
        table_ref[...], jnp.concatenate([high, low, high], axis=0), preferred_element_type=F32
    )


def combine(coefs, terms):
    total = None
    for coef, term in zip(coefs, terms):
        scaled = float(coef) * term
        total = scaled if total is None else total + scaled
    return total


def skew_apply(matrix, parts, rows=range(4)):
    plus = [parts[b] + parts[7 - b] for b in range(4)]
    minus = [parts[b] - parts[7 - b] for b in range(4)]
    result = [None] * 8
    for a in rows:
        even = combine([0.5 * (matrix[a, b] + matrix[a, 7 - b]) for b in range(4)], plus)
        odd = combine([0.5 * (matrix[a, b] - matrix[a, 7 - b]) for b in range(4)], minus)
        result[a] = even + odd
        result[7 - a] = odd - even
    return result


def to_spectral(parts):
    plus = [parts[a] + parts[9 - a] for a in range(5)]
    minus = [parts[a] - parts[9 - a] for a in range(5)]
    return [combine(BASIS[:5, i], plus if EVEN[i] else minus) for i in range(10)]


def from_spectral(parts):
    evens = [i for i in range(10) if EVEN[i]]
    odds = [i for i in range(10) if not EVEN[i]]
    result = [None] * 10
    for a in range(5):
        even = combine(BASIS[a, evens], [parts[i] for i in evens])
        odd = combine(BASIS[a, odds], [parts[i] for i in odds])
        result[a] = even + odd
        result[9 - a] = even - odd
    return result


def masks():
    layer = lax.broadcasted_iota(jnp.int32, (8, LANES), 0)
    elem = lax.broadcasted_iota(jnp.int32, (8, LANES), 1)
    return layer, elem > 0, elem < LANES - 1


def spread(values, first, last):
    layer, has_before, has_after = masks()
    cubes = values.reshape(values.shape[0] // 8, 8, LANES)
    before = pltpu.roll(cubes, 1, axis=2)
    after = pltpu.roll(cubes, LANES - 1, axis=2)
    before_mask = ((layer == first) & has_before)[None]
    after_mask = ((layer == last) & has_after)[None]
    result = jnp.where(before_mask, before, jnp.where(after_mask, after, 0.0))
    return result.reshape(values.shape)


def radial_sum(values):
    layer, has_before, has_after = masks()
    cubes = values.reshape(values.shape[0] // 8, 8, LANES)
    up = pltpu.roll(cubes, 1, axis=1)
    down = pltpu.roll(cubes, 7, axis=1)
    ends = jnp.where((layer == 0)[None], up, down)
    before = pltpu.roll(ends, 1, axis=2)
    after = pltpu.roll(ends, LANES - 1, axis=2)
    before_mask = ((layer == 0) & has_before)[None]
    after_mask = ((layer == 7) & has_after)[None]
    ends = jnp.where(before_mask, before, jnp.where(after_mask, after, 0.0))
    return (cubes + ends).reshape(values.shape)


def total(values):
    return jnp.sum(values, axis=(0, 1), keepdims=True)


def add_rows(block, extra):
    pieces = []
    for b in range(8):
        piece = block[8 * b : 8 * b + 8]
        pieces.append(piece + extra[b] if b in extra else piece)
    return jnp.concatenate(pieces, axis=0)


def is_even():
    return lax.axis_index("axial") % 2 == 0


def send_axial(inner_ref, outer_ref, low, high):
    even = is_even()
    row = 0
    for low_piece, high_piece in zip(low, high):
        size = low_piece.shape[0]
        inner_ref[row : row + size] = jnp.where(even, high_piece, low_piece)
        outer_ref[row : row + size] = jnp.where(even, low_piece, high_piece)
        row += size


def got_axial(inner_ref, outer_ref):
    even = is_even()

    def before(start, size):
        return jnp.where(even, outer_ref[start : start + size], inner_ref[start : start + size])

    def after(start, size):
        return jnp.where(even, inner_ref[start : start + size], outer_ref[start : start + size])

    return before, after


def conv_kernel(
    u_hbm, row_hbm, plane_hbm, grad_hbm,
    conv_ref, row_ref, out_ref, early_ref, in_ref, late_ref,
    u_ref, small_ref, plane_ref, grad_ref, sems,
):
    copies = [
        pltpu.make_async_copy(source, target, sems.at[k])
        for k, (source, target) in enumerate(
            ((u_hbm, u_ref), (plane_hbm, plane_ref), (grad_hbm, grad_ref), (row_hbm, small_ref))
        )
    ]
    for copy in copies:
        copy.start()
    row_ref[...] = jnp.zeros(row_ref.shape, F32)
    for copy in copies:
        copy.wait()
    size = small_ref.shape[1]
    for k in range(-(-size // LANES)):
        stop = min(LANES, size - LANES * k)
        row_ref[k : k + 1, :stop] = small_ref[:, LANES * k : LANES * k + stop]
    plane = plane_ref[...]
    fields = [[u_ref[d, a] for a in range(8)] for d in range(3)]
    low, high = [], []
    for comp in range(3):
        parts = fields[comp]
        flat = product(grad_ref, jnp.concatenate(parts, axis=1))
        along_a = skew_apply(DERIV, parts)
        for a in range(8):
            cols = slice(LANES * a, LANES * a + LANES)
            value = (
                fields[0][a] * along_a[a]
                + fields[1][a] * flat[:64, cols]
                + fields[2][a] * flat[64:, cols]
            )
            value = radial_sum(float(WEIGHTS[a]) * plane * value)
            conv_ref[comp, a] = value
            for side, rows in enumerate((value[:8], value[56:])):
                if a in (0, 7):
                    start = 16 * comp + (8 if a else 0)
                    late_ref[side, start : start + 8] = rows
                else:
                    start = 48 * comp + 8 * (a - 1)
                    early_ref[side, start : start + 8] = rows
            if a == 0:
                low.append(value)
            if a == 7:
                high.append(value)
    row = row_ref[...]
    send_axial(in_ref, out_ref, low + [row], high + [row])


def inverse_kernel(diff_ref, spectrum_ref, inverse_ref):
    mean = diff_ref[0]
    for a in range(1, 8):
        mean = mean + diff_ref[a]
    kbar = jnp.sum(mean, axis=0, keepdims=True) * (1.0 / 512.0)
    plane_spectrum = kbar * spectrum_ref[...] + mass_shift
    for i in range(10):
        inverse_ref[i] = 1.0 / (plane_spectrum + float(EIGVAL[i]) * kbar)


def conv_side_kernel(out_ref, in_ref, late_ref, row_ref, send_ref):
    before, after = got_axial(in_ref, out_ref)
    count = row_ref.shape[0]
    for side, b in ((0, 0), (1, 7)):
        for comp in range(3):
            first = slice(16 * comp, 16 * comp + 8)
            last = slice(16 * comp + 8, 16 * comp + 16)
            row = 64 * comp + 8 * b
            send_ref[side, first] = late_ref[side, first] + before(row, 8)
            send_ref[side, last] = late_ref[side, last] + after(row, 8)
        send_ref[side, 48:] = jnp.zeros((send_ref.shape[1] - 48, LANES), F32)
        for place, rows in enumerate((before(192, count), row_ref[...], after(192, count))):
            width = min(count, (send_ref.shape[1] - 48) // 3)
            start = 48 + place * width
            send_ref[side, start : start + width] = rows[:width]


def coarse_share(raw, near_ref):
    middle = raw[1]
    for a in range(2, 7):
        middle = middle + raw[a]
    per_axial = (0.5 * raw[0], middle + 0.5 * (raw[0] + raw[7]), 0.5 * raw[7])
    rows = []
    for part in per_axial:
        inner = part[8:16]
        for b in range(2, 7):
            inner = inner + part[8 * b : 8 * b + 8]
        ends = (part[:8], part[56:])
        for piece in (0.5 * ends[0], inner + 0.5 * (ends[0] + ends[1]), 0.5 * ends[1]):
            rows.append(jnp.sum(piece, axis=0, keepdims=True))
    rows = jnp.concatenate(rows + [jnp.zeros((7, LANES), F32)], axis=0)
    shares = jnp.sum(rows, axis=1, keepdims=True)
    return jnp.sum(shares * near_ref[...], axis=0, keepdims=True)


def send_sums(pay_ref, row, scalars):
    width = pay_ref.shape[1]
    place = lax.broadcasted_iota(jnp.int32, (1, width), 1)
    for k, value in enumerate(scalars):
        row = jnp.where(place == width - 1 - k, value, row)
    pay_ref[...] = jnp.broadcast_to(row, pay_ref.shape)


def got_sums(ref, scalars):
    row = jnp.sum(ref[...], axis=0, keepdims=True)
    width = row.shape[1]
    place = lax.broadcasted_iota(jnp.int32, (1, width), 1)
    values = [
        jnp.sum(jnp.where(place == width - 1 - k, row, 0.0), axis=1, keepdims=True)
        for k in range(scalars)
    ]
    return jnp.where(place >= width - TAIL, 0.0, row), values


def send_raw_ends(parts, in_ref, out_ref):
    send_axial(in_ref, out_ref, [parts[0], parts[1]], [parts[7], parts[6]])


def send_raw_rest(parts, g_ref, early_ref, late_ref):
    for a in range(8):
        g_ref[a] = parts[a]
    for side, (edge, inner) in enumerate(((0, 1), (7, 6))):
        edges = [part[8 * edge : 8 * edge + 8] for part in parts]
        inners = [part[8 * inner : 8 * inner + 8] for part in parts]
        for a in range(1, 7):
            early_ref[side, 8 * a - 8 : 8 * a] = edges[a]
            early_ref[side, 40 + 8 * a : 48 + 8 * a] = inners[a]
        late_ref[side, :8] = edges[0]
        late_ref[side, 8:16] = edges[7]
        late_ref[side, 16:24] = inners[0]
        late_ref[side, 24:32] = inners[7]


def send_raw(raw, g_ref, in_ref, out_ref, early_ref, late_ref):
    parts = [radial_sum(raw[a]) for a in range(8)]
    send_raw_ends(parts, in_ref, out_ref)
    send_raw_rest(parts, g_ref, early_ref, late_ref)


def raw_side_kernel(out_ref, in_ref, late_ref, row_ref, send_ref, pass_ref):
    pass_ref[...] = row_ref[...]
    before, after = got_axial(in_ref, out_ref)
    for side, (edge, inner) in enumerate(((0, 1), (7, 6))):
        send_ref[side, :8] = before(64 + 8 * edge, 8)
        send_ref[side, 8:16] = late_ref[side, :8] + before(8 * edge, 8)
        send_ref[side, 16:24] = late_ref[side, 8:16] + after(8 * edge, 8)
        send_ref[side, 24:32] = after(64 + 8 * edge, 8)
        send_ref[side, 32:40] = late_ref[side, 16:24] + before(8 * inner, 8)
        send_ref[side, 40:48] = late_ref[side, 24:32] + after(8 * inner, 8)


def divergence_kernel(
    early_ref, conv_ref, u_ref, out_ref, in_ref, late_ref, row_ref, plane_ref, over_ref, div_ref,
    g_ref, send_out_ref, send_early_ref, send_in_ref, send_late_ref, near_ref, pay_ref,
):
    before, after = got_axial(in_ref, out_ref)
    plane, over = plane_ref[...], over_ref[...]

    def side_rows(side, comp, a):
        if a in (0, 7):
            start = 16 * comp + (8 if a else 0)
            return late_ref[side, start : start + 8]
        start = 48 * comp + 8 * (a - 1)
        return early_ref[side, start : start + 8]

    moved = []
    for comp in range(3):
        parts = []
        for a in range(8):
            value = conv_ref[comp, a]
            if a == 0:
                value = value + before(64 * comp, 64)
            if a == 7:
                value = value + after(64 * comp, 64)
            value = add_rows(value, {0: side_rows(1, comp, a), 7: side_rows(0, comp, a)})
            scale = time_increment * (0.5 if a in (0, 7) else 1.0)
            parts.append(float(WEIGHTS[a]) * plane * u_ref[comp, a] - scale * over * value)
        moved.append(parts)
    flat = product(
        div_ref,
        jnp.concatenate([jnp.concatenate(moved[1], axis=1), jnp.concatenate(moved[2], axis=1)], axis=0),
    )
    along_a = skew_apply(DERIV.T, moved[0])
    raw = [along_a[a] + flat[:, LANES * a : LANES * a + LANES] for a in range(8)]
    send_raw(raw, g_ref, send_in_ref, send_out_ref, send_early_ref, send_late_ref)
    count = row_ref.shape[0]
    width = near_ref.shape[1] // LANES
    near_ref[...] = jnp.zeros(near_ref.shape, F32)
    packed = min(count, (late_ref.shape[1] - 48) // 3)
    for i in range(3):
        start = 48 + i * packed
        middle = (before(192, count), row_ref[...], after(192, count))[i]
        sides = (late_ref[1, start : start + packed], middle, late_ref[0, start : start + packed])
        for j, rows in enumerate(sides):
            for k in range(width):
                near_ref[3 * i + j : 3 * i + j + 1, LANES * k : LANES * k + LANES] = rows[k : k + 1]
    send_sums(pay_ref, coarse_share(raw, near_ref), [])


def got_planes(g_ref, in_ref, out_ref, early_ref, late_ref):
    before, after = got_axial(in_ref, out_ref)

    def edge_rows(side, e):
        if e in (0, 1, 8, 9):
            start = 8 * (0, 1, 8, 9).index(e)
            return late_ref[side, start : start + 8]
        return early_ref[side, 8 * e - 16 : 8 * e - 8]

    def inner_rows(side, a):
        if a in (0, 7):
            start = 40 if a else 32
            return late_ref[side, start : start + 8]
        return early_ref[side, 40 + 8 * a : 48 + 8 * a]

    zero = jnp.zeros((80, LANES), F32)
    planes = []
    for e in range(10):
        if e == 0:
            value = before(64, 64)
        elif e == 9:
            value = after(64, 64)
        else:
            value = g_ref[e - 1]
        if e == 1:
            value = value + before(0, 64)
        if e == 8:
            value = value + after(0, 64)
        value = add_rows(value, {0: edge_rows(1, e), 7: edge_rows(0, e)})
        if e in (0, 9):
            rows = [value, zero]
        else:
            rows = [value, spread(value, 6, 1), inner_rows(1, e - 1), inner_rows(0, e - 1)]
        planes.append(jnp.concatenate(rows, axis=0))
    return planes


def to_part(rows):
    return radial_sum(rows[:64] + spread(rows[64:128], 1, 6)), radial_sum(rows[128:144])


def solve_ends_kernel(
    g_ref, out_ref, in_ref, early_ref, late_ref, row_ref, inverse_ref, into_ref, outof_ref,
    planes_ref, middle_ref, ends_ref, send_out_ref, send_in_ref, pass_ref,
):
    pass_ref[...] = jnp.broadcast_to(row_ref[...], pass_ref.shape)
    planes = got_planes(g_ref, in_ref, out_ref, early_ref, late_ref)
    for e in range(10):
        planes_ref[e] = planes[e]
    flat = product(into_ref, jnp.concatenate(planes, axis=1))
    parts = to_spectral([flat[:, LANES * e : LANES * e + LANES] for e in range(10)])
    parts = [parts[i] * inverse_ref[i] for i in range(10)]
    parts = from_spectral(parts)
    flat = product(outof_ref, jnp.concatenate([parts[e] for e in (0, 1, 8, 9)], axis=1))
    ends = [flat[:, LANES * k : LANES * k + LANES] for k in range(4)]
    low, low_faces = to_part(ends[1])
    high, high_faces = to_part(ends[2])
    send_axial(
        send_in_ref,
        send_out_ref,
        [low, radial_sum(ends[0][:64]), low_faces],
        [high, radial_sum(ends[3][:64]), high_faces],
    )
    for k in range(4):
        ends_ref[k] = ends[k]
    for e in range(2, 8):
        middle_ref[e - 2] = parts[e]


def solve_rest_kernel(
    middle_ref, ends_ref, outof_ref, solved_ref, part_ref, send_early_ref, send_late_ref,
):
    flat = product(outof_ref, jnp.concatenate([middle_ref[k] for k in range(6)], axis=1))
    solved = [flat[:, LANES * k : LANES * k + LANES] for k in range(6)]
    solved = [ends_ref[0], ends_ref[1]] + solved + [ends_ref[2], ends_ref[3]]
    for e in range(10):
        solved_ref[e] = solved[e]
    for a in range(8):
        value, outer_b = to_part(solved[a + 1])
        part_ref[a] = value
        for side in range(2):
            edge = value[56 * side : 56 * side + 8]
            face = outer_b[8 * side : 8 * side + 8]
            if a in (0, 1, 6, 7):
                start = 8 * (0, 1, 6, 7).index(a)
                send_late_ref[side, start : start + 8] = edge
            else:
                send_early_ref[side, 8 * a - 16 : 8 * a - 8] = edge
            if a in (0, 7):
                start = 40 if a else 32
                send_late_ref[side, start : start + 8] = face
            else:
                send_early_ref[side, 24 + 8 * a : 32 + 8 * a] = face


def solved_side_kernel(out_ref, in_ref, late_ref, row_ref, send_ref, pass_ref):
    pass_ref[...] = row_ref[...]
    before, after = got_axial(in_ref, out_ref)
    for side, b in ((0, 0), (1, 7)):
        row = 8 * b
        send_ref[side, :8] = late_ref[side, :8] + before(row, 8)
        send_ref[side, 8:16] = late_ref[side, 8:16] + before(64 + row, 8)
        send_ref[side, 16:24] = late_ref[side, 16:24] + after(64 + row, 8)
        send_ref[side, 24:32] = late_ref[side, 24:32] + after(row, 8)
        send_ref[side, 32:40] = late_ref[side, 32:40] + before(128 + 8 * side, 8)
        send_ref[side, 40:48] = late_ref[side, 40:48] + after(128 + 8 * side, 8)


def last_side_kernel(out_ref, in_ref, late_ref, row_ref, bulk_ref, send_ref, pass_ref):
    send_ref[:, 48:] = bulk_ref[...]
    solved_side_kernel(out_ref, in_ref, late_ref, row_ref, send_ref, pass_ref)


def got_solved(part_ref, in_ref, out_ref, early_ref, late_ref):
    before, after = got_axial(in_ref, out_ref)
    extra = {0: (before, 0), 1: (before, 64), 6: (after, 64), 7: (after, 0)}

    def edge_rows(side, a):
        if a in extra:
            start = 8 * (0, 1, 6, 7).index(a)
            return late_ref[side, start : start + 8]
        return early_ref[side, 8 * a - 16 : 8 * a - 8]

    def face_rows(side, a):
        if a in (0, 7):
            start = 40 if a else 32
            return late_ref[side, start : start + 8]
        return early_ref[side, 24 + 8 * a : 32 + 8 * a]

    result = []
    for a in range(8):
        value = part_ref[a]
        if a in extra:
            side, start = extra[a]
            value = value + side(start, 64)
        result.append(
            add_rows(
                value,
                {0: edge_rows(1, a), 1: face_rows(1, a), 6: face_rows(0, a), 7: edge_rows(0, a)},
            )
        )
    return result


def add_coarse(parts, row, near_ref):
    values = jnp.sum(near_ref[...] * row, axis=1, keepdims=True)
    own = [[values[3 * i + j : 3 * i + j + 1] for j in range(3)] for i in range(3)]
    fields = []
    for i in range(3):
        ends = [0.5 * (own[i][1] + own[i][j]) for j in (0, 2)]
        rows = [jnp.broadcast_to(value, (8, LANES)) for value in (ends[0], own[i][1], ends[1])]
        fields.append(jnp.concatenate([rows[0]] + [rows[1]] * 6 + [rows[2]], axis=0))
    first, last = 0.5 * (fields[0] + fields[1]), 0.5 * (fields[1] + fields[2])
    return [
        parts[a] + (first if a == 0 else last if a == 7 else fields[1]) for a in range(8)
    ]


def flux_along(values, diff_ref, plane_ref):
    plane = plane_ref[...]
    slopes = skew_apply(DERIV, values)
    return [float(WEIGHTS[a]) * plane * diff_ref[a] * slopes[a] for a in range(8)]


def apply_layers(layers, values, flux, diff_ref, plane_ref, grad_ref, div_ref):
    plane = plane_ref[...]
    flat = product(grad_ref, jnp.concatenate([values[a] for a in layers], axis=1))
    across = []
    for k, a in enumerate(layers):
        coef = float(WEIGHTS[a]) * plane * diff_ref[a]
        coef = jnp.concatenate([coef, coef], axis=0)
        across.append(coef * flat[:, LANES * k : LANES * k + LANES])
    flat = product(div_ref, jnp.concatenate(across, axis=1))
    along_a = skew_apply(DERIV.T, flux, [a for a in layers if a < 4])
    return [
        along_a[a]
        + flat[:, LANES * k : LANES * k + LANES]
        + (mass_shift * float(WEIGHTS[a])) * plane * values[a]
        for k, a in enumerate(layers)
    ]


def apply_operator(values, diff_ref, plane_ref, grad_ref, div_ref):
    flux = flux_along(values, diff_ref, plane_ref)
    return apply_layers(range(8), values, flux, diff_ref, plane_ref, grad_ref, div_ref)


def dot_parts(first, second):
    result = first[0] * second[0]
    for a in range(1, 8):
        result = result + first[a] * second[a]
    return total(result)


def norm(row):
    return jnp.sum(row * row, axis=1, keepdims=True)


def dot_planes(first, second):
    result = None
    for e in range(10):
        stop = 64 if e in (0, 9) else 144
        term = first[e][:stop] * second[e][:stop]
        term = jnp.sum(term.reshape(stop // 8, 8, LANES), axis=0)
        result = term if result is None else result + term
    return total(result)


def first_apply_kernel(
    part_ref, out_ref, in_ref, early_ref, late_ref, near_ref, diff_ref, plane_ref, grad_ref, div_ref,
    sums_ref, planes_ref, solved_ref,
    z_ref, raw_ref, g_ref, send_out_ref, send_early_ref, send_in_ref, send_late_ref, row_ref, pay_ref,
):
    row, _ = got_sums(sums_ref, 0)
    values = got_solved(part_ref, in_ref, out_ref, early_ref, late_ref)
    values = add_coarse(values, row, near_ref)
    raw = apply_operator(values, diff_ref, plane_ref, grad_ref, div_ref)
    send_raw(raw, g_ref, send_in_ref, send_out_ref, send_early_ref, send_late_ref)
    for a in range(8):
        z_ref[a] = values[a]
        raw_ref[a] = raw[a]
    row_ref[0:1] = row
    scalars = [dot_planes(planes_ref, solved_ref), dot_parts(values, raw)]
    send_sums(pay_ref, coarse_share(raw, near_ref), scalars)


def first_step(sums_ref, row_ref):
    row_q, (local_rz, curv) = got_sums(sums_ref, 2)
    row_r = row_ref[0:1]
    rz = local_rz + norm(row_r)
    return row_r, row_q, rz, curv, rz / curv


END_LAYERS = (0, 1, 6, 7)


def apply_ends_kernel(
    part_ref, out_ref, in_ref, early_ref, late_ref, near_ref, diff_ref, plane_ref, grad_ref, div_ref,
    sums_ref, row_ref, z0_ref,
    y_ref, z_ref, flux_ref, ends_ref, send_out_ref, send_in_ref,
):
    _, row_q, _, _, alpha = first_step(sums_ref, row_ref)
    change = got_solved(part_ref, in_ref, out_ref, early_ref, late_ref)
    change = add_coarse(change, row_q, near_ref)
    values = [z0_ref[a] - alpha * change[a] for a in range(8)]
    flux = flux_along(values, diff_ref, plane_ref)
    ends = apply_layers(END_LAYERS, values, flux, diff_ref, plane_ref, grad_ref, div_ref)
    sent = {a: radial_sum(raw) for a, raw in zip(END_LAYERS, ends)}
    send_raw_ends(sent, send_in_ref, send_out_ref)
    for a in range(8):
        y_ref[a] = change[a]
        z_ref[a] = values[a]
        flux_ref[a] = flux[a]
    for k in range(4):
        ends_ref[k] = ends[k]


def apply_rest_kernel(
    z_ref, flux_ref, ends_ref, diff_ref, plane_ref, grad_ref, div_ref,
    raw_ref, g_ref, send_early_ref, send_late_ref,
):
    values = [z_ref[a] for a in range(8)]
    flux = [flux_ref[a] for a in range(8)]
    raw = apply_layers((2, 3, 4, 5), values, flux, diff_ref, plane_ref, grad_ref, div_ref)
    raw = [ends_ref[0], ends_ref[1]] + raw + [ends_ref[2], ends_ref[3]]
    send_raw_rest([radial_sum(part) for part in raw], g_ref, send_early_ref, send_late_ref)
    for a in range(8):
        raw_ref[a] = raw[a]


def first_dots_kernel(
    sums_ref, row_ref, near_ref, planes_r_ref, planes_q_ref, solved_r_ref, solved_q_ref,
    z_ref, raw_ref, old_raw_ref,
    planes_ref, solved_ref, pay_ref,
):
    alpha = first_step(sums_ref, row_ref)[4]
    planes, solved = [], []
    for e in range(10):
        planes.append(planes_r_ref[e] - alpha * planes_q_ref[e])
        solved.append(solved_r_ref[e] - alpha * solved_q_ref[e])
        planes_ref[e] = planes[e]
        solved_ref[e] = solved[e]
    values = [z_ref[a] for a in range(8)]
    raw = [raw_ref[a] for a in range(8)]
    scalars = [
        dot_planes(planes, solved),
        dot_planes(planes, solved_q_ref),
        dot_planes(planes_q_ref, solved),
        dot_planes(planes_q_ref, solved_q_ref),
        dot_parts(values, raw),
        dot_parts(values, [old_raw_ref[a] for a in range(8)]),
    ]
    send_sums(pay_ref, coarse_share(raw, near_ref), scalars)


def second_dots_kernel(
    row_ref, planes_r_ref, planes_q_ref, planes_w_ref, solved_r_ref, solved_q_ref, solved_w_ref,
    pay_ref,
):
    scalars = [
        dot_planes(planes_r_ref, solved_w_ref),
        dot_planes(planes_q_ref, solved_w_ref),
        dot_planes(planes_w_ref, solved_r_ref),
        dot_planes(planes_w_ref, solved_q_ref),
        dot_planes(planes_w_ref, solved_w_ref),
    ]
    row = row_ref[...]
    width = row.shape[1]
    place = lax.broadcasted_iota(jnp.int32, (1, width), 1)
    for k, value in enumerate(scalars):
        row = jnp.where(place == width - 7 - k, value, row)
    pay_ref[...] = jnp.broadcast_to(row, pay_ref.shape)


def last_kernel(
    part_ref, out_ref, in_ref, late_ref, near_ref, sums_ref, old_sums_ref, row_ref, _,
    y_ref, z0_ref, z1_ref, planes_r_ref, planes_q_ref, planes_w_ref,
    pressure_ref, residual_ref, direction_ref,
):
    row_r, row_q, rz0, curv0, alpha0 = first_step(old_sums_ref, row_ref)
    row_w, scalars = got_sums(sums_ref, 11)
    rr, rq, qr, qq, first_curv, cross, rw, qw, wr, wq, ww = scalars
    row_r = row_r - alpha0 * row_q
    rz1 = rr + norm(row_r)
    beta0 = rz1 / rz0
    curv1 = first_curv + beta0 * (2.0 * cross + beta0 * curv0)
    alpha1 = rz1 / curv1
    row = row_w + beta0 * row_q
    row_r = row_r - alpha1 * row
    step = -alpha1 * beta0
    rz2 = (
        rr
        - alpha1 * (rw + wr)
        + step * (rq + qr)
        + alpha1 * alpha1 * ww
        - alpha1 * step * (wq + qw)
        + step * step * qq
        + norm(row_r)
    )
    beta1 = rz2 / rz1
    change = got_solved(part_ref, in_ref, out_ref, late_ref.at[:, 48:], late_ref)
    change = add_coarse(change, row_w, near_ref)
    for a in range(8):
        first = z0_ref[a]
        second = z1_ref[a] + beta0 * first
        image = planes_w_ref[a + 1, :64] + beta0 * planes_q_ref[a + 1, :64]
        residual_ref[a] = planes_r_ref[a + 1, :64] - alpha1 * image
        pressure_ref[a] = alpha0 * first + alpha1 * second
        direction_ref[a] = (
            z1_ref[a] - alpha1 * (change[a] + beta0 * y_ref[a]) + beta1 * second
        )


def kernel_call(kernel, out_shapes, *args, **options):
    outs = [jax.ShapeDtypeStruct(shape, F32) for shape in out_shapes]
    return pl.pallas_call(
        kernel,
        out_shape=outs,
        compiler_params=pltpu.CompilerParams(vmem_limit_bytes=VMEM_GRANT),
        interpret=INTERPRET,
        **options,
    )(*args)


def axial_swap(inner_rows, outer_rows):
    count = lax.axis_size("axial")
    inner = [(i, i ^ 1) for i in range(count)]
    outer = [((2 * i + 1) % count, (2 * i + 2) % count) for i in range(count // 2)]
    outer = outer + [(b, a) for a, b in outer]
    from_outer = lax.ppermute(outer_rows, "axial", outer)
    from_inner = lax.ppermute(inner_rows, "axial", inner)
    return from_inner, from_outer


def azim_swap(sides):
    count = lax.axis_size("azim")
    if count == 2:
        return lax.ppermute(sides, "azim", [(0, 1), (1, 0)])
    after = lax.ppermute(sides[0], "azim", [((i + 1) % count, i) for i in range(count)])
    before = lax.ppermute(sides[1], "azim", [(i, (i + 1) % count) for i in range(count)])
    return jnp.stack([after, before])


def sum_steps():
    azim = lax.axis_size("azim")
    count = lax.axis_size("axial") * azim
    steps, step = [], 2 * azim
    while step < count:
        steps.append(step)
        step *= 2
    step = 1
    while step < azim:
        steps.append(step)
        step *= 2
    groups = [steps[k::4] for k in range(4)]
    groups[0] = groups[0] + [azim]
    return groups


def partial_sum(row, steps):
    count = lax.axis_size("axial") * lax.axis_size("azim")
    for step in steps:
        row = row[:1] + lax.ppermute(row, ALL, [(i, i ^ step) for i in range(count)])[:1]
    return row


def gather_sums(rows):
    return lax.all_to_all(rows, ALL, 0, 0, tiled=True)


def per_device(velocity, diffusivity, coarse_factor):
    shape = diffusivity.shape
    devices = lax.axis_size("axial") * lax.axis_size("azim")
    u = velocity.reshape(3, 8, 64, LANES)
    diff = diffusivity.reshape(8, 64, LANES)
    tables = constant_tables(LANES)
    plane, over, spectrum = tables["plane"], tables["over"], tables["spectrum"]
    grad, div, into, outof = tables["grad"], tables["div"], tables["into"], tables["outof"]
    coarse_size = coarse_factor.shape[1]
    width = -(-(coarse_size + TAIL) // LANES)
    count = 8 * -(-width // 8)

    field, sums, row_shape = (8, 64, LANES), (devices, width * LANES), (8, width * LANES)
    boxes = [(10, 144, LANES), (10, 144, LANES)]
    raw_sends = [(128, LANES), (2, 96, LANES), (128, LANES), (2, 32, LANES)]

    far = pl.BlockSpec(memory_space=pltpu.HBM)
    conv, row, *sends = kernel_call(
        conv_kernel,
        [(3,) + field, (count, LANES), (192 + count, LANES), (2, 144, LANES)]
        + [(192 + count, LANES), (2, 48, LANES)],
        *(pltpu.with_memory_space_constraint(x, pltpu.HBM) for x in (u, coarse_factor, plane, grad)),
        in_specs=[far] * 4,
        scratch_shapes=[
            pltpu.VMEM((3,) + field, F32),
            pltpu.VMEM((1, coarse_size), F32),
            pltpu.VMEM(plane.shape, F32),
            pltpu.VMEM(grad.shape, BF16),
            pltpu.SemaphoreType.DMA((4,)),
        ],
    )
    (inverse,) = kernel_call(inverse_kernel, [(10, 112, LANES)], diff, spectrum)

    def exchange(side_kernel, late_rows, sends, extra, extra_shape=None):
        send_out, send_early, send_in, send_late = sends
        inner, outer = axial_swap(send_in, send_out)
        early = azim_swap(send_early)
        shapes = [(2, late_rows, LANES)]
        shapes = shapes if extra_shape is None else shapes + [extra_shape]
        late, *passed = kernel_call(side_kernel, shapes, outer, inner, send_late, extra)
        return [outer, inner, early, azim_swap(late)] + passed

    one, copies = (1, width * LANES), (SUM_ROWS, width * LANES)
    groups = sum_steps()
    moved = exchange(conv_side_kernel, 48 + 8 * -(-3 * width // 8), sends, row)
    g, *sends, near, pay = kernel_call(
        divergence_kernel,
        [field] + raw_sends + [(16, width * LANES), copies],
        moved[2], conv, u, *moved[:2], moved[3], row, plane, over, div,
    )
    solver = (inverse, into, outof)
    operator = (near, diff, plane, grad, div)

    def solve(g, moved, pay):
        ends = [(6, 112, LANES), (4, 144, LANES), (144, LANES), (144, LANES), copies]
        planes, middle, ends, send_out, send_in, pay = kernel_call(
            solve_ends_kernel, boxes[:1] + ends, g, *moved, pay, *solver
        )
        solved, part, send_early, send_late = kernel_call(
            solve_rest_kernel,
            boxes[:1] + [field, (2, 80, LANES), (2, 48, LANES)],
            middle, ends, outof,
        )
        return planes, solved, part, send_out, send_early, send_in, send_late, pay


    *moved, pay = exchange(raw_side_kernel, 48, sends, partial_sum(pay, groups[0]), one)
    pay = partial_sum(pay, groups[1])
    planes_r, solved_r, part, *sends, pay = solve(g, moved, pay)
    *moved, pay = exchange(solved_side_kernel, 48, sends, partial_sum(pay, groups[2]), one)
    pay = partial_sum(pay, groups[3])
    z0, raw0, g, *sends, row_r, pay = kernel_call(
        first_apply_kernel,
        [field, field, field] + raw_sends + [row_shape, copies],
        part, *moved, *operator, pay, planes_r, solved_r,
    )
    *moved, pay = exchange(raw_side_kernel, 48, sends, partial_sum(pay, groups[0]), one)
    pay = partial_sum(pay, groups[1])
    planes_q, solved_q, part, *sends, pay = solve(g, moved, pay)
    *moved, pay = exchange(solved_side_kernel, 48, sends, partial_sum(pay, groups[2]), one)
    first_sums = partial_sum(pay, groups[3])
    y, z1, flux, ends, send_out, send_in = kernel_call(
        apply_ends_kernel,
        [field, field, field, (4, 64, LANES), (128, LANES), (128, LANES)],
        part, *moved, *operator, first_sums, row_r, z0,
    )
    raw1, g, send_early, send_late = kernel_call(
        apply_rest_kernel,
        [field, field, (2, 96, LANES), (2, 32, LANES)],
        z1, flux, ends, diff, plane, grad, div,
    )
    sends = send_out, send_early, send_in, send_late
    planes_r, solved_r, pay = kernel_call(
        first_dots_kernel,
        boxes + [one],
        first_sums, row_r, near, planes_r, planes_q, solved_r, solved_q, z1, raw1, raw0,
    )
    *moved, pay = exchange(raw_side_kernel, 48, sends, pay, one)
    planes_w, solved_w, part, *sends, pay = solve(g, moved, pay)
    (pay,) = kernel_call(
        second_dots_kernel, [one], pay[:1], planes_r, planes_q, planes_w, solved_r, solved_q, solved_w
    )
    gathered = gather_sums(jnp.broadcast_to(pay, sums))
    send_out, send_early, send_in, send_late = sends
    inner, outer = axial_swap(send_in, send_out)
    late, passed = kernel_call(
        last_side_kernel, [(2, 128, LANES), one], outer, inner, send_late, pay, send_early
    )
    moved = outer, inner, azim_swap(late)
    pressure, residual, direction = kernel_call(
        last_kernel,
        [field, field, field],
        part, *moved, near, gathered, first_sums, row_r, passed,
        y, z0, z1, planes_r, planes_q, planes_w,
    )
    return pressure.reshape(shape), residual.reshape(shape), direction.reshape(shape)


def solution(mesh):
    split = P(None, None, None, "axial", "azim", None)
    in_specs = (P(None, None, None, None, "axial", "azim", None), split, P(ALL, None))
    return jax.shard_map(
        per_device, mesh=mesh, in_specs=in_specs, out_specs=(split, split, split), check_vma=False
    )
```

```python
import math

import jax
import jax.numpy as jnp
import numpy as np
from jax import lax
from jax.experimental import pallas as pl
from jax.experimental.pallas import tpu as pltpu
from jax.sharding import PartitionSpec as P

ALL = ("axial", "azim")
time_increment = 0.02
mass_shift = 0.05
VMEM_GRANT = 20 << 20
TAIL = 16
SUM_ROWS = 32
gll_points = [
    -1.0,
    -0.8717401485096066,
    -0.5917001814331423,
    -0.20929921790247888,
    0.20929921790247888,
    0.5917001814331423,
    0.8717401485096066,
    1.0,
]


def legendre_value(order, point):
    before = 1.0
    current = point
    for step_idx in range(1, order):
        after = ((2 * step_idx + 1) * point * current - step_idx * before) / (step_idx + 1)
        before = current
        current = after
    return current


def jacobi_eigen(matrix):
    size_n = len(matrix)
    work = [list(row) for row in matrix]
    vectors = [
        [1.0 if row_idx == col_idx else 0.0 for col_idx in range(size_n)]
        for row_idx in range(size_n)
    ]
    for sweep_idx in range(15):
        for row_idx in range(size_n):
            for col_idx in range(row_idx + 1, size_n):
                off_value = work[row_idx][col_idx]
                if off_value != 0.0:
                    theta = (work[col_idx][col_idx] - work[row_idx][row_idx]) / (2.0 * off_value)
                    root_val = math.sqrt(theta * theta + 1.0)
                    tangent = 1.0 / (theta + root_val) if theta >= 0.0 else 1.0 / (theta - root_val)
                    cosine = 1.0 / math.sqrt(tangent * tangent + 1.0)
                    sine = tangent * cosine
                    for other in range(size_n):
                        left_val = work[other][row_idx]
                        right_val = work[other][col_idx]
                        work[other][row_idx] = cosine * left_val - sine * right_val
                        work[other][col_idx] = sine * left_val + cosine * right_val
                    for other in range(size_n):
                        left_val = work[row_idx][other]
                        right_val = work[col_idx][other]
                        work[row_idx][other] = cosine * left_val - sine * right_val
                        work[col_idx][other] = sine * left_val + cosine * right_val
                    for other in range(size_n):
                        left_val = vectors[other][row_idx]
                        right_val = vectors[other][col_idx]
                        vectors[other][row_idx] = cosine * left_val - sine * right_val
                        vectors[other][col_idx] = sine * left_val + cosine * right_val
    return ([work[row_idx][row_idx] for row_idx in range(size_n)], vectors)


def gll_tables():
    degree = 7
    points = degree + 1
    legendre_at = [legendre_value(degree, node_val) for node_val in gll_points]
    weights = [2.0 / (degree * (degree + 1) * value * value) for value in legendre_at]
    derivative = [[0.0] * points for row_idx in range(points)]
    for row_idx in range(points):
        for col_idx in range(points):
            if row_idx != col_idx:
                derivative[row_idx][col_idx] = legendre_at[row_idx] / (
                    legendre_at[col_idx] * (gll_points[row_idx] - gll_points[col_idx])
                )
    derivative[0][0] = -degree * (degree + 1) / 4.0
    derivative[degree][degree] = degree * (degree + 1) / 4.0
    stiffness = [
        [
            sum(
                (
                    derivative[mid_idx][row_idx] * weights[mid_idx] * derivative[mid_idx][col_idx]
                    for mid_idx in range(points)
                )
            )
            for col_idx in range(points)
        ]
        for row_idx in range(points)
    ]
    line_len = 3 * degree + 1
    big_stiff = [[0.0] * line_len for row_idx in range(line_len)]
    big_mass = [0.0] * line_len
    for element in range(3):
        offset = element * degree
        for row_idx in range(points):
            big_mass[offset + row_idx] += weights[row_idx]
            for col_idx in range(points):
                big_stiff[offset + row_idx][offset + col_idx] += stiffness[row_idx][col_idx]
    start_node = degree - 1
    box_len = degree + 3
    scaling = [1.0 / math.sqrt(big_mass[start_node + row_idx]) for row_idx in range(box_len)]
    symmetric = [
        [
            scaling[row_idx]
            * big_stiff[start_node + row_idx][start_node + col_idx]
            * scaling[col_idx]
            for col_idx in range(box_len)
        ]
        for row_idx in range(box_len)
    ]
    eigval, eigvec = jacobi_eigen(symmetric)
    fdm_basis = [
        [scaling[row_idx] * eigvec[row_idx][col_idx] for col_idx in range(box_len)]
        for row_idx in range(box_len)
    ]
    return (weights, derivative, fdm_basis, eigval)

WEIGHTS, DERIV, BASIS, EIGVAL = (np.asarray(t, np.float64) for t in gll_tables())


def f32(table):
    return jnp.asarray(table, jnp.float32)


F32 = jnp.float32
BF16 = jnp.bfloat16
LANES = 128
INTERPRET = False


def split_terms(table, depth):
    padded = np.zeros((table.shape[0], depth))
    padded[:, : table.shape[1]] = table
    high = padded.astype(jnp.bfloat16)
    low = (padded - high.astype(np.float64)).astype(jnp.bfloat16)
    return jnp.asarray(np.concatenate([high, high, low], axis=1))


def box_tables():
    pairs = [(b + 1, c + 1) for b in range(8) for c in range(8)]
    pairs += [(b + 1, {6: 0, 1: 9}.get(c)) for b in range(8) for c in range(8)]
    pairs += [(0, c + 1) for c in range(8)] + [(9, c + 1) for c in range(8)]
    table = np.zeros((144, 112))
    for row, (b, c) in enumerate(pairs):
        if c is not None:
            table[row, :100] = np.outer(BASIS[b], BASIS[c]).reshape(100)
    sums = np.ones(112)
    sums[:100] = (EIGVAL[:, None] + EIGVAL[None, :]).reshape(100)
    return table, sums


EYE = np.eye(8)
GRAD = np.concatenate([np.kron(DERIV, EYE), np.kron(EYE, DERIV)])
BOX_ROWS, SPECTRUM = box_tables()
EVEN = [bool(abs(BASIS[0, i] - BASIS[9, i]) < abs(BASIS[0, i] + BASIS[9, i])) for i in range(10)]


def constant_tables(radial):
    plane = (WEIGHTS[:, None] * WEIGHTS[None, :]).reshape(64, 1)
    mult_r = np.ones((8, radial))
    mult_r[0, 1:] = 2.0
    mult_r[7, :-1] = 2.0
    ends = np.array([2.0, 1, 1, 1, 1, 1, 1, 2.0])
    mult = (ends[:, None, None] * mult_r[None]).reshape(64, radial)
    return dict(
        plane=f32(np.broadcast_to(plane, (64, radial))),
        over=f32(1.0 / mult),
        spectrum=f32(np.broadcast_to(SPECTRUM[:, None], (112, radial))),
        grad=split_terms(GRAD, 64),
        div=split_terms(GRAD.T, 128),
        into=split_terms(BOX_ROWS.T, 144),
        outof=split_terms(BOX_ROWS, 112),
    )


def product(table_ref, values):
    high = values.astype(BF16)
    low = (values - high.astype(F32)).astype(BF16)
    return jnp.dot(
        table_ref[...], jnp.concatenate([high, low, high], axis=0), preferred_element_type=F32
    )


def combine(coefs, terms):
    total = None
    for coef, term in zip(coefs, terms):
        scaled = float(coef) * term
        total = scaled if total is None else total + scaled
    return total


def skew_apply(matrix, parts, rows=range(4)):
    plus = [parts[b] + parts[7 - b] for b in range(4)]
    minus = [parts[b] - parts[7 - b] for b in range(4)]
    result = [None] * 8
    for a in rows:
        even = combine([0.5 * (matrix[a, b] + matrix[a, 7 - b]) for b in range(4)], plus)
        odd = combine([0.5 * (matrix[a, b] - matrix[a, 7 - b]) for b in range(4)], minus)
        result[a] = even + odd
        result[7 - a] = odd - even
    return result


def to_spectral(parts):
    plus = [parts[a] + parts[9 - a] for a in range(5)]
    minus = [parts[a] - parts[9 - a] for a in range(5)]
    return [combine(BASIS[:5, i], plus if EVEN[i] else minus) for i in range(10)]


def from_spectral(parts):
    evens = [i for i in range(10) if EVEN[i]]
    odds = [i for i in range(10) if not EVEN[i]]
    result = [None] * 10
    for a in range(5):
        even = combine(BASIS[a, evens], [parts[i] for i in evens])
        odd = combine(BASIS[a, odds], [parts[i] for i in odds])
        result[a] = even + odd
        result[9 - a] = even - odd
    return result


def masks():
    layer = lax.broadcasted_iota(jnp.int32, (8, LANES), 0)
    elem = lax.broadcasted_iota(jnp.int32, (8, LANES), 1)
    return layer, elem > 0, elem < LANES - 1


def spread(values, first, last):
    layer, has_before, has_after = masks()
    cubes = values.reshape(values.shape[0] // 8, 8, LANES)
    before = pltpu.roll(cubes, 1, axis=2)
    after = pltpu.roll(cubes, LANES - 1, axis=2)
    before_mask = ((layer == first) & has_before)[None]
    after_mask = ((layer == last) & has_after)[None]
    result = jnp.where(before_mask, before, jnp.where(after_mask, after, 0.0))
    return result.reshape(values.shape)


def radial_sum(values):
    layer, has_before, has_after = masks()
    cubes = values.reshape(values.shape[0] // 8, 8, LANES)
    up = pltpu.roll(cubes, 1, axis=1)
    down = pltpu.roll(cubes, 7, axis=1)
    ends = jnp.where((layer == 0)[None], up, down)
    before = pltpu.roll(ends, 1, axis=2)
    after = pltpu.roll(ends, LANES - 1, axis=2)
    before_mask = ((layer == 0) & has_before)[None]
    after_mask = ((layer == 7) & has_after)[None]
    ends = jnp.where(before_mask, before, jnp.where(after_mask, after, 0.0))
    return (cubes + ends).reshape(values.shape)


def total(values):
    return jnp.sum(values, axis=(0, 1), keepdims=True)


def add_rows(block, extra):
    pieces = []
    for b in range(8):
        piece = block[8 * b : 8 * b + 8]
        pieces.append(piece + extra[b] if b in extra else piece)
    return jnp.concatenate(pieces, axis=0)


def is_even():
    return lax.axis_index("axial") % 2 == 0


def send_axial(inner_ref, outer_ref, low, high):
    even = is_even()
    row = 0
    for low_piece, high_piece in zip(low, high):
        size = low_piece.shape[0]
        inner_ref[row : row + size] = jnp.where(even, high_piece, low_piece)
        outer_ref[row : row + size] = jnp.where(even, low_piece, high_piece)
        row += size


def got_axial(inner_ref, outer_ref):
    even = is_even()

    def before(start, size):
        return jnp.where(even, outer_ref[start : start + size], inner_ref[start : start + size])

    def after(start, size):
        return jnp.where(even, inner_ref[start : start + size], outer_ref[start : start + size])

    return before, after


def conv_kernel(
    u_hbm, row_hbm, plane_hbm, grad_hbm,
    conv_ref, row_ref, out_ref, early_ref, in_ref, late_ref,
    u_ref, small_ref, plane_ref, grad_ref, sems,
):
    copies = [
        pltpu.make_async_copy(source, target, sems.at[k])
        for k, (source, target) in enumerate(
            ((u_hbm, u_ref), (plane_hbm, plane_ref), (grad_hbm, grad_ref), (row_hbm, small_ref))
        )
    ]
    for copy in copies:
        copy.start()
    row_ref[...] = jnp.zeros(row_ref.shape, F32)
    for copy in copies:
        copy.wait()
    size = small_ref.shape[1]
    for k in range(-(-size // LANES)):
        stop = min(LANES, size - LANES * k)
        row_ref[k : k + 1, :stop] = small_ref[:, LANES * k : LANES * k + stop]
    plane = plane_ref[...]
    fields = [[u_ref[d, a] for a in range(8)] for d in range(3)]
    low, high = [], []
    for comp in range(3):
        parts = fields[comp]
        flat = product(grad_ref, jnp.concatenate(parts, axis=1))
        along_a = skew_apply(DERIV, parts)
        for a in range(8):
            cols = slice(LANES * a, LANES * a + LANES)
            value = (
                fields[0][a] * along_a[a]
                + fields[1][a] * flat[:64, cols]
                + fields[2][a] * flat[64:, cols]
            )
            value = radial_sum(float(WEIGHTS[a]) * plane * value)
            conv_ref[comp, a] = value
            for side, rows in enumerate((value[:8], value[56:])):
                if a in (0, 7):
                    start = 16 * comp + (8 if a else 0)
                    late_ref[side, start : start + 8] = rows
                else:
                    start = 48 * comp + 8 * (a - 1)
                    early_ref[side, start : start + 8] = rows
            if a == 0:
                low.append(value)
            if a == 7:
                high.append(value)
    row = row_ref[...]
    send_axial(in_ref, out_ref, low + [row], high + [row])


def inverse_kernel(diff_ref, spectrum_ref, inverse_ref):
    mean = diff_ref[0]
    for a in range(1, 8):
        mean = mean + diff_ref[a]
    kbar = jnp.sum(mean, axis=0, keepdims=True) * (1.0 / 512.0)
    plane_spectrum = kbar * spectrum_ref[...] + mass_shift
    for i in range(10):
        inverse_ref[i] = 1.0 / (plane_spectrum + float(EIGVAL[i]) * kbar)


def conv_side_kernel(out_ref, in_ref, late_ref, row_ref, send_ref):
    before, after = got_axial(in_ref, out_ref)
    count = row_ref.shape[0]
    for side, b in ((0, 0), (1, 7)):
        for comp in range(3):
            first = slice(16 * comp, 16 * comp + 8)
            last = slice(16 * comp + 8, 16 * comp + 16)
            row = 64 * comp + 8 * b
            send_ref[side, first] = late_ref[side, first] + before(row, 8)
            send_ref[side, last] = late_ref[side, last] + after(row, 8)
        send_ref[side, 48:] = jnp.zeros((send_ref.shape[1] - 48, LANES), F32)
        for place, rows in enumerate((before(192, count), row_ref[...], after(192, count))):
            width = min(count, (send_ref.shape[1] - 48) // 3)
            start = 48 + place * width
            send_ref[side, start : start + width] = rows[:width]


def coarse_share(raw, near_ref):
    middle = raw[1]
    for a in range(2, 7):
        middle = middle + raw[a]
    per_axial = (0.5 * raw[0], middle + 0.5 * (raw[0] + raw[7]), 0.5 * raw[7])
    rows = []
    for part in per_axial:
        inner = part[8:16]
        for b in range(2, 7):
            inner = inner + part[8 * b : 8 * b + 8]
        ends = (part[:8], part[56:])
        for piece in (0.5 * ends[0], inner + 0.5 * (ends[0] + ends[1]), 0.5 * ends[1]):
            rows.append(jnp.sum(piece, axis=0, keepdims=True))
    rows = jnp.concatenate(rows + [jnp.zeros((7, LANES), F32)], axis=0)
    shares = jnp.sum(rows, axis=1, keepdims=True)
    return jnp.sum(shares * near_ref[...], axis=0, keepdims=True)


def send_sums(pay_ref, row, scalars):
    width = pay_ref.shape[1]
    place = lax.broadcasted_iota(jnp.int32, (1, width), 1)
    for k, value in enumerate(scalars):
        row = jnp.where(place == width - 1 - k, value, row)
    pay_ref[...] = jnp.broadcast_to(row, pay_ref.shape)


def got_sums(ref, scalars):
    row = jnp.sum(ref[...], axis=0, keepdims=True)
    width = row.shape[1]
    place = lax.broadcasted_iota(jnp.int32, (1, width), 1)
    values = [
        jnp.sum(jnp.where(place == width - 1 - k, row, 0.0), axis=1, keepdims=True)
        for k in range(scalars)
    ]
    return jnp.where(place >= width - TAIL, 0.0, row), values


def send_raw_ends(parts, in_ref, out_ref):
    send_axial(in_ref, out_ref, [parts[0], parts[1]], [parts[7], parts[6]])


def send_raw_rest(parts, g_ref, early_ref, late_ref):
    for a in range(8):
        g_ref[a] = parts[a]
    for side, (edge, inner) in enumerate(((0, 1), (7, 6))):
        edges = [part[8 * edge : 8 * edge + 8] for part in parts]
        inners = [part[8 * inner : 8 * inner + 8] for part in parts]
        for a in range(1, 7):
            early_ref[side, 8 * a - 8 : 8 * a] = edges[a]
            early_ref[side, 40 + 8 * a : 48 + 8 * a] = inners[a]
        late_ref[side, :8] = edges[0]
        late_ref[side, 8:16] = edges[7]
        late_ref[side, 16:24] = inners[0]
        late_ref[side, 24:32] = inners[7]


def send_raw(raw, g_ref, in_ref, out_ref, early_ref, late_ref):
    parts = [radial_sum(raw[a]) for a in range(8)]
    send_raw_ends(parts, in_ref, out_ref)
    send_raw_rest(parts, g_ref, early_ref, late_ref)


def raw_side_kernel(out_ref, in_ref, late_ref, row_ref, send_ref, pass_ref):
    pass_ref[...] = row_ref[...]
    before, after = got_axial(in_ref, out_ref)
    for side, (edge, inner) in enumerate(((0, 1), (7, 6))):
        send_ref[side, :8] = before(64 + 8 * edge, 8)
        send_ref[side, 8:16] = late_ref[side, :8] + before(8 * edge, 8)
        send_ref[side, 16:24] = late_ref[side, 8:16] + after(8 * edge, 8)
        send_ref[side, 24:32] = after(64 + 8 * edge, 8)
        send_ref[side, 32:40] = late_ref[side, 16:24] + before(8 * inner, 8)
        send_ref[side, 40:48] = late_ref[side, 24:32] + after(8 * inner, 8)


def divergence_kernel(
    early_ref, conv_ref, u_ref, out_ref, in_ref, late_ref, row_ref, plane_ref, over_ref, div_ref,
    g_ref, send_out_ref, send_early_ref, send_in_ref, send_late_ref, near_ref, pay_ref,
):
    before, after = got_axial(in_ref, out_ref)
    plane, over = plane_ref[...], over_ref[...]

    def side_rows(side, comp, a):
        if a in (0, 7):
            start = 16 * comp + (8 if a else 0)
            return late_ref[side, start : start + 8]
        start = 48 * comp + 8 * (a - 1)
        return early_ref[side, start : start + 8]

    moved = []
    for comp in range(3):
        parts = []
        for a in range(8):
            value = conv_ref[comp, a]
            if a == 0:
                value = value + before(64 * comp, 64)
            if a == 7:
                value = value + after(64 * comp, 64)
            value = add_rows(value, {0: side_rows(1, comp, a), 7: side_rows(0, comp, a)})
            scale = time_increment * (0.5 if a in (0, 7) else 1.0)
            parts.append(float(WEIGHTS[a]) * plane * u_ref[comp, a] - scale * over * value)
        moved.append(parts)
    flat = product(
        div_ref,
        jnp.concatenate([jnp.concatenate(moved[1], axis=1), jnp.concatenate(moved[2], axis=1)], axis=0),
    )
    along_a = skew_apply(DERIV.T, moved[0])
    raw = [along_a[a] + flat[:, LANES * a : LANES * a + LANES] for a in range(8)]
    send_raw(raw, g_ref, send_in_ref, send_out_ref, send_early_ref, send_late_ref)
    count = row_ref.shape[0]
    width = near_ref.shape[1] // LANES
    near_ref[...] = jnp.zeros(near_ref.shape, F32)
    packed = min(count, (late_ref.shape[1] - 48) // 3)
    for i in range(3):
        start = 48 + i * packed
        middle = (before(192, count), row_ref[...], after(192, count))[i]
        sides = (late_ref[1, start : start + packed], middle, late_ref[0, start : start + packed])
        for j, rows in enumerate(sides):
            for k in range(width):
                near_ref[3 * i + j : 3 * i + j + 1, LANES * k : LANES * k + LANES] = rows[k : k + 1]
    send_sums(pay_ref, coarse_share(raw, near_ref), [])


def got_planes(g_ref, in_ref, out_ref, early_ref, late_ref):
    before, after = got_axial(in_ref, out_ref)

    def edge_rows(side, e):
        if e in (0, 1, 8, 9):
            start = 8 * (0, 1, 8, 9).index(e)
            return late_ref[side, start : start + 8]
        return early_ref[side, 8 * e - 16 : 8 * e - 8]

    def inner_rows(side, a):
        if a in (0, 7):
            start = 40 if a else 32
            return late_ref[side, start : start + 8]
        return early_ref[side, 40 + 8 * a : 48 + 8 * a]

    zero = jnp.zeros((80, LANES), F32)
    planes = []
    for e in range(10):
        if e == 0:
            value = before(64, 64)
        elif e == 9:
            value = after(64, 64)
        else:
            value = g_ref[e - 1]
        if e == 1:
            value = value + before(0, 64)
        if e == 8:
            value = value + after(0, 64)
        value = add_rows(value, {0: edge_rows(1, e), 7: edge_rows(0, e)})
        if e in (0, 9):
            rows = [value, zero]
        else:
            rows = [value, spread(value, 6, 1), inner_rows(1, e - 1), inner_rows(0, e - 1)]
        planes.append(jnp.concatenate(rows, axis=0))
    return planes


def to_part(rows):
    return radial_sum(rows[:64] + spread(rows[64:128], 1, 6)), radial_sum(rows[128:144])


def solve_ends_kernel(
    g_ref, out_ref, in_ref, early_ref, late_ref, row_ref, inverse_ref, into_ref, outof_ref,
    planes_ref, middle_ref, ends_ref, send_out_ref, send_in_ref, pass_ref,
):
    pass_ref[...] = jnp.broadcast_to(row_ref[...], pass_ref.shape)
    planes = got_planes(g_ref, in_ref, out_ref, early_ref, late_ref)
    for e in range(10):
        planes_ref[e] = planes[e]
    flat = product(into_ref, jnp.concatenate(planes, axis=1))
    parts = to_spectral([flat[:, LANES * e : LANES * e + LANES] for e in range(10)])
    parts = [parts[i] * inverse_ref[i] for i in range(10)]
    parts = from_spectral(parts)
    flat = product(outof_ref, jnp.concatenate([parts[e] for e in (0, 1, 8, 9)], axis=1))
    ends = [flat[:, LANES * k : LANES * k + LANES] for k in range(4)]
    low, low_faces = to_part(ends[1])
    high, high_faces = to_part(ends[2])
    send_axial(
        send_in_ref,
        send_out_ref,
        [low, radial_sum(ends[0][:64]), low_faces],
        [high, radial_sum(ends[3][:64]), high_faces],
    )
    for k in range(4):
        ends_ref[k] = ends[k]
    for e in range(2, 8):
        middle_ref[e - 2] = parts[e]


def solve_rest_kernel(
    middle_ref, ends_ref, outof_ref, solved_ref, part_ref, send_early_ref, send_late_ref,
):
    flat = product(outof_ref, jnp.concatenate([middle_ref[k] for k in range(6)], axis=1))
    solved = [flat[:, LANES * k : LANES * k + LANES] for k in range(6)]
    solved = [ends_ref[0], ends_ref[1]] + solved + [ends_ref[2], ends_ref[3]]
    for e in range(10):
        solved_ref[e] = solved[e]
    for a in range(8):
        value, outer_b = to_part(solved[a + 1])
        part_ref[a] = value
        for side in range(2):
            edge = value[56 * side : 56 * side + 8]
            face = outer_b[8 * side : 8 * side + 8]
            if a in (0, 1, 6, 7):
                start = 8 * (0, 1, 6, 7).index(a)
                send_late_ref[side, start : start + 8] = edge
            else:
                send_early_ref[side, 8 * a - 16 : 8 * a - 8] = edge
            if a in (0, 7):
                start = 40 if a else 32
                send_late_ref[side, start : start + 8] = face
            else:
                send_early_ref[side, 24 + 8 * a : 32 + 8 * a] = face


def first_rest_kernel(
    middle_ref, ends_ref, outof_ref, planes_ref,
    solved_ref, part_ref, send_early_ref, send_late_ref, dot_ref,
):
    solve_rest_kernel(
        middle_ref, ends_ref, outof_ref, solved_ref, part_ref, send_early_ref, send_late_ref
    )
    dot_ref[...] = jnp.broadcast_to(dot_planes(planes_ref, solved_ref), dot_ref.shape)


def solved_side_kernel(out_ref, in_ref, late_ref, row_ref, send_ref, pass_ref):
    pass_ref[...] = row_ref[...]
    before, after = got_axial(in_ref, out_ref)
    for side, b in ((0, 0), (1, 7)):
        row = 8 * b
        send_ref[side, :8] = late_ref[side, :8] + before(row, 8)
        send_ref[side, 8:16] = late_ref[side, 8:16] + before(64 + row, 8)
        send_ref[side, 16:24] = late_ref[side, 16:24] + after(64 + row, 8)
        send_ref[side, 24:32] = late_ref[side, 24:32] + after(row, 8)
        send_ref[side, 32:40] = late_ref[side, 32:40] + before(128 + 8 * side, 8)
        send_ref[side, 40:48] = late_ref[side, 40:48] + after(128 + 8 * side, 8)


def last_side_kernel(out_ref, in_ref, late_ref, row_ref, bulk_ref, send_ref, pass_ref):
    send_ref[:, 48:] = bulk_ref[...]
    solved_side_kernel(out_ref, in_ref, late_ref, row_ref, send_ref, pass_ref)


def got_solved(part_ref, in_ref, out_ref, early_ref, late_ref):
    before, after = got_axial(in_ref, out_ref)
    extra = {0: (before, 0), 1: (before, 64), 6: (after, 64), 7: (after, 0)}

    def edge_rows(side, a):
        if a in extra:
            start = 8 * (0, 1, 6, 7).index(a)
            return late_ref[side, start : start + 8]
        return early_ref[side, 8 * a - 16 : 8 * a - 8]

    def face_rows(side, a):
        if a in (0, 7):
            start = 40 if a else 32
            return late_ref[side, start : start + 8]
        return early_ref[side, 24 + 8 * a : 32 + 8 * a]

    result = []
    for a in range(8):
        value = part_ref[a]
        if a in extra:
            side, start = extra[a]
            value = value + side(start, 64)
        result.append(
            add_rows(
                value,
                {0: edge_rows(1, a), 1: face_rows(1, a), 6: face_rows(0, a), 7: edge_rows(0, a)},
            )
        )
    return result


def add_coarse(parts, row, near_ref):
    values = jnp.sum(near_ref[...] * row, axis=1, keepdims=True)
    own = [[values[3 * i + j : 3 * i + j + 1] for j in range(3)] for i in range(3)]
    fields = []
    for i in range(3):
        ends = [0.5 * (own[i][1] + own[i][j]) for j in (0, 2)]
        rows = [jnp.broadcast_to(value, (8, LANES)) for value in (ends[0], own[i][1], ends[1])]
        fields.append(jnp.concatenate([rows[0]] + [rows[1]] * 6 + [rows[2]], axis=0))
    first, last = 0.5 * (fields[0] + fields[1]), 0.5 * (fields[1] + fields[2])
    return [
        parts[a] + (first if a == 0 else last if a == 7 else fields[1]) for a in range(8)
    ]


def flux_along(values, diff_ref, plane_ref):
    plane = plane_ref[...]
    slopes = skew_apply(DERIV, values)
    return [float(WEIGHTS[a]) * plane * diff_ref[a] * slopes[a] for a in range(8)]


def apply_layers(layers, values, flux, diff_ref, plane_ref, grad_ref, div_ref):
    plane = plane_ref[...]
    flat = product(grad_ref, jnp.concatenate([values[a] for a in layers], axis=1))
    across = []
    for k, a in enumerate(layers):
        coef = float(WEIGHTS[a]) * plane * diff_ref[a]
        coef = jnp.concatenate([coef, coef], axis=0)
        across.append(coef * flat[:, LANES * k : LANES * k + LANES])
    flat = product(div_ref, jnp.concatenate(across, axis=1))
    along_a = skew_apply(DERIV.T, flux, [a for a in layers if a < 4])
    return [
        along_a[a]
        + flat[:, LANES * k : LANES * k + LANES]
        + (mass_shift * float(WEIGHTS[a])) * plane * values[a]
        for k, a in enumerate(layers)
    ]


def apply_operator(values, diff_ref, plane_ref, grad_ref, div_ref):
    flux = flux_along(values, diff_ref, plane_ref)
    return apply_layers(range(8), values, flux, diff_ref, plane_ref, grad_ref, div_ref)


def dot_parts(first, second):
    result = first[0] * second[0]
    for a in range(1, 8):
        result = result + first[a] * second[a]
    return total(result)


def norm(row):
    return jnp.sum(row * row, axis=1, keepdims=True)


def dot_planes(first, second):
    result = None
    for e in range(10):
        stop = 64 if e in (0, 9) else 144
        term = first[e][:stop] * second[e][:stop]
        term = jnp.sum(term.reshape(stop // 8, 8, LANES), axis=0)
        result = term if result is None else result + term
    return total(result)


def first_apply_kernel(
    part_ref, out_ref, in_ref, early_ref, late_ref, near_ref, diff_ref, plane_ref, grad_ref, div_ref,
    sums_ref, dot_ref,
    z_ref, raw_ref, g_ref, send_out_ref, send_early_ref, send_in_ref, send_late_ref, row_ref, pay_ref,
):
    row, _ = got_sums(sums_ref, 0)
    values = got_solved(part_ref, in_ref, out_ref, early_ref, late_ref)
    values = add_coarse(values, row, near_ref)
    raw = apply_operator(values, diff_ref, plane_ref, grad_ref, div_ref)
    send_raw(raw, g_ref, send_in_ref, send_out_ref, send_early_ref, send_late_ref)
    for a in range(8):
        z_ref[a] = values[a]
        raw_ref[a] = raw[a]
    row_ref[0:1] = row
    scalars = [dot_ref[0:1, 0:1], dot_parts(values, raw)]
    send_sums(pay_ref, coarse_share(raw, near_ref), scalars)


def first_step(sums_ref, row_ref):
    row_q, (local_rz, curv) = got_sums(sums_ref, 2)
    row_r = row_ref[0:1]
    rz = local_rz + norm(row_r)
    return row_r, row_q, rz, curv, rz / curv


END_LAYERS = (0, 1, 6, 7)


def apply_ends_kernel(
    part_ref, out_ref, in_ref, early_ref, late_ref, near_ref, diff_ref, plane_ref, grad_ref, div_ref,
    sums_ref, row_ref, z0_ref,
    y_ref, z_ref, flux_ref, ends_ref, send_out_ref, send_in_ref,
):
    _, row_q, _, _, alpha = first_step(sums_ref, row_ref)
    change = got_solved(part_ref, in_ref, out_ref, early_ref, late_ref)
    change = add_coarse(change, row_q, near_ref)
    values = [z0_ref[a] - alpha * change[a] for a in range(8)]
    flux = flux_along(values, diff_ref, plane_ref)
    ends = apply_layers(END_LAYERS, values, flux, diff_ref, plane_ref, grad_ref, div_ref)
    sent = {a: radial_sum(raw) for a, raw in zip(END_LAYERS, ends)}
    send_raw_ends(sent, send_in_ref, send_out_ref)
    for a in range(8):
        y_ref[a] = change[a]
        z_ref[a] = values[a]
        flux_ref[a] = flux[a]
    for k in range(4):
        ends_ref[k] = ends[k]


def apply_rest_kernel(
    z_ref, flux_ref, ends_ref, diff_ref, plane_ref, grad_ref, div_ref,
    raw_ref, g_ref, send_early_ref, send_late_ref,
):
    values = [z_ref[a] for a in range(8)]
    flux = [flux_ref[a] for a in range(8)]
    raw = apply_layers((2, 3, 4, 5), values, flux, diff_ref, plane_ref, grad_ref, div_ref)
    raw = [ends_ref[0], ends_ref[1]] + raw + [ends_ref[2], ends_ref[3]]
    send_raw_rest([radial_sum(part) for part in raw], g_ref, send_early_ref, send_late_ref)
    for a in range(8):
        raw_ref[a] = raw[a]


def first_dots_kernel(
    sums_ref, row_ref, near_ref, planes_r_ref, planes_q_ref, solved_r_ref, solved_q_ref,
    z_ref, raw_ref, old_raw_ref,
    planes_ref, solved_ref, pay_ref,
):
    alpha = first_step(sums_ref, row_ref)[4]
    planes, solved = [], []
    for e in range(10):
        planes.append(planes_r_ref[e] - alpha * planes_q_ref[e])
        solved.append(solved_r_ref[e] - alpha * solved_q_ref[e])
        planes_ref[e] = planes[e]
        solved_ref[e] = solved[e]
    values = [z_ref[a] for a in range(8)]
    raw = [raw_ref[a] for a in range(8)]
    scalars = [
        dot_planes(planes, solved),
        dot_planes(planes, solved_q_ref),
        dot_planes(planes_q_ref, solved),
        dot_planes(planes_q_ref, solved_q_ref),
        dot_parts(values, raw),
        dot_parts(values, [old_raw_ref[a] for a in range(8)]),
    ]
    send_sums(pay_ref, coarse_share(raw, near_ref), scalars)


def second_dots_kernel(
    row_ref, planes_r_ref, planes_q_ref, planes_w_ref, solved_r_ref, solved_q_ref, solved_w_ref,
    pay_ref,
):
    scalars = [
        dot_planes(planes_r_ref, solved_w_ref),
        dot_planes(planes_q_ref, solved_w_ref),
        dot_planes(planes_w_ref, solved_r_ref),
        dot_planes(planes_w_ref, solved_q_ref),
        dot_planes(planes_w_ref, solved_w_ref),
    ]
    row = row_ref[...]
    width = row.shape[1]
    place = lax.broadcasted_iota(jnp.int32, (1, width), 1)
    for k, value in enumerate(scalars):
        row = jnp.where(place == width - 7 - k, value, row)
    pay_ref[...] = jnp.broadcast_to(row, pay_ref.shape)


def last_kernel(
    part_ref, out_ref, in_ref, late_ref, near_ref, sums_ref, old_sums_ref, row_ref, _,
    y_ref, z0_ref, z1_ref, planes_r_ref, planes_q_ref, planes_w_ref,
    pressure_ref, residual_ref, direction_ref,
):
    row_r, row_q, rz0, curv0, alpha0 = first_step(old_sums_ref, row_ref)
    row_w, scalars = got_sums(sums_ref, 11)
    rr, rq, qr, qq, first_curv, cross, rw, qw, wr, wq, ww = scalars
    row_r = row_r - alpha0 * row_q
    rz1 = rr + norm(row_r)
    beta0 = rz1 / rz0
    curv1 = first_curv + beta0 * (2.0 * cross + beta0 * curv0)
    alpha1 = rz1 / curv1
    row = row_w + beta0 * row_q
    row_r = row_r - alpha1 * row
    step = -alpha1 * beta0
    rz2 = (
        rr
        - alpha1 * (rw + wr)
        + step * (rq + qr)
        + alpha1 * alpha1 * ww
        - alpha1 * step * (wq + qw)
        + step * step * qq
        + norm(row_r)
    )
    beta1 = rz2 / rz1
    change = got_solved(part_ref, in_ref, out_ref, late_ref.at[:, 48:], late_ref)
    change = add_coarse(change, row_w, near_ref)
    for a in range(8):
        first = z0_ref[a]
        second = z1_ref[a] + beta0 * first
        image = planes_w_ref[a + 1, :64] + beta0 * planes_q_ref[a + 1, :64]
        residual_ref[a] = planes_r_ref[a + 1, :64] - alpha1 * image
        pressure_ref[a] = alpha0 * first + alpha1 * second
        direction_ref[a] = (
            z1_ref[a] - alpha1 * (change[a] + beta0 * y_ref[a]) + beta1 * second
        )


def kernel_call(kernel, out_shapes, *args, **options):
    outs = [jax.ShapeDtypeStruct(shape, F32) for shape in out_shapes]
    return pl.pallas_call(
        kernel,
        out_shape=outs,
        compiler_params=pltpu.CompilerParams(vmem_limit_bytes=VMEM_GRANT),
        interpret=INTERPRET,
        **options,
    )(*args)


def axial_swap(inner_rows, outer_rows):
    count = lax.axis_size("axial")
    inner = [(i, i ^ 1) for i in range(count)]
    outer = [((2 * i + 1) % count, (2 * i + 2) % count) for i in range(count // 2)]
    outer = outer + [(b, a) for a, b in outer]
    from_outer = lax.ppermute(outer_rows, "axial", outer)
    from_inner = lax.ppermute(inner_rows, "axial", inner)
    return from_inner, from_outer


def azim_swap(sides):
    count = lax.axis_size("azim")
    if count == 2:
        return lax.ppermute(sides, "azim", [(0, 1), (1, 0)])
    after = lax.ppermute(sides[0], "azim", [((i + 1) % count, i) for i in range(count)])
    before = lax.ppermute(sides[1], "azim", [(i, (i + 1) % count) for i in range(count)])
    return jnp.stack([after, before])


def sum_steps():
    azim = lax.axis_size("azim")
    count = lax.axis_size("axial") * azim
    steps, step = [], 2 * azim
    while step < count:
        steps.append(step)
        step *= 2
    step = 1
    while step < azim:
        steps.append(step)
        step *= 2
    groups = [steps[k::4] for k in range(4)]
    groups[0] = groups[0] + [azim]
    return groups


def partial_sum(row, steps):
    count = lax.axis_size("axial") * lax.axis_size("azim")
    for step in steps:
        row = row[:1] + lax.ppermute(row, ALL, [(i, i ^ step) for i in range(count)])[:1]
    return row


def gather_sums(rows):
    return lax.all_to_all(rows, ALL, 0, 0, tiled=True)


def per_device(velocity, diffusivity, coarse_factor):
    shape = diffusivity.shape
    devices = lax.axis_size("axial") * lax.axis_size("azim")
    u = velocity.reshape(3, 8, 64, LANES)
    diff = diffusivity.reshape(8, 64, LANES)
    tables = constant_tables(LANES)
    plane, over, spectrum = tables["plane"], tables["over"], tables["spectrum"]
    grad, div, into, outof = tables["grad"], tables["div"], tables["into"], tables["outof"]
    coarse_size = coarse_factor.shape[1]
    width = -(-(coarse_size + TAIL) // LANES)
    count = 8 * -(-width // 8)

    field, sums, row_shape = (8, 64, LANES), (devices, width * LANES), (8, width * LANES)
    boxes = [(10, 144, LANES), (10, 144, LANES)]
    raw_sends = [(128, LANES), (2, 96, LANES), (128, LANES), (2, 32, LANES)]

    far = pl.BlockSpec(memory_space=pltpu.HBM)
    conv, row, *sends = kernel_call(
        conv_kernel,
        [(3,) + field, (count, LANES), (192 + count, LANES), (2, 144, LANES)]
        + [(192 + count, LANES), (2, 48, LANES)],
        *(pltpu.with_memory_space_constraint(x, pltpu.HBM) for x in (u, coarse_factor, plane, grad)),
        in_specs=[far] * 4,
        scratch_shapes=[
            pltpu.VMEM((3,) + field, F32),
            pltpu.VMEM((1, coarse_size), F32),
            pltpu.VMEM(plane.shape, F32),
            pltpu.VMEM(grad.shape, BF16),
            pltpu.SemaphoreType.DMA((4,)),
        ],
    )
    (inverse,) = kernel_call(inverse_kernel, [(10, 112, LANES)], diff, spectrum)

    def exchange(side_kernel, late_rows, sends, extra, extra_shape=None):
        send_out, send_early, send_in, send_late = sends
        inner, outer = axial_swap(send_in, send_out)
        early = azim_swap(send_early)
        shapes = [(2, late_rows, LANES)]
        shapes = shapes if extra_shape is None else shapes + [extra_shape]
        late, *passed = kernel_call(side_kernel, shapes, outer, inner, send_late, extra)
        return [outer, inner, early, azim_swap(late)] + passed

    one, copies = (1, width * LANES), (SUM_ROWS, width * LANES)
    groups = sum_steps()
    moved = exchange(conv_side_kernel, 48 + 8 * -(-3 * width // 8), sends, row)
    g, *sends, near, pay = kernel_call(
        divergence_kernel,
        [field] + raw_sends + [(16, width * LANES), copies],
        moved[2], conv, u, *moved[:2], moved[3], row, plane, over, div,
    )
    solver = (inverse, into, outof)
    operator = (near, diff, plane, grad, div)

    def solve(g, moved, pay, first=False):
        ends = [(6, 112, LANES), (4, 144, LANES), (144, LANES), (144, LANES), copies]
        planes, middle, ends, send_out, send_in, pay = kernel_call(
            solve_ends_kernel, boxes[:1] + ends, g, *moved, pay, *solver
        )
        shapes = boxes[:1] + [field, (2, 80, LANES), (2, 48, LANES)]
        if first:
            solved, part, send_early, send_late, dot = kernel_call(
                first_rest_kernel, shapes + [(8, LANES)], middle, ends, outof, planes
            )
            return dot, planes, solved, part, send_out, send_early, send_in, send_late, pay
        solved, part, send_early, send_late = kernel_call(
            solve_rest_kernel, shapes, middle, ends, outof
        )
        return planes, solved, part, send_out, send_early, send_in, send_late, pay


    *moved, pay = exchange(raw_side_kernel, 48, sends, partial_sum(pay, groups[0]), one)
    pay = partial_sum(pay, groups[1])
    dot, planes_r, solved_r, part, *sends, pay = solve(g, moved, pay, True)
    *moved, pay = exchange(solved_side_kernel, 48, sends, partial_sum(pay, groups[2]), one)
    pay = partial_sum(pay, groups[3])
    z0, raw0, g, *sends, row_r, pay = kernel_call(
        first_apply_kernel,
        [field, field, field] + raw_sends + [row_shape, copies],
        part, *moved, *operator, pay, dot,
    )
    *moved, pay = exchange(raw_side_kernel, 48, sends, partial_sum(pay, groups[0]), one)
    pay = partial_sum(pay, groups[1])
    planes_q, solved_q, part, *sends, pay = solve(g, moved, pay)
    *moved, pay = exchange(solved_side_kernel, 48, sends, partial_sum(pay, groups[2]), one)
    first_sums = partial_sum(pay, groups[3])
    y, z1, flux, ends, send_out, send_in = kernel_call(
        apply_ends_kernel,
        [field, field, field, (4, 64, LANES), (128, LANES), (128, LANES)],
        part, *moved, *operator, first_sums, row_r, z0,
    )
    raw1, g, send_early, send_late = kernel_call(
        apply_rest_kernel,
        [field, field, (2, 96, LANES), (2, 32, LANES)],
        z1, flux, ends, diff, plane, grad, div,
    )
    sends = send_out, send_early, send_in, send_late
    planes_r, solved_r, pay = kernel_call(
        first_dots_kernel,
        boxes + [one],
        first_sums, row_r, near, planes_r, planes_q, solved_r, solved_q, z1, raw1, raw0,
    )
    *moved, pay = exchange(raw_side_kernel, 48, sends, pay, one)
    planes_w, solved_w, part, *sends, pay = solve(g, moved, pay)
    (pay,) = kernel_call(
        second_dots_kernel, [one], pay[:1], planes_r, planes_q, planes_w, solved_r, solved_q, solved_w
    )
    gathered = gather_sums(jnp.broadcast_to(pay, sums))
    send_out, send_early, send_in, send_late = sends
    inner, outer = axial_swap(send_in, send_out)
    late, passed = kernel_call(
        last_side_kernel, [(2, 128, LANES), one], outer, inner, send_late, pay, send_early
    )
    moved = outer, inner, azim_swap(late)
    pressure, residual, direction = kernel_call(
        last_kernel,
        [field, field, field],
        part, *moved, near, gathered, first_sums, row_r, passed,
        y, z0, z1, planes_r, planes_q, planes_w,
    )
    return pressure.reshape(shape), residual.reshape(shape), direction.reshape(shape)


def solution(mesh):
    split = P(None, None, None, "axial", "azim", None)
    in_specs = (P(None, None, None, None, "axial", "azim", None), split, P(ALL, None))
    return jax.shard_map(
        per_device, mesh=mesh, in_specs=in_specs, out_specs=(split, split, split), check_vma=False
    )
```
